32 devices in a mesh: tp: 4 (over y, core), dp: 2 (over x), grp: 4 (over z).
Axes of the slice: x: 2, y: 2, z: 4, core: 2. Of those that a mesh axis runs over, the one named last changes fastest.
Arguments:
- tokens: bfloat16 [16, 1024, 768], P(('dp', 'grp')), may hold values from -6 to 6
- sigma_index: int32 [16], P(('dp', 'grp')), may hold values from 0 to 63
- absorbed: int32 [16, 1024], P(('dp', 'grp')), may hold values 0 or 1
- cotangent: bfloat16 [16, 1024, 768], P(('dp', 'grp')), may hold values from -6 to 6
- time_table: float32 [64, 128], replicated, may hold values from -6 to 6
- in_weight: float32 [768, 7, 768], P('dp', None, 'tp'), may hold values from -0.21875 to 0.21875
- back_weight: float32 [5, 768, 768], P(None, 'tp', 'dp'), may hold values from -1.1547005 to 1.1547005
- ada_weight: float32 [128, 6, 768], P('dp', None, 'tp'), may hold values from -0.25 to 0.25
- small_params: float32 [9, 768], P(None, 'dp'), may hold values from -1.2 to 2.2
- up_bias: float32 [4, 768], P(None, ('tp', 'dp')), may hold values from -3 to 3
- in_first: float32 [4, 768, 7, 768], P('grp', 'dp', None, 'tp'), may hold values from -32 to 32
- back_first: float32 [4, 5, 768, 768], P('grp', None, 'tp', 'dp'), may hold values from -32 to 32
- ada_first: float32 [4, 128, 6, 768], P('grp', 'dp', None, 'tp'), may hold values from -32 to 32
- small_first: float32 [4, 9, 768], P('grp', None, 'dp'), may hold values from -32 to 32
- bias_first: float32 [4, 4, 768], P('grp', None, ('tp', 'dp')), may hold values from -32 to 32
- in_second: float32 [4, 768, 7, 768], P('grp', 'dp', None, 'tp'), may hold values from 1.024 to 16.384
- back_second: float32 [4, 5, 768, 768], P('grp', None, 'tp', 'dp'), may hold values from 1.024 to 16.384
- ada_second: float32 [4, 128, 6, 768], P('grp', 'dp', None, 'tp'), may hold values from 1.024 to 16.384
- small_second: float32 [4, 9, 768], P('grp', None, 'dp'), may hold values from 1.024 to 16.384
- bias_second: float32 [4, 4, 768], P('grp', None, ('tp', 'dp')), may hold values from 1.024 to 16.384
- in_moment: float32 [768, 7, 768], P('dp', None, 'tp'), may hold values from -0.09375 to 0.09375
- back_moment: float32 [5, 768, 768], P(None, 'tp', 'dp'), may hold values from -0.09375 to 0.09375
- ada_moment: float32 [128, 6, 768], P('dp', None, 'tp'), may hold values from -0.09375 to 0.09375
- small_moment: float32 [9, 768], P(None, 'dp'), may hold values from -0.875 to 0.875
- bias_moment: float32 [4, 768], P(None, ('tp', 'dp')), may hold values from -0.875 to 0.875
Outputs:
- block_out: bfloat16 [16, 1024, 768], P(('dp', 'grp'))
- input_grad: float32 [16, 1024, 768], P(('dp', 'grp'))
- in_first_new: float32 [4, 768, 7, 768], P('grp', 'dp', None, 'tp')
- back_first_new: float32 [4, 5, 768, 768], P('grp', None, 'tp', 'dp')
- ada_first_new: float32 [4, 128, 6, 768], P('grp', 'dp', None, 'tp')
- small_first_new: float32 [4, 9, 768], P('grp', None, 'dp')
- bias_first_new: float32 [4, 4, 768], P('grp', None, ('tp', 'dp'))
- in_second_new: float32 [4, 768, 7, 768], P('grp', 'dp', None, 'tp')
- back_second_new: float32 [4, 5, 768, 768], P('grp', None, 'tp', 'dp')
- ada_second_new: float32 [4, 128, 6, 768], P('grp', 'dp', None, 'tp')
- small_second_new: float32 [4, 9, 768], P('grp', None, 'dp')
- bias_second_new: float32 [4, 4, 768], P('grp', None, ('tp', 'dp'))
- in_weight_new: float32 [768, 7, 768], P('dp', None, 'tp')
- back_weight_new: float32 [5, 768, 768], P(None, 'tp', 'dp')
- ada_weight_new: float32 [128, 6, 768], P('dp', None, 'tp')
- small_params_new: float32 [9, 768], P(None, 'dp')
- up_bias_new: float32 [4, 768], P(None, ('tp', 'dp'))
- in_diff: float32 [768, 7, 768], P('dp', None, 'tp')
- back_diff: float32 [5, 768, 768], P(None, 'tp', 'dp')
- ada_diff: float32 [128, 6, 768], P('dp', None, 'tp')
- small_diff: float32 [9, 768], P(None, 'dp')
- bias_diff: float32 [4, 768], P(None, ('tp', 'dp'))
- in_moment_new: float32 [768, 7, 768], P('dp', None, 'tp')
- back_moment_new: float32 [5, 768, 768], P(None, 'tp', 'dp')
- ada_moment_new: float32 [128, 6, 768], P('dp', None, 'tp')
- small_moment_new: float32 [9, 768], P(None, 'dp')
- bias_moment_new: float32 [4, 768], P(None, ('tp', 'dp'))
The draws below stay inside these ranges and needn't reach their ends.
All inputs are finite; a program needn't handle non-finite values. No bound on the sum of `absorbed` on one device may be relied on, other than what follows from the above.
Results may differ from the reference program's by a relative error of at most 0.018.
Values may be sent and summed in bfloat16 or wider, within the bound.
A program may use at most 192 MiB of HBM per device.

```python
import math
import jax
import jax.numpy as jnp
from jax import lax

D = 768
HEADS = 12
FF = 3072
CD = 128
HEAD_DIM = 64
LEN = 1024
NSIG = 64
STEP = 10
SEQ_DEV = 2
SEQS = 16
N_DP = 2
N_GRP = 4


def draw_back_weight(key, part):
    noise_draw = jax.random.truncated_normal(key, -4.0, 4.0, (5, D, D), jnp.float32)
    slot_ids = jnp.arange(5)
    slot_scale = jnp.where(slot_ids == 0, LEN ** 0.5 / 4.0 / D ** 0.5, 1.0 / FF ** 0.5)
    return noise_draw * slot_scale[:, None, None]


def draw_small_params(key, part):
    noise_draw = jax.random.truncated_normal(key, -4.0, 4.0, (9, D), jnp.float32)
    row_ids = jnp.arange(9)
    centre = jnp.where((row_ids <= 1) | (row_ids == 5) | (row_ids == 8), 1.0, 0.0)
    spread = jnp.where(row_ids <= 1, 0.15, 0.3)
    return centre[:, None] + spread[:, None] * noise_draw


def touch_ends(drawn, key, least, high):
    index_at = [jax.random.randint(jax.random.fold_in(key, axis), (), 0, length) for axis, length in enumerate(drawn.shape)]
    main_axis = drawn.shape.index(max(drawn.shape))
    beside = index_at[:main_axis] + [(index_at[main_axis] + 1) % drawn.shape[main_axis]] + index_at[main_axis + 1:]
    return drawn.at[tuple(index_at)].set(least).at[tuple(beside)].set(high)


def block_levels(key, extent, shards, least, top_value):
    factor_of = 1.0
    for axis_at, blocks in shards:
        steps = jax.random.uniform(jax.random.fold_in(jax.random.fold_in(key, 6), axis_at), (blocks,), jnp.float32, least / len(shards), top_value / len(shards))
        factor_of = factor_of * jnp.repeat(jnp.exp(steps), extent[axis_at] // blocks).reshape((-1,) + (1,) * (len(extent) - 1 - axis_at))
    return factor_of


def normal_values(key, extent, deviation, reach, pieces=(), kind=jnp.bfloat16):
    drawn = deviation * jax.random.normal(key, extent, jnp.float32)
    if pieces:
        drawn = drawn * block_levels(key, extent, pieces, -0.22, 0.18)
    return jnp.clip(drawn, -reach, reach).astype(kind)


def setup_inputs(seed: int = 0) -> dict:
    keys = jax.random.split(jax.random.key(seed), 26)
    return {
        "tokens": normal_values(keys[0], (SEQS, LEN, D), 1.0, 6.0, ((0, 8),)),
        "sigma_index": touch_ends(jax.random.randint(keys[1], (SEQS,), 0, NSIG), jax.random.fold_in(keys[1], 1), 0, NSIG - 1).astype(jnp.int32),
        "absorbed": touch_ends((jax.random.randint(keys[2], (SEQS, LEN), 0, 2) < 1).astype(jnp.int32), jax.random.fold_in(keys[2], 1), 0, 1),
        "cotangent": normal_values(keys[3], (SEQS, LEN, D), 1.0, 6.0, ((0, 8),)),
        "time_table": normal_values(keys[4], (NSIG, CD), 1.0, 6.0, (), jnp.float32),
        "in_weight": normal_values(keys[5], (D, 7, D), D ** -0.5, 0.21875, ((0, 2), (2, 4)), jnp.float32),
        "back_weight": draw_back_weight(jax.random.fold_in(keys[25], 71), 0),
        "ada_weight": normal_values(keys[7], (CD, 6, D), (4 * CD) ** -0.5, 0.25, ((0, 2), (2, 4)), jnp.float32),
        "small_params": draw_small_params(jax.random.fold_in(keys[25], 71), 0),
        "up_bias": normal_values(keys[9], (4, D), 0.5, 3.0, ((1, 8),), jnp.float32),
        "in_first": normal_values(keys[10], (N_GRP, D, 7, D), (0.08 * (N_DP * SEQ_DEV * LEN) ** 0.5), 32.0, ((0, 4), (1, 2), (3, 4)), jnp.float32),
        "back_first": normal_values(keys[11], (N_GRP, 5, D, D), (0.08 * (N_DP * SEQ_DEV * LEN) ** 0.5), 32.0, ((0, 4), (2, 4), (3, 2)), jnp.float32),
        "ada_first": normal_values(keys[12], (N_GRP, CD, 6, D), (0.08 * (N_DP * SEQ_DEV * LEN) ** 0.5), 32.0, ((0, 4), (1, 2), (3, 4)), jnp.float32),
        "small_first": normal_values(keys[13], (N_GRP, 9, D), (0.08 * (N_DP * SEQ_DEV * LEN) ** 0.5), 32.0, ((0, 4), (2, 2)), jnp.float32),
        "bias_first": normal_values(keys[14], (N_GRP, 4, D), (0.08 * (N_DP * SEQ_DEV * LEN) ** 0.5), 32.0, ((0, 4), (2, 8)), jnp.float32),
        "in_second": jnp.clip(jnp.exp(math.log(16.384) - 2.7725887 * jax.random.uniform(keys[15], (N_GRP, D, 7, D), jnp.float32) ** block_levels(keys[15], (N_GRP, D, 7, D), ((0, 4), (1, 2), (3, 4)), -0.2, 0.2)), 1.024, 16.384),
        "back_second": jnp.clip(jnp.exp(math.log(16.384) - 2.7725887 * jax.random.uniform(keys[16], (N_GRP, 5, D, D), jnp.float32) ** block_levels(keys[16], (N_GRP, 5, D, D), ((0, 4), (2, 4), (3, 2)), -0.2, 0.2)), 1.024, 16.384),
        "ada_second": jnp.clip(jnp.exp(math.log(16.384) - 2.7725887 * jax.random.uniform(keys[17], (N_GRP, CD, 6, D), jnp.float32) ** block_levels(keys[17], (N_GRP, CD, 6, D), ((0, 4), (1, 2), (3, 4)), -0.2, 0.2)), 1.024, 16.384),
        "small_second": jnp.clip(jnp.exp(math.log(16.384) - 2.7725887 * jax.random.uniform(keys[18], (N_GRP, 9, D), jnp.float32) ** block_levels(keys[18], (N_GRP, 9, D), ((0, 4), (2, 2)), -0.2, 0.2)), 1.024, 16.384),
        "bias_second": jnp.clip(jnp.exp(math.log(16.384) - 2.7725887 * jax.random.uniform(keys[19], (N_GRP, 4, D), jnp.float32) ** block_levels(keys[19], (N_GRP, 4, D), ((0, 4), (2, 8)), -0.2, 0.2)), 1.024, 16.384),
        "in_moment": normal_values(keys[20], (D, 7, D), 0.015, 0.09375, ((0, 2), (2, 4)), jnp.float32),
        "back_moment": normal_values(keys[21], (5, D, D), 0.015, 0.09375, ((1, 4), (2, 2)), jnp.float32),
        "ada_moment": normal_values(keys[22], (CD, 6, D), 0.015, 0.09375, ((0, 2), (2, 4)), jnp.float32),
        "small_moment": normal_values(keys[23], (9, D), 0.15, 0.875, ((1, 2),), jnp.float32),
        "bias_moment": normal_values(keys[24], (4, D), 0.15, 0.875, ((1, 8),), jnp.float32),
    }


@jax.custom_vjp
def low(v):
    return lax.optimization_barrier(v.astype(jnp.bfloat16)).astype(jnp.float32)

@jax.custom_vjp
def low_back(v):
    return v

def low_keep(v):
    return (low(v), None)

def low_pass(kept, grad):
    return (grad,)

def back_keep(v):
    return (v, None)

def back_low(kept, grad):
    return (low(grad),)
low.defvjp(low_keep, low_pass)
low_back.defvjp(back_keep, back_low)
highest = lax.Precision.HIGHEST
norm_eps = 1e-05
beta_one = 0.9
beta_two = 0.999
adam_eps = 1e-08
decay_rate = 0.1
rate_matrix = 0.03
rate_small = 0.3
outer_mu = 0.9
outer_rate = 0.7

def layer_norm(values, gain_row):
    row_mean = lax.optimization_barrier(jnp.mean(values, axis=-1, keepdims=True))
    centered = values - row_mean
    variance = lax.optimization_barrier(jnp.mean(centered * centered, axis=-1, keepdims=True))
    return centered * lax.rsqrt(variance + norm_eps) * gain_row

def modulate(values, gain_row, shift_row, scale_row):
    return layer_norm(values, gain_row) * (1.0 + scale_row) + shift_row

def rotary(values):
    length = values.shape[-3]
    head_size = values.shape[-1]
    half_size = head_size // 2
    frequency = 10000.0 ** (-2.0 * jnp.arange(half_size, dtype=jnp.float32) / head_size)
    angles = jnp.arange(length, dtype=jnp.float32)[:, None] * frequency[None, :]
    cosine = jnp.cos(angles)[:, None, :]
    sine_part = jnp.sin(angles)[:, None, :]
    lower = values[..., :half_size]
    upper = values[..., half_size:]
    return jnp.concatenate([lower * cosine - upper * sine_part, upper * cosine + lower * sine_part], axis=-1)

def gelu_tanh(values):
    return 0.5 * values * (1.0 + jnp.tanh(0.7978845608028654 * (values + 0.044715 * values * values * values)))

def attend_rows(query_rows, key_rows, value_rows):
    scores = low_back(jnp.einsum('rhe,khe->hrk', query_rows, key_rows, precision=highest) * 0.125)
    shifted = jnp.exp(scores - lax.optimization_barrier(jnp.max(scores, axis=-1, keepdims=True)))
    attn_probs = low(shifted / lax.optimization_barrier(jnp.sum(shifted, axis=-1, keepdims=True)))
    return low(low_back(jnp.einsum('hrk,khe->rhe', attn_probs, value_rows, precision=highest)))

def forward(params, token_rows, condition):
    in_weight, back_weight, ada_weight, small_params, up_bias = params
    in_matrix = low(in_weight)
    back_matrix = low(back_weight)
    ada_matrix = low(ada_weight)
    small_rows = low(small_params)
    bias_rows = low(up_bias)
    modulation = jnp.einsum('sc,cad->sad', low(condition), ada_matrix, precision=highest) + small_rows[3:9][None]
    up_weight = in_matrix[:, 3:7, :].reshape(D, FF)
    down_weight = back_matrix[1:5].reshape(FF, D)
    row_block = min(512, LEN)

    def one_sequence(inputs):
        values_in, mod_rows = inputs
        first_hidden = low(modulate(values_in, small_rows[0], mod_rows[0], mod_rows[1]))
        projected = low_back(jnp.einsum('ld,dae->lae', first_hidden, in_matrix[:, 0:3, :], precision=highest))
        queries = low(rotary(projected[:, 0].reshape(LEN, HEADS, HEAD_DIM)))
        key_rows = low(rotary(projected[:, 1].reshape(LEN, HEADS, HEAD_DIM)))
        value_rows = low(projected[:, 2].reshape(LEN, HEADS, HEAD_DIM))
        blocks = queries.reshape(LEN // row_block, row_block, HEADS, HEAD_DIM)
        mixed_heads = lax.map(jax.checkpoint(lambda query_rows: attend_rows(query_rows, key_rows, value_rows)), blocks)
        attended = jnp.dot(mixed_heads.reshape(LEN, D), back_matrix[0], precision=highest)
        after_attn = values_in + mod_rows[2] * low_back(attended)
        second_hidden = low(modulate(after_attn, small_rows[1], mod_rows[3], mod_rows[4]))
        pre_act = low_back(jnp.dot(second_hidden, up_weight, precision=highest) + bias_rows.reshape(FF))
        activation_values = low(gelu_tanh(pre_act))
        branch = low_back(jnp.dot(activation_values, down_weight, precision=highest) + small_rows[2])
        return after_attn + mod_rows[5] * branch
    return lax.map(one_sequence, (token_rows, modulation))

def adam_step(weight, gradient, first_moment, second_moment, rate, decay):
    first_new = beta_one * first_moment + (1.0 - beta_one) * gradient
    second_new = beta_two * second_moment + (1.0 - beta_two) * gradient * gradient
    first_hat = first_new / (1.0 - beta_one ** STEP)
    second_hat = second_new / (1.0 - beta_two ** STEP)
    return (first_new, second_new, weight - rate * (first_hat / (jnp.sqrt(second_hat) + adam_eps) + decay * weight))

def reference(tokens, sigma_index, absorbed, cotangent, time_table, in_weight, back_weight, ada_weight, small_params, up_bias, in_first, back_first, ada_first, small_first, bias_first, in_second, back_second, ada_second, small_second, bias_second, in_moment, back_moment, ada_moment, small_moment, bias_moment):
    params = (in_weight, back_weight, ada_weight, small_params, up_bias)
    firsts = (in_first, back_first, ada_first, small_first, bias_first)
    seconds = (in_second, back_second, ada_second, small_second, bias_second)
    moments = (in_moment, back_moment, ada_moment, small_moment, bias_moment)
    rates = (rate_matrix, rate_matrix, rate_matrix, rate_small, rate_small)
    decays = (decay_rate, decay_rate, decay_rate, 0.0, 0.0)
    group_rows = N_DP * SEQ_DEV

    def by_group(array):
        shaped = array.reshape((N_DP, N_GRP, SEQ_DEV) + array.shape[1:])
        return jnp.swapaxes(shaped, 0, 1).reshape((N_GRP, group_rows) + array.shape[1:])

    def from_group(array):
        shaped = array.reshape((N_GRP, N_DP, SEQ_DEV) + array.shape[2:])
        return jnp.swapaxes(shaped, 0, 1).reshape((N_GRP * N_DP * SEQ_DEV,) + array.shape[2:])
    token_groups = by_group(tokens.astype(jnp.float32))
    condition_groups = by_group(jax.nn.silu(time_table[sigma_index]))
    grad_groups = by_group(cotangent.astype(jnp.float32) * absorbed.astype(jnp.float32)[:, :, None])
    outputs = []
    input_grads = []
    new_firsts = [[], [], [], [], []]
    new_seconds = [[], [], [], [], []]
    diff_totals = [jnp.zeros_like(item) for item in params]
    for group in range(N_GRP):
        condition = condition_groups[group]
        result, pull = jax.vjp(lambda weights, rows: forward(weights, rows, condition), params, token_groups[group])
        param_grads, token_grad = pull(grad_groups[group])
        outputs.append(result)
        input_grads.append(token_grad)
        for which in range(5):
            first_new, second_new, weight_group = adam_step(params[which], param_grads[which], firsts[which][group], seconds[which][group], rates[which], decays[which])
            new_firsts[which].append(first_new)
            new_seconds[which].append(second_new)
            diff_totals[which] = diff_totals[which] + (params[which] - weight_group)
    block_out = from_group(jnp.stack(outputs)).astype(jnp.bfloat16)
    input_grad = from_group(jnp.stack(input_grads))
    first_out = [jnp.stack(item) for item in new_firsts]
    second_out = [jnp.stack(item) for item in new_seconds]
    diffs = [item / N_GRP for item in diff_totals]
    moment_out = [outer_mu * moments[which] + diffs[which] for which in range(5)]
    weight_out = [params[which] - outer_rate * (diffs[which] + outer_mu * moment_out[which]) for which in range(5)]
    return (block_out, input_grad, first_out[0], first_out[1], first_out[2], first_out[3], first_out[4], second_out[0], second_out[1], second_out[2], second_out[3], second_out[4], weight_out[0], weight_out[1], weight_out[2], weight_out[3], weight_out[4], diffs[0], diffs[1], diffs[2], diffs[3], diffs[4], moment_out[0], moment_out[1], moment_out[2], moment_out[3], moment_out[4])
```

```python
import functools

import jax
import jax.numpy as jnp
import numpy as np
from jax import lax
from jax.experimental import pallas as pl
from jax.experimental.pallas import tpu as pltpu
from jax.sharding import PartitionSpec as P

HEAD_DIM = 64
STEP = 10
MESH = pl.DeviceIdType.MESH
ANY = pl.BlockSpec(memory_space=pl.ANY)
VMEM = pl.BlockSpec(memory_space=pltpu.VMEM)
MIB = 2**20

f32 = jnp.float32
bf16 = jnp.bfloat16
highest = lax.Precision.HIGHEST
norm_eps = 1e-05
beta_one = 0.9
beta_two = 0.999
adam_eps = 1e-08
decay_rate = 0.1
rate_matrix = 0.03
rate_small = 0.3
outer_mu = 0.9
outer_rate = 0.7
gelu_a = 0.7978845608028654
gelu_b = 0.044715


def nn(a, b):
    return lax.dot_general(a, b, (((1,), (0,)), ((), ())), preferred_element_type=f32)


def nt(a, b):
    return lax.dot_general(a, b, (((1,), (1,)), ((), ())), preferred_element_type=f32)


def tn(a, b):
    return lax.dot_general(a, b, (((0,), (0,)), ((), ())), preferred_element_type=f32)


def fold(values):
    return jnp.sum(values.reshape(values.shape[0] // 8, 8, values.shape[1]), axis=0)


def normalize(values):
    mean = jnp.mean(values, axis=-1, keepdims=True)
    centered = values - mean
    variance = jnp.mean(centered * centered, axis=-1, keepdims=True)
    inverse = lax.rsqrt(variance + norm_eps)
    return centered * inverse, inverse


def norm_pull(grad_hat, hat, inverse):
    first = jnp.mean(grad_hat, axis=-1, keepdims=True)
    second = jnp.mean(grad_hat * hat, axis=-1, keepdims=True)
    return inverse * (grad_hat - first - hat * second)


def adam_parts(gradient, first, second):
    first_new = beta_one * first + (1.0 - beta_one) * gradient
    second_new = beta_two * second + (1.0 - beta_two) * gradient * gradient
    return first_new, second_new


def adam_diff(weight, first_new, second_new, rate, decay):
    first_hat = first_new / (1.0 - beta_one**STEP)
    second_hat = second_new / (1.0 - beta_two**STEP)
    return rate * (first_hat / (jnp.sqrt(second_hat) + adam_eps) + decay * weight)


def mod_kernel(cores, cond, wa, ps, bu, mod_out, ps_out, bu_out, c_got, parts, got, ps_low, bu_low, csem, psem, bsem, msem):
    t, d = lax.axis_index("tp"), lax.axis_index("dp")
    n_tp = mod_out.shape[0]
    s = t // cores
    c = lax.rem(t, cores)
    barrier = pltpu.get_barrier_semaphore()
    others = []
    for dt in range(n_tp):
        for dd in range(2):
            if dt or dd:
                others.append((lax.rem(t + dt, n_tp), lax.rem(d + dd, 2)))
    for pt, pd in others:
        pl.semaphore_signal(barrier, inc=1, device_id={"tp": pt, "dp": pd}, device_id_type=MESH)
    pl.semaphore_wait(barrier, len(others))
    cc = pltpu.make_async_remote_copy(
        src_ref=cond.at[1 - d], dst_ref=c_got, send_sem=csem.at[0], recv_sem=csem.at[1],
        device_id={"dp": 1 - d}, device_id_type=MESH)
    cc.start()
    ps_low[...] = ps[...].astype(bf16).astype(f32)
    bu_low[...] = bu[...].astype(bf16).astype(f32)
    ps_out[d] = ps_low[...]
    bu_out[s, d] = bu_low[...]
    pc = pltpu.make_async_remote_copy(
        src_ref=ps_low, dst_ref=ps_out.at[d], send_sem=psem.at[0], recv_sem=psem.at[1],
        device_id={"dp": 1 - d}, device_id_type=MESH)
    pc.start()
    bcs = []
    for ds, dd in ((0, 1), (1, 0), (1, 1)):
        bc = pltpu.make_async_remote_copy(
            src_ref=bu_low, dst_ref=bu_out.at[s, d], send_sem=bsem.at[0, ds, dd], recv_sem=bsem.at[1, ds, dd],
            device_id={"tp": lax.rem(s + ds, 2) * cores + c, "dp": lax.rem(d + dd, 2)}, device_id_type=MESH)
        bc.start()
        bcs.append(bc)
    parts[...] = jnp.zeros_like(parts)
    mine = cond[d].astype(bf16)
    for a in range(6):
        product = nn(mine, wa[a].astype(bf16))
        for ss in range(2):
            parts[d, ss, a : a + 1, :] = product[ss : ss + 1]
    cc.wait()
    theirs = c_got[...].astype(bf16)
    for a in range(6):
        product = nn(theirs, wa[a].astype(bf16))
        for ss in range(2):
            parts[1 - d, ss, a : a + 1, :] = product[ss : ss + 1]
    sends = []
    for i, (pt, pd) in enumerate(others):
        mc = pltpu.make_async_remote_copy(
            src_ref=parts.at[pd, pt // cores], dst_ref=got.at[t, d], send_sem=msem.at[0, i], recv_sem=msem.at[1, i],
            device_id={"tp": pt, "dp": pd}, device_id_type=MESH)
        mc.start()
        sends.append(mc)
    got[t, d] = parts[d, s]
    for mc in sends:
        mc.wait()
    pc.wait()
    for bc in bcs:
        bc.wait()
    mod_out[...] = got[:, 0] + got[:, 1]


def exchange_modulation(cores, cond, wa, ps, bu):
    n_tp = lax.axis_size("tp")
    half_c, width = wa.shape[1:]
    return pl.pallas_call(
        functools.partial(mod_kernel, cores),
        out_shape=(
            jax.ShapeDtypeStruct((n_tp, 8, width), f32),
            jax.ShapeDtypeStruct((2,) + ps.shape, f32),
            jax.ShapeDtypeStruct((2, 2) + bu.shape, f32),
        ),
        in_specs=[VMEM] * 4,
        out_specs=(VMEM,) * 3,
        scratch_shapes=[
            pltpu.VMEM((8, half_c), f32),
            pltpu.VMEM((2, 2, 8, width), f32),
            pltpu.VMEM((n_tp, 2, 8, width), f32),
            pltpu.VMEM(ps.shape, f32),
            pltpu.VMEM(bu.shape, f32),
            pltpu.SemaphoreType.DMA((2,)),
            pltpu.SemaphoreType.DMA((2,)),
            pltpu.SemaphoreType.DMA((2, 2, 2)),
            pltpu.SemaphoreType.DMA((2, 2 * n_tp - 1)),
        ],
        compiler_params=pltpu.CompilerParams(collective_id=0, has_side_effects=True),
        name="mod_exchange",
    )(cond, wa, ps, bu)


def gather_kernel(cores, wi, wb, wq, wo, wu, wd, lsem, ssem, rsem):
    t, d = lax.axis_index("tp"), lax.axis_index("dp")
    s = t // cores
    c = lax.rem(t, cores)
    rows, cols = wi.shape[1:]
    xdev = {"dp": 1 - d}
    ydev = {"tp": (1 - s) * cores + c}

    def block(a, ss, dd):
        where = (pl.ds(pl.multiple_of(ss * rows, 16), rows), pl.ds(pl.multiple_of(dd * cols, 128), cols))
        if a < 3:
            return wq.at[(a,) + where]
        if a == 3:
            return wo.at[where]
        if a < 8:
            return wu.at[(a - 4,) + where]
        return wd.at[(a - 8,) + where]

    def own(a):
        if a < 3:
            return wi.at[a]
        if a == 3:
            return wb.at[0]
        if a < 8:
            return wi.at[a - 1]
        return wb.at[a - 7]

    def remote(kind, a, source, target, device):
        return pltpu.make_async_remote_copy(
            src_ref=source, dst_ref=target, send_sem=ssem.at[kind, a], recv_sem=rsem.at[kind, a],
            device_id=device, device_id_type=MESH)

    barrier = pltpu.get_barrier_semaphore()
    for dev in (xdev, ydev):
        pl.semaphore_signal(barrier, inc=1, device_id=dev, device_id_type=MESH)
    pl.semaphore_wait(barrier, 2)
    xs, ys, zs, ls = [], [], [], []
    for a in range(12):
        xs.append(remote(0, a, own(a), block(a, s, d), xdev))
        ys.append(remote(1, a, own(a), block(a, s, d), ydev))
        xs[a].start()
        ys[a].start()
        ls.append(pltpu.make_async_copy(own(a), block(a, s, d), lsem.at[a]))
        ls[a].start()
    for a in range(12):
        if a % 2 == 0:
            xs[a].wait_recv()
            zs.append(remote(2, a, block(a, s, 1 - d), block(a, s, 1 - d), ydev))
        else:
            ys[a].wait_recv()
            zs.append(remote(2, a, block(a, 1 - s, d), block(a, 1 - s, d), xdev))
        zs[a].start()
    for a in range(12):
        xs[a].wait_send()
        ys[a].wait_send()
        (ys if a % 2 == 0 else xs)[a].wait_recv()
        zs[a].wait()
        ls[a].wait()


def gather_weights(cores, wi, wb):
    rows, cols = wi.shape[1:]
    full = (2 * rows, 2 * cols)
    return pl.pallas_call(
        functools.partial(gather_kernel, cores),
        out_shape=(
            jax.ShapeDtypeStruct((3,) + full, bf16),
            jax.ShapeDtypeStruct(full, bf16),
            jax.ShapeDtypeStruct((4,) + full, bf16),
            jax.ShapeDtypeStruct((4,) + full, bf16),
        ),
        in_specs=[ANY, ANY],
        out_specs=(ANY,) * 4,
        scratch_shapes=[
            pltpu.SemaphoreType.DMA((12,)),
            pltpu.SemaphoreType.DMA((3, 12)),
            pltpu.SemaphoreType.DMA((3, 12)),
        ],
        compiler_params=pltpu.CompilerParams(collective_id=1, has_side_effects=True),
        name="weight_gather",
    )(wi, wb)


def turn(values, cosine, sine):
    heads = values.shape[0] // HEAD_DIM
    half = HEAD_DIM // 2
    out = []
    for h in range(heads):
        low = values[h * HEAD_DIM : h * HEAD_DIM + half]
        high = values[h * HEAD_DIM + half : (h + 1) * HEAD_DIM]
        out.append(low * cosine - high * sine)
        out.append(high * cosine + low * sine)
    return jnp.concatenate(out, axis=0)


def project_kernel(tok, vecs, wq, cosine, sine, h1, q_t, k_t, v_t, k_r, v_r):
    hat, _ = normalize(tok[...].astype(f32))
    hidden = hat * vecs[0:1] * (1.0 + vecs[4:5]) + vecs[3:4]
    low = hidden.astype(bf16)
    h1[...] = low
    cos, sin = cosine[...], sine[...]
    q_t[...] = (turn(nt(wq[0], low), cos, sin) * 0.125).astype(bf16)
    keys = turn(nt(wq[1], low), cos, sin)
    k_t[...] = keys.astype(bf16)
    k_r[...] = keys.T.astype(bf16)
    values = nt(wq[2], low)
    v_t[...] = values.astype(bf16)
    v_r[...] = values.T.astype(bf16)


def project(tok, vecs, wq, cosine, sine):
    length, width = tok.shape
    heads_width = wq.shape[1]
    step = 256
    half = HEAD_DIM // 2
    return pl.pallas_call(
        project_kernel,
        grid=(length // step,),
        out_shape=(
            jax.ShapeDtypeStruct((length, width), bf16),
            jax.ShapeDtypeStruct((heads_width, length), bf16),
            jax.ShapeDtypeStruct((heads_width, length), bf16),
            jax.ShapeDtypeStruct((heads_width, length), bf16),
            jax.ShapeDtypeStruct((length, heads_width), bf16),
            jax.ShapeDtypeStruct((length, heads_width), bf16),
        ),
        in_specs=[
            pl.BlockSpec((step, width), lambda i: (i, 0)),
            pl.BlockSpec(vecs.shape, lambda i: (0, 0)),
            pl.BlockSpec(wq.shape, lambda i: (0, 0, 0)),
            pl.BlockSpec((half, step), lambda i: (0, i)),
            pl.BlockSpec((half, step), lambda i: (0, i)),
        ],
        out_specs=(
            pl.BlockSpec((step, width), lambda i: (i, 0)),
            pl.BlockSpec((heads_width, step), lambda i: (0, i)),
            pl.BlockSpec((heads_width, step), lambda i: (0, i)),
            pl.BlockSpec((heads_width, step), lambda i: (0, i)),
            pl.BlockSpec((step, heads_width), lambda i: (i, 0)),
            pl.BlockSpec((step, heads_width), lambda i: (i, 0)),
        ),
        compiler_params=pltpu.CompilerParams(vmem_limit_bytes=48 * MIB),
        name="project",
    )(tok, vecs, wq, cosine, sine)


def only_head(pair, h):
    row = lax.broadcasted_iota(jnp.int32, pair.shape, 0)
    return jnp.where(row // HEAD_DIM == h, pair, jnp.zeros_like(pair))


def attend_kernel(k_r, q_t, v_t, probs, inv, o_t):
    for h in range(2):
        scores = nn(k_r[...], only_head(q_t[...], h))
        top = jnp.max(scores, axis=0, keepdims=True)
        shifted = jnp.exp(scores - top)
        inverse = 1.0 / jnp.sum(shifted, axis=0, keepdims=True)
        low = shifted.astype(bf16)
        probs[h] = low
        inv[0, h : h + 1, :] = inverse
        rows = slice(h * HEAD_DIM, (h + 1) * HEAD_DIM)
        o_t[rows, :] = (nn(v_t[rows, :], low) * inverse).astype(bf16)


def attend(k_r, q_t, v_t):
    length, heads_width = k_r.shape
    pairs = heads_width // (2 * HEAD_DIM)
    step = 256
    pw = 2 * HEAD_DIM
    return pl.pallas_call(
        attend_kernel,
        grid=(pairs, length // step),
        out_shape=(
            jax.ShapeDtypeStruct((2 * pairs, length, length), bf16),
            jax.ShapeDtypeStruct((pairs, 2, length), f32),
            jax.ShapeDtypeStruct((heads_width, length), bf16),
        ),
        in_specs=[
            pl.BlockSpec((length, pw), lambda p, i: (0, p)),
            pl.BlockSpec((pw, step), lambda p, i: (p, i)),
            pl.BlockSpec((pw, length), lambda p, i: (p, 0)),
        ],
        out_specs=(
            pl.BlockSpec((2, length, step), lambda p, i: (p, 0, i)),
            pl.BlockSpec((1, 2, step), lambda p, i: (p, 0, i)),
            pl.BlockSpec((pw, step), lambda p, i: (p, i)),
        ),
        compiler_params=pltpu.CompilerParams(vmem_limit_bytes=48 * MIB),
        name="attend",
    )(k_r, q_t, v_t)


def sibling_of(cores):
    t = lax.axis_index("tp")
    s = t // cores
    c = lax.rem(t, cores)
    return s, c, {"tp": s * cores + (1 - c)}


def greet(device):
    barrier = pltpu.get_barrier_semaphore()
    pl.semaphore_signal(barrier, inc=1, device_id=device, device_id_type=MESH)
    pl.semaphore_wait(barrier, 1)


def mix_kernel(cores, o_t, wo, tok, vecs, attn, x1, h2, away, got, tbuf, tsem, asem, hsem):
    s, c, sibling = sibling_of(cores)
    half = attn.shape[0]
    own = pl.ds(pl.multiple_of(c * half, 128), half)
    other = pl.ds(pl.multiple_of((1 - c) * half, 128), half)
    tc = pltpu.make_async_copy(tok.at[own], tbuf, tsem)
    tc.start()
    greet(sibling)
    away[...] = tn(o_t[:, other], wo[...])
    send = pltpu.make_async_remote_copy(
        src_ref=away, dst_ref=got, send_sem=asem.at[0], recv_sem=asem.at[1], device_id=sibling, device_id_type=MESH)
    send.start()
    attn[...] = tn(o_t[:, own], wo[...])
    tc.wait()
    send.wait()
    step = 128

    @pl.loop(0, half // step)
    def _(i):
        r = pl.ds(pl.multiple_of(i * step, step), step)
        total = attn[r] + got[r]
        attn[r] = total
        rows = tbuf[r].astype(f32) + vecs[5:6] * total
        x1[r] = rows
        hat, _ = normalize(rows)
        hidden = hat * vecs[1:2] * (1.0 + vecs[7:8]) + vecs[6:7]
        h2[pl.ds(pl.multiple_of(c * half + i * step, step), step)] = hidden.astype(bf16)

    back = pltpu.make_async_remote_copy(
        src_ref=h2.at[own], dst_ref=h2.at[own], send_sem=hsem.at[0], recv_sem=hsem.at[1],
        device_id=sibling, device_id_type=MESH)
    back.start()
    back.wait()


def mix(cores, o_t, wo, tok, vecs):
    length, width = tok.shape
    half = length // cores
    return pl.pallas_call(
        functools.partial(mix_kernel, cores),
        out_shape=(
            jax.ShapeDtypeStruct((half, width), f32),
            jax.ShapeDtypeStruct((half, width), f32),
            jax.ShapeDtypeStruct((length, width), bf16),
        ),
        in_specs=[VMEM, VMEM, ANY, VMEM],
        out_specs=(VMEM,) * 3,
        scratch_shapes=[
            pltpu.VMEM((half, width), f32),
            pltpu.VMEM((half, width), f32),
            pltpu.VMEM((half, width), bf16),
            pltpu.SemaphoreType.DMA,
            pltpu.SemaphoreType.DMA((2,)),
            pltpu.SemaphoreType.DMA((2,)),
        ],
        compiler_params=pltpu.CompilerParams(collective_id=2, has_side_effects=True, vmem_limit_bytes=48 * MIB),
        name="attention_mix",
    )(o_t, wo, tok, vecs)


def feed_kernel(h2, gy, vecs, bias, wu, wd, mlp, dh2, gu, gd, gb, z_s, du_s, gm_s, b_s):
    length, width = h2.shape
    hidden = wu.shape[0]
    chunk = width
    step = 256
    b_s[...] = jnp.zeros_like(b_s)

    @pl.loop(0, length // step)
    def _(i):
        r = pl.ds(pl.multiple_of(i * step, step), step)
        rows = h2[r]
        gm = (gy[r].astype(f32) * vecs[8:9]).astype(bf16)
        gm_s[r] = gm
        forward = jnp.zeros((step, width), f32)
        backward = jnp.zeros((step, width), f32)
        for j in range(hidden // chunk):
            cols = slice(j * chunk, (j + 1) * chunk)
            u = nt(rows, wu[cols]) + bias[:, cols]
            square = u * u
            inner = jnp.tanh(gelu_a * (u + gelu_b * square * u))
            z = (0.5 * u * (1.0 + inner)).astype(bf16)
            slope = 0.5 * (1.0 + inner) + 0.5 * u * (1.0 - inner * inner) * gelu_a * (1.0 + 3.0 * gelu_b * square)
            du = (nt(gm, wd[cols]) * slope).astype(bf16)
            z_s[r, cols] = z
            du_s[r, cols] = du
            b_s[:, cols] += fold(du.astype(f32))
            forward += nn(z, wd[cols])
            backward += nn(du, wu[cols])
        mlp[r] = forward.astype(bf16)
        dh2[r] = backward.astype(bf16)

    gb[...] = jnp.sum(b_s[...], axis=0, keepdims=True)
    for j in range(hidden // step):
        cols = slice(j * step, (j + 1) * step)
        gd[cols] = tn(z_s[:, cols], gm_s[...]).astype(bf16)
        gu[cols] = tn(du_s[:, cols], h2[...]).astype(bf16)


def feed(h2, gy, vecs, bias, wu, wd):
    length, width = h2.shape
    hidden = wu.shape[0]
    return pl.pallas_call(
        feed_kernel,
        out_shape=(
            jax.ShapeDtypeStruct((length, width), bf16),
            jax.ShapeDtypeStruct((length, width), bf16),
            jax.ShapeDtypeStruct((hidden, width), bf16),
            jax.ShapeDtypeStruct((hidden, width), bf16),
            jax.ShapeDtypeStruct((1, hidden), f32),
        ),
        in_specs=[VMEM] * 6,
        out_specs=(VMEM,) * 5,
        scratch_shapes=[
            pltpu.VMEM((length, hidden), bf16),
            pltpu.VMEM((length, hidden), bf16),
            pltpu.VMEM((length, width), bf16),
            pltpu.VMEM((8, hidden), f32),
        ],
        compiler_params=pltpu.CompilerParams(vmem_limit_bytes=56 * MIB),
        name="feed_forward",
    )(h2, gy, vecs, bias, wu, wd)


def middle_kernel(cores, mlp, dh2, x1, attn, gy, vecs, out, dx1, ga, stats, got, acc, msem, gsem):
    s, c, sibling = sibling_of(cores)
    half = x1.shape[0]
    own = pl.ds(pl.multiple_of(c * half, 128), half)
    other = pl.ds(pl.multiple_of((1 - c) * half, 128), half)
    greet(sibling)
    sends = []
    for i, ref in enumerate((mlp, dh2)):
        cp = pltpu.make_async_remote_copy(
            src_ref=ref.at[other], dst_ref=got.at[i], send_sem=msem.at[0, i], recv_sem=msem.at[1, i],
            device_id=sibling, device_id_type=MESH)
        cp.start()
        sends.append(cp)
    acc[...] = jnp.zeros_like(acc)
    for cp in sends:
        cp.wait()
    step = 128

    @pl.loop(0, half // step)
    def _(i):
        r = pl.ds(pl.multiple_of(i * step, step), step)
        g = pl.ds(pl.multiple_of(c * half + i * step, step), step)
        rows = x1[r]
        branch = mlp[g].astype(f32) + got[0, r].astype(f32) + vecs[2:3]
        out[r] = (rows + vecs[8:9] * branch).astype(bf16)
        grad = gy[g].astype(f32)
        dh = dh2[g].astype(f32) + got[1, r].astype(f32)
        hat, inverse = normalize(rows)
        acc[0] += fold(dh)
        acc[1] += fold(dh * hat)
        total = grad + norm_pull(dh * (vecs[1:2] * (1.0 + vecs[7:8])), hat, inverse)
        dx1[r] = total
        acc[2] += fold(total * attn[r])
        acc[3] += fold(grad * branch)
        acc[4] += fold((vecs[8:9] * grad).astype(bf16).astype(f32))
        ga[g] = (vecs[5:6] * total).astype(bf16)

    back = pltpu.make_async_remote_copy(
        src_ref=ga.at[own], dst_ref=ga.at[own], send_sem=gsem.at[0], recv_sem=gsem.at[1],
        device_id=sibling, device_id_type=MESH)
    back.start()
    stats[...] = jnp.zeros_like(stats)
    for i in range(5):
        stats[i : i + 1] = jnp.sum(acc[i], axis=0, keepdims=True)
    back.wait()


def middle(cores, mlp, dh2, x1, attn, gy, vecs):
    length, width = mlp.shape
    half = length // cores
    return pl.pallas_call(
        functools.partial(middle_kernel, cores),
        out_shape=(
            jax.ShapeDtypeStruct((half, width), bf16),
            jax.ShapeDtypeStruct((half, width), f32),
            jax.ShapeDtypeStruct((length, width), bf16),
            jax.ShapeDtypeStruct((8, width), f32),
        ),
        in_specs=[VMEM] * 6,
        out_specs=(VMEM,) * 4,
        scratch_shapes=[
            pltpu.VMEM((2, half, width), bf16),
            pltpu.VMEM((5, 8, width), f32),
            pltpu.SemaphoreType.DMA((2, 2)),
            pltpu.SemaphoreType.DMA((2,)),
        ],
        compiler_params=pltpu.CompilerParams(collective_id=3, has_side_effects=True, vmem_limit_bytes=48 * MIB),
        name="middle",
    )(mlp, dh2, x1, attn, gy, vecs)


def pull_kernel(ga, wo, o_t, inv, probs, q_t, k_t, v_t, v_r, cosine, sine, h1, wq, dh1, gq, go, do_s, ds_s, dqkv):
    p = pl.program_id(0)
    length, width = ga.shape
    pw = 2 * HEAD_DIM
    heads_width = wq.shape[1]
    step = 256
    do_t = nt(wo[...], ga[...])
    go[...] = nn(o_t[...], ga[...]).astype(bf16)
    for h in range(2):
        rows = slice(h * HEAD_DIM, (h + 1) * HEAD_DIM)
        do_s[rows] = (do_t[rows] * inv[0, h : h + 1, :]).astype(bf16)
    raw = []
    for h in range(2):
        rows = slice(h * HEAD_DIM, (h + 1) * HEAD_DIM)
        delta = jnp.sum(do_s[rows].astype(f32) * o_t[rows].astype(f32), axis=0, keepdims=True)
        dq = []
        for i in range(length // step):
            cols = slice(i * step, (i + 1) * step)
            dp = nn(v_r[...], only_head(do_s[:, cols], h))
            ds = (probs[h, :, cols].astype(f32) * (dp - delta[:, cols])).astype(bf16)
            ds_s[:, cols] = ds
            dq.append(nn(k_t[rows], ds))
        dk = nt(q_t[rows], ds_s[...])
        dv = nt(do_s[rows], probs[h])
        raw.append((jnp.concatenate(dq, axis=1) * 0.125, dk, dv))
    cos, sin = cosine[...], sine[...]
    for k in range(3):
        both = jnp.concatenate([raw[0][k], raw[1][k]], axis=0)
        if k < 2:
            both = turn(both, cos, -sin)
        at = pl.multiple_of(k * heads_width + p * pw, pw)
        dqkv[pl.ds(at, pw)] = both.astype(bf16)

    @pl.when(p == pl.num_programs(0) - 1)
    def _():
        for k in range(3):
            part = slice(k * heads_width, (k + 1) * heads_width)
            gq[k] = nn(dqkv[part], h1[...]).astype(bf16)

        @pl.loop(0, length // step)
        def _(i):
            r = pl.ds(pl.multiple_of(i * step, step), step)
            total = jnp.zeros((step, width), f32)
            for k in range(3):
                part = slice(k * heads_width, (k + 1) * heads_width)
                total += tn(dqkv[part, r], wq[k])
            dh1[r] = total.astype(bf16)


def pull_attention(ga, wo, o_t, inv, probs, q_t, k_t, v_r, cosine, sine, h1, wq):
    length, width = ga.shape
    heads_width = wq.shape[1]
    pw = 2 * HEAD_DIM
    pairs = heads_width // pw
    half = HEAD_DIM // 2

    def body(ga, wo, o_t, inv, probs, q_t, k_t, v_r, cosine, sine, h1, wq, *rest):
        return pull_kernel(ga, wo, o_t, inv, probs, q_t, k_t, None, v_r, cosine, sine, h1, wq, *rest)

    return pl.pallas_call(
        body,
        grid=(pairs,),
        out_shape=(
            jax.ShapeDtypeStruct((length, width), bf16),
            jax.ShapeDtypeStruct((3, heads_width, width), bf16),
            jax.ShapeDtypeStruct((heads_width, width), bf16),
        ),
        in_specs=[
            pl.BlockSpec((length, width), lambda p: (0, 0)),
            pl.BlockSpec((pw, width), lambda p: (p, 0)),
            pl.BlockSpec((pw, length), lambda p: (p, 0)),
            pl.BlockSpec((1, 2, length), lambda p: (p, 0, 0)),
            pl.BlockSpec((2, length, length), lambda p: (p, 0, 0)),
            pl.BlockSpec((pw, length), lambda p: (p, 0)),
            pl.BlockSpec((pw, length), lambda p: (p, 0)),
            pl.BlockSpec((length, pw), lambda p: (0, p)),
            pl.BlockSpec((half, length), lambda p: (0, 0)),
            pl.BlockSpec((half, length), lambda p: (0, 0)),
            pl.BlockSpec((length, width), lambda p: (0, 0)),
            pl.BlockSpec((3, heads_width, width), lambda p: (0, 0, 0)),
        ],
        out_specs=(
            pl.BlockSpec((length, width), lambda p: (0, 0)),
            pl.BlockSpec((3, heads_width, width), lambda p: (0, 0, 0)),
            pl.BlockSpec((pw, width), lambda p: (p, 0)),
        ),
        scratch_shapes=[
            pltpu.VMEM((pw, length), bf16),
            pltpu.VMEM((length, length), bf16),
            pltpu.VMEM((3 * heads_width, length), bf16),
        ],
        compiler_params=pltpu.CompilerParams(vmem_limit_bytes=56 * MIB),
        name="attention_pull",
    )(ga, wo, o_t, inv, probs, q_t, k_t, v_r, cosine, sine, h1, wq)


def last_kernel(cores, spans, dh1, dx1, tok, out, vecs, stats, gb, cond, block_out, grad_out, shared,
                got, tbuf, grad, acc, small, dsem, tsem, osem, fsem, lsem, vsem):
    t, d = lax.axis_index("tp"), lax.rem(lax.axis_index("dp"), spans)
    n_tp = shared.shape[0]
    s, c, sibling = sibling_of(cores)
    across = {"tp": (1 - s) * cores + c}
    half = dx1.shape[0]
    own = pl.ds(pl.multiple_of(c * half, 128), half)
    other = pl.ds(pl.multiple_of((1 - c) * half, 128), half)
    barrier = pltpu.get_barrier_semaphore()
    others = []
    for dt in range(n_tp):
        for dd in range(spans):
            if dt or dd:
                dev = {"tp": lax.rem(t + dt, n_tp)}
                if spans > 1:
                    dev["dp"] = lax.rem(d + dd, spans)
                others.append(dev)
    for dev in others:
        pl.semaphore_signal(barrier, inc=1, device_id=dev, device_id_type=MESH)
    tc = pltpu.make_async_copy(tok.at[own], tbuf, tsem)
    tc.start()
    pl.semaphore_wait(barrier, len(others))

    def spread(kind, source, target):
        copies = []
        for i, dev in enumerate((sibling, across)):
            copies.append(pltpu.make_async_remote_copy(
                src_ref=source, dst_ref=target.at[s, own], send_sem=osem.at[0, kind, i], recv_sem=osem.at[1, kind, i],
                device_id=dev, device_id_type=MESH))
            copies[i].start()
        local = pltpu.make_async_copy(source, target.at[s, own], lsem.at[kind])
        local.start()
        return copies, local

    def pass_on(kind, copies, target):
        copies[1].wait_recv()
        forward = pltpu.make_async_remote_copy(
            src_ref=target.at[1 - s, own], dst_ref=target.at[1 - s, own], send_sem=fsem.at[0, kind],
            recv_sem=fsem.at[1, kind], device_id=sibling, device_id_type=MESH)
        forward.start()
        return forward

    first = pltpu.make_async_remote_copy(
        src_ref=dh1.at[other], dst_ref=got, send_sem=dsem.at[0], recv_sem=dsem.at[1],
        device_id=sibling, device_id_type=MESH)
    first.start()
    ocopies, olocal = spread(0, out, block_out)
    acc[...] = jnp.zeros_like(acc)
    tc.wait()
    first.wait()
    step = 128

    @pl.loop(0, half // step)
    def _(i):
        r = pl.ds(pl.multiple_of(i * step, step), step)
        g = pl.ds(pl.multiple_of(c * half + i * step, step), step)
        dh = dh1[g].astype(f32) + got[r].astype(f32)
        hat, inverse = normalize(tbuf[r].astype(f32))
        acc[0] += fold(dh)
        acc[1] += fold(dh * hat)
        total = dx1[r] + norm_pull(dh * (vecs[0:1] * (1.0 + vecs[4:5])), hat, inverse)
        grad[r] = total.astype(bf16)

    gcopies, glocal = spread(1, grad, grad_out)
    shift1 = jnp.sum(acc[0], axis=0, keepdims=True)
    turn1 = jnp.sum(acc[1], axis=0, keepdims=True)
    small[...] = jnp.zeros_like(small)
    small[0:1] = shift1
    small[1:2] = turn1 * vecs[0:1]
    small[2:3] = stats[2:3]
    small[3:4] = stats[0:1]
    small[4:5] = stats[1:2] * vecs[1:2]
    small[5:6] = stats[3:4]
    small[6:7] = turn1 * (1.0 + vecs[4:5])
    small[7:8] = stats[1:2] * (1.0 + vecs[7:8])
    small[8:9] = stats[4:5]
    small[9:11] = gb[...]
    small[11:12, 0 : cond.shape[1]] = cond[...]
    shared[t, d] = small[...]
    vsends = []
    for i, dev in enumerate(others):
        cp = pltpu.make_async_remote_copy(
            src_ref=small, dst_ref=shared.at[t, d], send_sem=vsem.at[0, i], recv_sem=vsem.at[1, i],
            device_id=dev, device_id_type=MESH)
        cp.start()
        vsends.append(cp)
    forwards = [pass_on(0, ocopies, block_out), pass_on(1, gcopies, grad_out)]
    for copies, local, forward in zip((ocopies, gcopies), (olocal, glocal), forwards):
        copies[0].wait()
        copies[1].wait_send()
        local.wait()
        forward.wait()
    for cp in vsends:
        cp.wait()


def last(cores, spans, seqs, dh1, dx1, tok, out, vecs, stats, gb, cond):
    length, width = tok.shape
    n_tp = lax.axis_size("tp")
    half = length // cores
    return pl.pallas_call(
        functools.partial(last_kernel, cores, spans),
        out_shape=(
            jax.ShapeDtypeStruct((seqs, length, width), bf16),
            jax.ShapeDtypeStruct((seqs, length, width), bf16),
            jax.ShapeDtypeStruct((n_tp, spans, 16, width), f32),
        ),
        in_specs=[VMEM, VMEM, ANY, ANY, VMEM, VMEM, VMEM, VMEM],
        out_specs=(ANY, ANY, VMEM),
        scratch_shapes=[
            pltpu.VMEM((half, width), bf16),
            pltpu.VMEM((half, width), bf16),
            pltpu.VMEM((half, width), bf16),
            pltpu.VMEM((2, 8, width), f32),
            pltpu.VMEM((16, width), f32),
            pltpu.SemaphoreType.DMA((2,)),
            pltpu.SemaphoreType.DMA,
            pltpu.SemaphoreType.DMA((2, 2, 2)),
            pltpu.SemaphoreType.DMA((2, 2)),
            pltpu.SemaphoreType.DMA((2,)),
            pltpu.SemaphoreType.DMA((2, spans * n_tp - 1)),
        ],
        compiler_params=pltpu.CompilerParams(collective_id=4, has_side_effects=True, vmem_limit_bytes=48 * MIB),
        name="last_norm",
    )(dh1, dx1, tok, out, vecs, stats, gb, cond)


def step_kernel(cores, gq, go, gu, gd, wi, wb, mi, mb, vi, vb, ea, es, eb,
                gsum, total, ta, ts, tb,
                grads, wts, firsts, seconds, got_a, send_b, got_b, diff, got_p, got_h, a_p, a_h, s_all, b_all, a_low, s_low, b_low,
                lsem, asem, bsem, psem, hsem, fsem, esem, ap_sem, ah_sem, af_sem, ss_sem, bs_sem):
    t, d, g = lax.axis_index("tp"), lax.axis_index("dp"), lax.axis_index("grp")
    s = t // cores
    c = lax.rem(t, cores)
    rows, cols = wi.shape[1:]
    xdev = {"dp": 1 - d}
    ydev = {"tp": (1 - s) * cores + c}
    inner = jnp.logical_or(g == 1, g == 2)
    outer = jnp.logical_not(inner)
    low_side = g < 2
    pair = jnp.where(g == 0, 1, jnp.where(g == 1, 0, jnp.where(g == 2, 3, 2)))
    pdev = {"grp": pair}
    mdev = {"grp": 3 - g}
    mine = jnp.where(g == 1, 0, 1)
    hrows = rows // 2

    def remote(source, target, send, recv, device):
        return pltpu.make_async_remote_copy(
            src_ref=source, dst_ref=target, send_sem=send, recv_sem=recv, device_id=device, device_id_type=MESH)

    def r_at(ss):
        return pl.ds(pl.multiple_of(ss * rows, 16), rows)

    def c_at(dd):
        return pl.ds(pl.multiple_of(dd * cols, 128), cols)

    loads = []
    for a in range(12):
        ref = gq.at[a] if a < 3 else gu.at[a - 3] if a < 7 else go if a == 7 else gd.at[a - 8]
        loads.append(pltpu.make_async_copy(ref, grads.at[a], lsem.at[a]))
    for i, (src, dst) in enumerate(((wi, wts), (mi, firsts), (vi, seconds))):
        loads.append(pltpu.make_async_copy(src, dst.at[pl.ds(0, 7)], lsem.at[12 + i]))
    for i, (src, dst) in enumerate(((wb, wts), (mb, firsts), (vb, seconds))):
        loads.append(pltpu.make_async_copy(src, dst.at[pl.ds(7, 5)], lsem.at[15 + i]))
    for cp in loads:
        cp.start()

    barrier = pltpu.get_barrier_semaphore()
    for dev in (xdev, ydev, {"grp": lax.rem(g + 1, 4)}, {"grp": lax.rem(g + 2, 4)}, {"grp": lax.rem(g + 3, 4)}):
        pl.semaphore_signal(barrier, inc=1, device_id=dev, device_id_type=MESH)
    pl.semaphore_wait(barrier, 5)

    a_low[...] = ea[...].astype(bf16)
    s_low[...] = es[...].astype(bf16).astype(f32)
    b_low[...] = eb[...].astype(bf16).astype(f32)
    tiny = []
    for i in range(3):
        dev = {"grp": lax.rem(g + 1 + i, 4)}
        tiny.append(remote(s_low, s_all.at[g], ss_sem.at[0, i], ss_sem.at[1, i], dev))
        tiny.append(remote(b_low, b_all.at[g], bs_sem.at[0, i], bs_sem.at[1, i], dev))
    for cp in tiny:
        cp.start()
    s_all[g] = s_low[...]
    b_all[g] = b_low[...]

    def first_send(a, k):
        if a % 2 == 0:
            return remote(grads.at[a, r_at(1 - s), pl.ds(k * cols, cols)], got_a.at[a, k], asem.at[0, a, k], asem.at[1, a, k], ydev)
        return remote(grads.at[a, pl.ds(k * rows, rows), c_at(1 - d)], got_a.at[a, k], asem.at[0, a, k], asem.at[1, a, k], xdev)

    def first_wait(a):
        for k in range(2):
            remote(got_a.at[a, k], got_a.at[a, k], asem.at[0, a, k], asem.at[1, a, k], xdev).wait()

    for a in range(12):
        loads[a].wait()
        for k in range(2):
            first_send(a, k).start()
    for cp in loads[12:]:
        cp.wait()

    def second_send(a, parity):
        dev = xdev if parity == 0 else ydev
        return remote(send_b.at[a], got_b.at[a], bsem.at[0, a], bsem.at[1, a], dev)

    def pair_send(a):
        return remote(diff.at[a], got_p.at[a], psem.at[0, a], psem.at[1, a], pdev)

    def h_at(k):
        return pl.ds(pl.multiple_of(k * hrows, 16), hrows)

    def half_send(a):
        return remote(got_p.at[a, h_at(1 - mine)], got_h.at[a], hsem.at[0, a], hsem.at[1, a], mdev)

    def final_mid(a):
        return remote(total.at[a, h_at(mine)], total.at[a, h_at(mine)], fsem.at[0, a, 0], fsem.at[1, a, 0], mdev)

    def final_pair(a):
        return remote(total.at[a, h_at(mine)], total.at[a, h_at(mine)], fsem.at[0, a, 1], fsem.at[1, a, 1], pdev)

    def final_pass(a):
        return remote(total.at[a, h_at(1 - mine)], total.at[a, h_at(1 - mine)], fsem.at[0, a, 2], fsem.at[1, a, 2], pdev)

    def stage_b(a, parity):
        first_wait(a)
        if parity == 0:
            send_b[a] = (grads[a, r_at(s), c_at(1 - d)].astype(f32) + got_a[a, 1 - d].astype(f32)).astype(bf16)
        else:
            send_b[a] = (grads[a, r_at(1 - s), c_at(d)].astype(f32) + got_a[a, 1 - s].astype(f32)).astype(bf16)
        second_send(a, parity).start()

    def stage_c(a, parity):
        second_send(a, parity).wait()
        keep = got_a[a, d] if parity == 0 else got_a[a, s]
        gradient = grads[a, r_at(s), c_at(d)].astype(f32) + keep.astype(f32) + got_b[a].astype(f32)
        gsum[a] = gradient
        first_new, second_new = adam_parts(gradient, firsts[a], seconds[a])
        diff[a] = adam_diff(wts[a], first_new, second_new, rate_matrix, decay_rate).astype(bf16)

        @pl.when(outer)
        def _():
            pair_send(a).start()

    def stage_d(a):
        pair_send(a).wait_recv()
        got_p[a] = (diff[a].astype(f32) + got_p[a].astype(f32)).astype(bf16)
        half_send(a).start()

    def stage_e(a):
        half_send(a).wait_recv()
        total[a, h_at(mine)] = (got_p[a, h_at(mine)].astype(f32) + got_h[a].astype(f32)).astype(bf16)
        final_mid(a).start()
        final_pair(a).start()

    def stage_f(a):
        remote(got_h.at[a], got_h.at[a], fsem.at[0, a, 0], fsem.at[1, a, 0], mdev).wait_recv()
        final_pass(a).start()

    n = 6

    @pl.loop(0, n + 4)
    def _(i):
        @pl.when(i < n)
        def _():
            for k in range(2):
                stage_b(2 * i + k, k)

        @pl.when(jnp.logical_and(i >= 1, i < n + 1))
        def _():
            for k in range(2):
                stage_c(2 * (i - 1) + k, k)

        @pl.when(jnp.logical_and(inner, jnp.logical_and(i >= 2, i < n + 2)))
        def _():
            for k in range(2):
                stage_d(2 * (i - 2) + k)

        @pl.when(jnp.logical_and(inner, jnp.logical_and(i >= 3, i < n + 3)))
        def _():
            for k in range(2):
                stage_e(2 * (i - 3) + k)

        @pl.when(jnp.logical_and(inner, i >= 4))
        def _():
            for k in range(2):
                stage_f(2 * (i - 4) + k)

    ah = a_low.shape[0] // 2

    def ada_at(ref, k):
        return ref.at[pl.ds(k * ah, ah)]

    a_pair = remote(a_low, a_p, ap_sem.at[0], ap_sem.at[1], pdev)
    a_half = remote(ada_at(a_p, 1 - mine), a_h, ah_sem.at[0], ah_sem.at[1], mdev)
    a_mid = remote(ada_at(ta, mine), ada_at(ta, mine), af_sem.at[0, 0], af_sem.at[1, 0], mdev)
    a_out = remote(ada_at(ta, mine), ada_at(ta, mine), af_sem.at[0, 1], af_sem.at[1, 1], pdev)
    a_pass = remote(ada_at(ta, 1 - mine), ada_at(ta, 1 - mine), af_sem.at[0, 2], af_sem.at[1, 2], pdev)

    @pl.when(outer)
    def _():
        a_pair.start()
        a_pair.wait_send()
        remote(a_h, a_h, af_sem.at[0, 1], af_sem.at[1, 1], pdev).wait_recv()
        remote(a_h, a_h, af_sem.at[0, 2], af_sem.at[1, 2], pdev).wait_recv()

        @pl.loop(0, 12)
        def _(a):
            pair_send(a).wait_send()
            remote(got_h.at[a], got_h.at[a], fsem.at[0, a, 1], fsem.at[1, a, 1], pdev).wait_recv()
            remote(got_h.at[a], got_h.at[a], fsem.at[0, a, 2], fsem.at[1, a, 2], pdev).wait_recv()

    @pl.when(inner)
    def _():
        a_pair.wait_recv()
        a_p[...] = (a_p[...].astype(f32) + a_low[...].astype(f32)).astype(bf16)
        a_half.start()
        a_half.wait()
        ta[pl.ds(mine * ah, ah)] = (a_p[pl.ds(mine * ah, ah)].astype(f32) + a_h[...].astype(f32)).astype(bf16)
        a_mid.start()
        a_out.start()
        a_mid.wait()
        a_pass.start()
        a_out.wait_send()
        a_pass.wait_send()

        @pl.loop(0, 12)
        def _(a):
            half_send(a).wait_send()
            final_mid(a).wait_send()
            final_pair(a).wait_send()
            final_pass(a).wait_send()

    for cp in tiny:
        cp.wait()
    ts[...] = (s_all[0] + s_all[1]) + (s_all[2] + s_all[3])
    tb[...] = (b_all[0] + b_all[1]) + (b_all[2] + b_all[3])


def step_exchange(cores, gq, go, gu, gd, wi, wb, mi, mb, vi, vb, ea, es, eb):
    rows, cols = wi.shape[1:]
    slot = (12, rows, cols)
    dma = pltpu.SemaphoreType.DMA
    return pl.pallas_call(
        functools.partial(step_kernel, cores),
        out_shape=(
            jax.ShapeDtypeStruct(slot, f32),
            jax.ShapeDtypeStruct(slot, bf16),
            jax.ShapeDtypeStruct(ea.shape, bf16),
            jax.ShapeDtypeStruct(es.shape, f32),
            jax.ShapeDtypeStruct(eb.shape, f32),
        ),
        in_specs=[ANY] * 10 + [VMEM] * 3,
        out_specs=(VMEM,) * 5,
        scratch_shapes=[
            pltpu.VMEM((12, 2 * rows, 2 * cols), bf16),
            pltpu.VMEM(slot, f32),
            pltpu.VMEM(slot, f32),
            pltpu.VMEM(slot, f32),
            pltpu.VMEM((12, 2, rows, cols), bf16),
            pltpu.VMEM(slot, bf16),
            pltpu.VMEM(slot, bf16),
            pltpu.VMEM(slot, bf16),
            pltpu.VMEM(slot, bf16),
            pltpu.VMEM((12, rows // 2, cols), bf16),
            pltpu.VMEM(ea.shape, bf16),
            pltpu.VMEM((ea.shape[0] // 2,) + ea.shape[1:], bf16),
            pltpu.VMEM((4,) + es.shape, f32),
            pltpu.VMEM((4,) + eb.shape, f32),
            pltpu.VMEM(ea.shape, bf16),
            pltpu.VMEM(es.shape, f32),
            pltpu.VMEM(eb.shape, f32),
            dma((18,)),
            dma((2, 12, 2)),
            dma((2, 12)),
            dma((2, 12)),
            dma((2, 12)),
            dma((2, 12, 3)),
            dma((2,)),
            dma((2,)),
            dma((2,)),
            dma((2, 3)),
            dma((2, 3)),
            dma((2, 3)),
        ],
        compiler_params=pltpu.CompilerParams(collective_id=5, has_side_effects=True, vmem_limit_bytes=58 * MIB),
        name="step_exchange",
    )(gq, go, gu, gd, wi, wb, mi, mb, vi, vb, ea, es, eb)


def angle_tables(length):
    half = HEAD_DIM // 2
    frequency = np.float32(10000.0) ** (np.float32(-2.0) * np.arange(half, dtype=np.float32) / np.float32(HEAD_DIM))
    angles = frequency[:, None] * np.arange(length, dtype=np.float32)[None, :]
    return jnp.asarray(np.cos(angles)), jnp.asarray(np.sin(angles))


def on_device(
    tokens, sigma_index, absorbed, cotangent, time_table,
    in_weight, back_weight, ada_weight, small_params, up_bias,
    in_first, back_first, ada_first, small_first, bias_first,
    in_second, back_second, ada_second, small_second, bias_second,
    in_moment, back_moment, ada_moment, small_moment, bias_moment,
):
    n_tp, n_dp, n_grp = lax.axis_size("tp"), lax.axis_size("dp"), lax.axis_size("grp")
    seqs, length, width = tokens.shape
    cores = n_tp // seqs
    part = in_weight.shape[2]
    heads_width = seqs * part
    direct = n_dp == 2 and n_grp == 4 and seqs == 2 and cores == 2
    t, d = lax.axis_index("tp"), lax.axis_index("dp")
    s = t // cores
    c = lax.rem(t, cores)
    groups = [[a * cores + b for a in range(seqs)] for b in range(cores)]

    table_ids = jnp.arange(time_table.shape[0], dtype=jnp.int32)
    onehot = (sigma_index[:, None] == table_ids[None, :]).astype(f32)
    condition = jax.nn.silu(jnp.dot(onehot, time_table, precision=highest))
    cond_low = condition.astype(bf16).astype(f32)
    cond_width = cond_low.shape[1]

    wi_t = jnp.transpose(in_weight, (1, 2, 0))
    wa_t = jnp.transpose(ada_weight, (1, 0, 2))
    tok = lax.dynamic_index_in_dim(tokens, s, 0, keepdims=False)
    flags = lax.dynamic_index_in_dim(absorbed, s, 0, keepdims=False)
    gy = lax.dynamic_index_in_dim(cotangent, s, 0, keepdims=False) * flags.astype(bf16)[:, None]
    cond_row = lax.dynamic_index_in_dim(cond_low, s, 0, keepdims=True)

    if direct:
        cond_in = jnp.zeros((2, 8, cond_width // 2), f32)
        cond_in = cond_in.at[:, :seqs].set(jnp.transpose(cond_low.reshape(seqs, 2, cond_width // 2), (1, 0, 2)))
        mod_parts, ps_all, bu_all = exchange_modulation(cores, cond_in, wa_t, small_params, up_bias)
        small_rows = jnp.transpose(ps_all, (1, 0, 2)).reshape(9, width)
        mod_rows = jnp.transpose(mod_parts[:, :6], (1, 0, 2)).reshape(6, width) + small_rows[3:9]
        bias_row = jnp.transpose(bu_all, (2, 0, 1, 3)).reshape(1, 4 * heads_width)
        wq, wo, wu, wd = gather_weights(cores, wi_t.astype(bf16), back_weight.astype(bf16))
    else:
        def over_tp(x, axis):
            return lax.all_gather(x, "tp", axis=axis, tiled=True, axis_index_groups=groups)

        wi_all = over_tp(lax.all_gather(wi_t.astype(bf16), "dp", axis=2, tiled=True), 1)
        wb_all = over_tp(lax.all_gather(back_weight.astype(bf16), "dp", axis=2, tiled=True), 1)
        wq, wo, wu, wd = wi_all[:3], wb_all[0], wi_all[3:], wb_all[1:]
        bu_all = over_tp(lax.all_gather(up_bias.astype(bf16), "dp", axis=1, tiled=True)[None], 0)
        bias_row = jnp.transpose(bu_all, (1, 0, 2)).reshape(1, 4 * heads_width).astype(f32)
        small_rows = lax.all_gather(small_params.astype(bf16), "dp", axis=1, tiled=True).astype(f32)
        wa_all = lax.all_gather(ada_weight.astype(bf16), "dp", axis=0, tiled=True)
        mod_part = jnp.einsum("sc,cad->sad", cond_low.astype(bf16), wa_all, preferred_element_type=f32)
        mod_all = lax.all_gather(mod_part, "tp", axis=2, tiled=True)
        mod_rows = lax.dynamic_index_in_dim(mod_all, s, 0, keepdims=False) + small_rows[3:9]

    vecs = jnp.concatenate([small_rows[0:3], mod_rows, jnp.zeros((7, width), f32)], axis=0)
    cosine, sine = angle_tables(length)
    wu = wu.reshape(4 * heads_width, width)
    wd = wd.reshape(4 * heads_width, width)

    h1, q_t, k_t, v_t, k_r, v_r = project(tok, vecs, wq, cosine, sine)
    probs, inv, o_t = attend(k_r, q_t, v_t)
    attn, x1, h2 = mix(cores, o_t, wo, tok, vecs)
    mlp, dh2, gu, gd, gb = feed(h2, gy, vecs, bias_row, wu, wd)
    out, dx1, ga, stats = middle(cores, mlp, dh2, x1, attn, gy, vecs)
    dh1, gq, go = pull_attention(ga, wo, o_t, inv, probs, q_t, k_t, v_r, cosine, sine, h1, wq)
    gb = gb.reshape(2, width)
    gu = gu.reshape(4, heads_width, width)
    gd = gd.reshape(4, heads_width, width)
    block_out, grad_low, shared = last(cores, 2 if direct else 1, seqs, dh1, dx1, tok, out, vecs, stats, gb, cond_row)
    input_grad = grad_low.astype(f32)

    if not direct:
        shared = lax.all_gather(shared[:, 0], "dp", axis=1)
    by_seq = shared.reshape(seqs, cores, n_dp, 16, width).sum(axis=1)
    dmod = by_seq[:, :, 0:6]
    conds = shared.reshape(seqs, cores, n_dp, 16, width)[:, 0, :, 11, :cond_width]
    small_grad = jnp.concatenate([by_seq[:, :, 6:9].sum(axis=(0, 1)), dmod.sum(axis=(0, 1))], axis=0)
    bias_sum = shared.reshape(seqs, cores, n_dp, 16, width)[:, :, :, 9:11].sum(axis=(0, 2))
    bias_sum = bias_sum.reshape(cores, 4, seqs, part)
    mine = lax.dynamic_index_in_dim(lax.dynamic_index_in_dim(bias_sum, c, 0, keepdims=False), s, 1, keepdims=False)
    bias_grad = lax.dynamic_slice_in_dim(mine, d * (part // n_dp), part // n_dp, 1)
    small_shard = lax.dynamic_slice_in_dim(small_grad, d * (width // n_dp), width // n_dp, 1)
    dmod_cols = lax.dynamic_slice_in_dim(dmod, t * part, part, 3)
    cond_cols = lax.dynamic_slice_in_dim(conds, d * (cond_width // n_dp), cond_width // n_dp, 2)
    ada_grad = jnp.sum(cond_cols[:, :, None, :, None] * dmod_cols[:, :, :, None, :], axis=(0, 1))

    am, av = jnp.transpose(ada_first[0], (1, 0, 2)), jnp.transpose(ada_second[0], (1, 0, 2))
    ada_m, ada_v = adam_parts(ada_grad, am, av)
    ada_d = adam_diff(wa_t, ada_m, ada_v, rate_matrix, decay_rate)
    small_m, small_v = adam_parts(small_shard, small_first[0], small_second[0])
    small_d = adam_diff(small_params, small_m, small_v, rate_small, 0.0)
    bias_m, bias_v = adam_parts(bias_grad, bias_first[0], bias_second[0])
    bias_d = adam_diff(up_bias, bias_m, bias_v, rate_small, 0.0)

    mi, vi = jnp.transpose(in_first[0], (1, 2, 0)), jnp.transpose(in_second[0], (1, 2, 0))
    mb, vb = back_first[0], back_second[0]
    if direct:
        gsum, total, ada_t, small_t, bias_t = step_exchange(
            cores, gq, go, gu, gd, wi_t, back_weight, mi, mb, vi, vb, ada_d, small_d, bias_d)
        gi, gbk = gsum[:7], gsum[7:]
        di, db = total[:7].astype(f32), total[7:].astype(f32)
        ada_t = ada_t.astype(f32)
    else:
        def scatter(x):
            x = lax.psum_scatter(x, "tp", scatter_dimension=1, tiled=True, axis_index_groups=groups)
            return lax.psum_scatter(x, "dp", scatter_dimension=2, tiled=True).astype(f32)

        def over_groups(x):
            return lax.psum(x.astype(bf16), "grp").astype(f32)

        gi = scatter(jnp.concatenate([gq, gu], axis=0))
        gbk = scatter(jnp.concatenate([go[None], gd], axis=0))
        im, iv = adam_parts(gi, mi, vi)
        bm, bv = adam_parts(gbk, mb, vb)
        di = over_groups(adam_diff(wi_t, im, iv, rate_matrix, decay_rate))
        db = over_groups(adam_diff(back_weight, bm, bv, rate_matrix, decay_rate))
        ada_t, small_t, bias_t = over_groups(ada_d), over_groups(small_d), over_groups(bias_d)
    in_m, in_v = adam_parts(gi, mi, vi)
    back_m, back_v = adam_parts(gbk, mb, vb)

    def outer(weight, moment, summed):
        diff = summed / n_grp
        moment_new = outer_mu * moment + diff
        return weight - outer_rate * (diff + outer_mu * moment_new), diff, moment_new

    def back_in(x):
        return jnp.transpose(x, (2, 0, 1))

    def back_ada(x):
        return jnp.transpose(x, (1, 0, 2))

    in_w, in_diff, in_mom = (back_in(x) for x in outer(wi_t, jnp.transpose(in_moment, (1, 2, 0)), di))
    back_w, back_diff, back_mom = outer(back_weight, back_moment, db)
    ada_w, ada_diff, ada_mom = (back_ada(x) for x in outer(wa_t, jnp.transpose(ada_moment, (1, 0, 2)), ada_t))
    small_w, small_diff, small_mom = outer(small_params, small_moment, small_t)
    bias_w, bias_diff, bias_mom = outer(up_bias, bias_moment, bias_t)
    return (
        block_out, input_grad,
        back_in(in_m)[None], back_m[None], back_ada(ada_m)[None], small_m[None], bias_m[None],
        back_in(in_v)[None], back_v[None], back_ada(ada_v)[None], small_v[None], bias_v[None],
        in_w, back_w, ada_w, small_w, bias_w,
        in_diff, back_diff, ada_diff, small_diff, bias_diff,
        in_mom, back_mom, ada_mom, small_mom, bias_mom,
    )


def solution(mesh):
    rows = P(("dp", "grp"), None, None)
    shared = (
        P("dp", None, "tp"), P(None, "tp", "dp"), P("dp", None, "tp"), P(None, "dp"), P(None, ("tp", "dp")),
    )
    grouped = (
        P("grp", "dp", None, "tp"), P("grp", None, "tp", "dp"), P("grp", "dp", None, "tp"),
        P("grp", None, "dp"), P("grp", None, ("tp", "dp")),
    )
    in_specs = (rows, P(("dp", "grp")), P(("dp", "grp"), None), rows, P()) + shared + grouped + grouped + shared
    out_specs = (rows, rows) + grouped + grouped + shared + shared + shared
    return jax.shard_map(on_device, mesh=mesh, in_specs=in_specs, out_specs=out_specs, check_vma=False)
```

```python
import functools
from types import SimpleNamespace

import jax
import jax.numpy as jnp
import numpy as np
from jax import lax
from jax.experimental import pallas as pl
from jax.experimental.pallas import tpu as pltpu
from jax.sharding import PartitionSpec as P

HEAD_DIM = 64
STEP = 10
MESH = pl.DeviceIdType.MESH
ANY = pl.BlockSpec(memory_space=pl.ANY)
VMEM = pl.BlockSpec(memory_space=pltpu.VMEM)
MIB = 2**20

f32 = jnp.float32
bf16 = jnp.bfloat16
highest = lax.Precision.HIGHEST
norm_eps = 1e-05
beta_one = 0.9
beta_two = 0.999
adam_eps = 1e-08
decay_rate = 0.1
rate_matrix = 0.03
rate_small = 0.3
outer_mu = 0.9
outer_rate = 0.7
gelu_a = 0.7978845608028654
gelu_b = 0.044715


def nn(a, b):
    return lax.dot_general(a, b, (((1,), (0,)), ((), ())), preferred_element_type=f32)


def nt(a, b):
    return lax.dot_general(a, b, (((1,), (1,)), ((), ())), preferred_element_type=f32)


def tn(a, b):
    return lax.dot_general(a, b, (((0,), (0,)), ((), ())), preferred_element_type=f32)


def fold(values):
    return jnp.sum(values.reshape(values.shape[0] // 8, 8, values.shape[1]), axis=0)


def normalize(values):
    mean = jnp.mean(values, axis=-1, keepdims=True)
    centered = values - mean
    variance = jnp.mean(centered * centered, axis=-1, keepdims=True)
    inverse = lax.rsqrt(variance + norm_eps)
    return centered * inverse, inverse


def norm_pull(grad_hat, hat, inverse):
    first = jnp.mean(grad_hat, axis=-1, keepdims=True)
    second = jnp.mean(grad_hat * hat, axis=-1, keepdims=True)
    return inverse * (grad_hat - first - hat * second)


def adam_parts(gradient, first, second):
    first_new = beta_one * first + (1.0 - beta_one) * gradient
    second_new = beta_two * second + (1.0 - beta_two) * gradient * gradient
    return first_new, second_new


def adam_diff(weight, first_new, second_new, rate, decay):
    first_hat = first_new / (1.0 - beta_one**STEP)
    second_hat = second_new / (1.0 - beta_two**STEP)
    return rate * (first_hat / (jnp.sqrt(second_hat) + adam_eps) + decay * weight)


def at(start, size, unit=128):
    return pl.ds(pl.multiple_of(start, unit), size)


def remote(source, target, send, recv, device):
    return pltpu.make_async_remote_copy(
        src_ref=source, dst_ref=target, send_sem=send, recv_sem=recv, device_id=device, device_id_type=MESH)


def turn(values, cosine, sine):
    heads = values.shape[0] // HEAD_DIM
    half = HEAD_DIM // 2
    out = []
    for h in range(heads):
        low = values[h * HEAD_DIM : h * HEAD_DIM + half]
        high = values[h * HEAD_DIM + half : (h + 1) * HEAD_DIM]
        out.append(low * cosine - high * sine)
        out.append(high * cosine + low * sine)
    return jnp.concatenate(out, axis=0)


def only_head(pair, h):
    row = lax.broadcasted_iota(jnp.int32, pair.shape, 0)
    return jnp.where(row // HEAD_DIM == h, pair, jnp.zeros_like(pair))


def greet(devices):
    barrier = pltpu.get_barrier_semaphore()
    for device in devices:
        pl.semaphore_signal(barrier, inc=1, device_id=device, device_id_type=MESH)
    pl.semaphore_wait(barrier, len(devices))


def plane_devices(t, d, n_tp, spans):
    others = []
    for dt in range(n_tp):
        for dd in range(spans):
            if dt or dd:
                dev = {"tp": lax.rem(t + dt, n_tp)}
                if spans > 1:
                    dev["dp"] = lax.rem(d + dd, spans)
                others.append(dev)
    return others


def forward_kernel(direct, cores, n_tp, names, *args):
    R = SimpleNamespace(**dict(zip(names, args)))
    t, d = lax.axis_index("tp"), lax.axis_index("dp")
    s = t // cores
    c = lax.rem(t, cores)
    length, width = R.tok.shape
    half = length // cores
    slot_rows = R.weights.shape[1]
    rows, cols = slot_rows // 2, width // 2
    own, other = at(c * half, half), at((1 - c) * half, half)
    sibling = {"tp": s * cores + (1 - c)}
    xdev = {"dp": 1 - d}
    ydev = {"tp": (1 - s) * cores + c}

    tok_load = pltpu.make_async_copy(R.tok_all.at[s], R.tok, R.load_sem.at[0])
    cot_load = pltpu.make_async_copy(R.cot_all.at[s], R.cot, R.load_sem.at[1])

    if direct:
        stages = (R.attn, R.x1, R.away)

        def staged(a):
            return stages[a // 4].at[pl.ds((a % 4 // 2) * rows, rows), pl.ds((a % 2) * cols, cols)]

        weight_loads = []
        for a in range(12):
            source = R.wi.at[a] if a < 3 else R.wb.at[0] if a == 3 else R.wi.at[a - 1] if a < 8 else R.wb.at[a - 7]
            weight_loads.append(pltpu.make_async_copy(source, staged(a), R.stage_sem.at[a]))
            weight_loads[a].start()
    else:
        weight_load = pltpu.make_async_copy(R.weights_in, R.weights, R.stage_sem.at[0])
        weight_load.start()
    tok_load.start()
    cot_load.start()

    def block(a, ss, dd):
        return R.weights.at[a, at(ss * rows, rows, 16), at(dd * cols, cols)]

    def hop(kind, a):
        if kind == 0:
            ref, dev = block(a, s, d), xdev
        elif kind == 1:
            ref, dev = block(a, s, d), ydev
        elif kind == 2:
            ref, dev = block(a, s, 1 - d), ydev
        else:
            ref, dev = block(a, 1 - s, d), xdev
        k = min(kind, 2)
        return remote(ref, ref, R.wsend.at[k, a], R.wrecv.at[k, a], dev)

    def pass_on(m):
        hop(0, 2 * m).wait_recv()
        hop(2, 2 * m).start()
        hop(1, 2 * m + 1).wait_recv()
        hop(3, 2 * m + 1).start()

    def arrived(m):
        hop(1, 2 * m).wait_recv()
        hop(2, 2 * m).wait_recv()
        hop(0, 2 * m + 1).wait_recv()
        hop(3, 2 * m + 1).wait_recv()

    if direct:
        others = plane_devices(t, d, n_tp, 2)
        R.cond[...] = jnp.zeros_like(R.cond)
        for ss in range(2):
            row = R.table[pl.ds(R.sigma[ss], 1), :]
            R.cond[ss : ss + 1, :] = (row / (1.0 + jnp.exp(-row))).astype(bf16).astype(f32)
        turned = pltpu.roll(R.cond[...], R.cond.shape[1] // 2, 1)
        R.cond_near[...] = jnp.where(d == 0, R.cond[...], turned)
        R.cond_far[...] = jnp.where(d == 1, R.cond[...], turned)
        R.ps_low[...] = R.ps[...].astype(bf16).astype(f32)
        R.bu_low[...] = R.bu[...].astype(bf16).astype(f32)
        greet(others)
        cc = remote(R.cond_far, R.cond_got, R.small_sem.at[0, 0], R.small_sem.at[1, 0], xdev)
        cc.start()
        pc = remote(R.ps_low, R.ps_all.at[d], R.small_sem.at[0, 1], R.small_sem.at[1, 1], xdev)
        pc.start()
        bcs = []
        for i, (ds, dd) in enumerate(((0, 1), (1, 0), (1, 1))):
            dev = {"tp": lax.rem(s + ds, 2) * cores + c, "dp": lax.rem(d + dd, 2)}
            bcs.append(remote(R.bu_low, R.bu_all.at[s, d], R.small_sem.at[0, 2 + i], R.small_sem.at[1, 2 + i], dev))
            bcs[i].start()

        def launch(a):
            weight_loads[a].wait()
            R.weights[a, at(s * rows, rows, 16), at(d * cols, cols)] = staged(a)[...].astype(bf16)
            hop(0, a).start()
            hop(1, a).start()

        for a in range(4):
            launch(a)
        R.ps_all[d] = R.ps_low[...]
        R.bu_all[s, d] = R.bu_low[...]
        span = R.wa.shape[1]
        R.parts[...] = jnp.zeros_like(R.parts)

        def partial_mod(source, dd):
            lhs = source[...][:, :span].astype(bf16)
            for a in range(6):
                product = nn(lhs, R.wa[a].astype(bf16))
                for ss in range(2):
                    R.parts[dd, ss, a : a + 1, :] = product[ss : ss + 1]

        partial_mod(R.cond_near, d)
        cc.wait()
        partial_mod(R.cond_got, 1 - d)
        mods = []
        for i, dev in enumerate(others):
            mods.append(remote(
                R.parts.at[dev["dp"], dev["tp"] // cores], R.mod_got.at[t, d], R.mod_sem.at[0, i], R.mod_sem.at[1, i], dev))
            mods[i].start()
        R.mod_got[t, d] = R.parts[d, s]
        R.cond_out[d] = R.cond_near[...]
        R.cond_out[1 - d] = R.cond_got[...]
        for a in range(4, 12):
            launch(a)
        pass_on(0)
        pc.wait()
        for bc in bcs:
            bc.wait()
        for mc in mods:
            mc.wait()
        small_rows = jnp.concatenate([R.ps_all[0], R.ps_all[1]], axis=1)
        mod_rows = jnp.concatenate([R.mod_got[tt, 0] + R.mod_got[tt, 1] for tt in range(n_tp)], axis=1)
        R.vecs[...] = jnp.zeros_like(R.vecs)
        R.vecs[0:3] = small_rows[0:3]
        R.vecs[3:9] = mod_rows[0:6] + small_rows[3:9]
        R.bias[...] = jnp.concatenate(
            [R.bu_all[ss, dd, j : j + 1, :] for j in range(4) for ss in range(2) for dd in range(2)], axis=1)
        pass_on(1)
    else:
        greet([sibling])
        R.vecs[...] = R.vecs_in[...]
        R.bias[...] = R.bias_in[...]
        R.cond_out[...] = jnp.zeros_like(R.cond_out)

    tok_load.wait()
    step = 256

    @pl.loop(0, length // step)
    def _(i):
        r = at(i * step, step)
        hat, _ = normalize(R.tok[r].astype(f32))
        hidden = hat * (R.vecs[0:1] * (1.0 + R.vecs[4:5])) + R.vecs[3:4]
        R.h1[r] = hidden.astype(bf16)

    outs = []

    def emit(source, target):
        cp = pltpu.make_async_copy(source, target, R.out_sem.at[len(outs)])
        cp.start()
        outs.append(cp)

    emit(R.h1, R.h1_out)

    if direct:
        arrived(0)
        arrived(1)
        pass_on(2)
    else:
        weight_load.wait()
    emit(R.weights.at[pl.ds(0, 4)], R.wq_out)

    @pl.loop(0, length // step)
    def _(i):
        r = at(i * step, step)
        low = R.h1[r]
        cos, sin = R.cosine[:, r], R.sine[:, r]
        R.q_t[:, r] = (turn(nt(R.weights[0], low), cos, sin) * 0.125).astype(bf16)
        keys = turn(nt(R.weights[1], low), cos, sin).astype(bf16)
        R.k_t[:, r] = keys
        R.k_r[r] = keys.T
        values = nt(R.weights[2], low).astype(bf16)
        R.v_t[:, r] = values
        R.v_r[r] = values.T

    emit(R.q_t, R.q_out)
    emit(R.k_t, R.k_out)
    emit(R.v_r, R.v_out)

    heads = R.probs.shape[0]

    @pl.loop(0, heads)
    def _(h):
        pair = at(h // 2 * 2 * HEAD_DIM, 2 * HEAD_DIM)
        one = at(h * HEAD_DIM, HEAD_DIM, HEAD_DIM)
        scores = nn(R.k_r[:, pair], only_head(R.q_t[pair, :], lax.rem(h, 2)))
        top = jnp.max(scores, axis=0, keepdims=True)
        shifted = jnp.exp(scores - top)
        inverse = 1.0 / jnp.sum(shifted, axis=0, keepdims=True)
        low = shifted.astype(bf16)
        R.probs[h] = low
        R.inv_out[h] = inverse
        R.o_t[one, :] = (nn(R.v_t[one, :], low) * inverse).astype(bf16)
        if direct:
            @pl.when(jnp.logical_and(h >= 1, h < 4))
            def _():
                pass_on(h + 2)

    for h in range(heads):
        emit(R.probs.at[h], R.probs_out.at[h])
    emit(R.o_t, R.o_out)

    away = remote(R.away, R.got, R.pair_sem.at[0, 0], R.pair_sem.at[1, 0], sibling)
    R.away[...] = tn(R.o_t[:, other], R.weights[3])
    away.start()
    R.attn[...] = tn(R.o_t[:, own], R.weights[3])
    away.wait()
    small = 128

    @pl.loop(0, half // small)
    def _(i):
        r = at(i * small, small)
        total = R.attn[r] + R.got[r]
        R.attn[r] = total
        after = R.tok[at(c * half + i * small, small)].astype(f32) + R.vecs[5:6] * total
        R.x1[r] = after
        hat, _ = normalize(after)
        hidden = hat * (R.vecs[1:2] * (1.0 + R.vecs[7:8])) + R.vecs[6:7]
        R.h2[at(c * half + i * small, small)] = hidden.astype(bf16)

    share = remote(R.h2.at[own], R.h2.at[own], R.pair_sem.at[0, 1], R.pair_sem.at[1, 1], sibling)
    share.start()
    for cp in outs:
        cp.wait()
    flags = jnp.broadcast_to(R.flags[pl.ds(s, 1), :].astype(f32), (128, length)).T
    R.column[...] = flags
    cot_load.wait()

    chunks = 2
    if direct:
        arrived(2)
        arrived(3)

    def weight(first, j):
        return R.weights[first + 2 * j : first + 2 * j + 2].reshape(2 * slot_rows, width)

    def up(r):
        low = R.h2[r]
        for j in range(chunks):
            u = nt(low, weight(4, j)) + R.bias[:, j * width : (j + 1) * width]
            square = u * u
            inner = jnp.tanh(gelu_a * (u + gelu_b * square * u))
            z = 0.5 * u * (1.0 + inner)
            slope = 0.5 * (1.0 + inner) + 0.5 * u * (1.0 - inner * inner) * gelu_a * (1.0 + 3.0 * gelu_b * square)
            R.probs[j, r, 0:width] = z.astype(bf16)
            R.probs[2 + j, r, 0:width] = slope.astype(bf16)

    @pl.loop(0, half // step)
    def _(i):
        up(at(c * half + i * step, step))

    share.wait()

    @pl.loop(0, half // step)
    def _(i):
        up(at((1 - c) * half + i * step, step))

    if direct:
        arrived(4)
        arrived(5)
    R.bias_sum[...] = jnp.zeros_like(R.bias_sum)

    def down(r):
        grad = R.cot[r].astype(f32) * jnp.concatenate([R.column[r]] * (width // 128), axis=1)
        R.cot[r] = grad.astype(bf16)
        gm = (R.vecs[8:9] * grad).astype(bf16)
        R.probs[4, r, 0:width] = gm
        forward = jnp.zeros((step, width), f32)
        backward = jnp.zeros((step, width), f32)
        for j in range(chunks):
            du = (nt(gm, weight(8, j)) * R.probs[2 + j, r, 0:width].astype(f32)).astype(bf16)
            R.probs[2 + j, r, 0:width] = du
            R.bias_sum[:, j * width : (j + 1) * width] += fold(du.astype(f32))
            forward += nn(R.probs[j, r, 0:width], weight(8, j))
            backward += nn(du, weight(4, j))
        R.probs[5, r, 0:width] = forward.astype(bf16)
        R.dh2[r] = backward.astype(bf16)

    @pl.loop(0, half // step)
    def _(i):
        down(at((1 - c) * half + i * step, step))

    trades = [
        remote(R.probs.at[5, other, pl.ds(0, width)], R.trade.at[0], R.pair_sem.at[0, 2], R.pair_sem.at[1, 2], sibling),
        remote(R.dh2.at[other], R.trade.at[1], R.pair_sem.at[0, 3], R.pair_sem.at[1, 3], sibling),
    ]
    for cp in trades:
        cp.start()

    @pl.loop(0, half // step)
    def _(i):
        down(at(c * half + i * step, step))

    R.acc[...] = jnp.zeros_like(R.acc)
    for cp in trades:
        cp.wait()

    @pl.loop(0, half // small)
    def _(i):
        r = at(i * small, small)
        g = at(c * half + i * small, small)
        after = R.x1[r]
        branch = R.probs[5, g, 0:width].astype(f32) + R.trade[0, r].astype(f32) + R.vecs[2:3]
        R.out[r] = (after + R.vecs[8:9] * branch).astype(bf16)
        grad = R.cot[g].astype(f32)
        dh = R.dh2[g].astype(f32) + R.trade[1, r].astype(f32)
        hat, inverse = normalize(after)
        total = grad + norm_pull(dh * (R.vecs[1:2] * (1.0 + R.vecs[7:8])), hat, inverse)
        R.x1[r] = total
        R.ga[g] = (R.vecs[5:6] * total).astype(bf16)
        R.acc[0] += fold(dh)
        R.acc[1] += fold(dh * hat)
        R.acc[2] += fold(total * R.attn[r])
        R.acc[3] += fold(grad * branch)
        R.acc[4] += fold(R.probs[4, g, 0:width].astype(f32))

    give = remote(R.ga.at[own], R.ga.at[own], R.pair_sem.at[0, 4], R.pair_sem.at[1, 4], sibling)
    give.start()
    outs.clear()
    emit(R.x1, R.dx1_out)
    emit(R.out, R.block_half)
    emit(R.vecs, R.vecs_out)
    R.stats[...] = jnp.zeros_like(R.stats)
    for i in range(5):
        R.stats[i : i + 1] = jnp.sum(R.acc[i], axis=0, keepdims=True)
    R.gb[...] = jnp.sum(R.bias_sum[...], axis=0, keepdims=True)

    for k in range(4):
        where = pl.ds((k % 2) * slot_rows, slot_rows)
        R.gd[k] = tn(R.probs[k // 2, :, where], R.probs[4, :, 0:width]).astype(bf16)
        emit(R.gd.at[k], R.gd_out.at[k])
    for k in range(4):
        where = pl.ds((k % 2) * slot_rows, slot_rows)
        R.gu[k] = tn(R.probs[2 + k // 2, :, where], R.h2[...]).astype(bf16)
        emit(R.gu.at[k], R.gu_out.at[k])
    give.wait()
    emit(R.ga, R.ga_out)
    if direct:
        for a in range(12):
            hop(0, a).wait_send()
            hop(1, a).wait_send()
            hop(2 + a % 2, a).wait_send()
    for cp in outs:
        cp.wait()


def forward(direct, cores, length, width, slot_rows, first, tokens, flags, cotangent, cosine, sine):
    n_tp = lax.axis_size("tp")
    half = length // cores
    heads = slot_rows // HEAD_DIM
    dma = pltpu.SemaphoreType.DMA
    smem = pl.BlockSpec(memory_space=pltpu.SMEM)
    arr = jax.ShapeDtypeStruct
    vm = pltpu.VMEM
    if direct:
        lead = [("sigma", smem), ("table", VMEM), ("wa", VMEM), ("ps", VMEM), ("bu", VMEM), ("wi", ANY), ("wb", ANY)]
        cond_shape = (2, 8, 128)
    else:
        lead = [("weights_in", ANY), ("vecs_in", VMEM), ("bias_in", VMEM)]
        cond_shape = (2, 8, 128)
    ins = lead + [("tok_all", ANY), ("flags", VMEM), ("cot_all", ANY), ("cosine", VMEM), ("sine", VMEM)]
    outs = [
        ("h1_out", arr((length, width), bf16), ANY),
        ("wq_out", arr((4, slot_rows, width), bf16), ANY),
        ("q_out", arr((slot_rows, length), bf16), ANY),
        ("k_out", arr((slot_rows, length), bf16), ANY),
        ("v_out", arr((length, slot_rows), bf16), ANY),
        ("probs_out", arr((heads, length, length), bf16), ANY),
        ("inv_out", arr((heads, 1, length), f32), VMEM),
        ("o_out", arr((slot_rows, length), bf16), ANY),
        ("dx1_out", arr((half, width), f32), ANY),
        ("block_half", arr((half, width), bf16), ANY),
        ("vecs_out", arr((16, width), f32), ANY),
        ("stats", arr((8, width), f32), VMEM),
        ("gb", arr((1, 4 * slot_rows), f32), VMEM),
        ("gd_out", arr((4, slot_rows, width), bf16), ANY),
        ("gu_out", arr((4, slot_rows, width), bf16), ANY),
        ("ga_out", arr((length, width), bf16), ANY),
        ("cond_out", arr(cond_shape, f32), VMEM),
    ]
    scratch = [
        ("tok", vm((length, width), bf16)),
        ("cot", vm((length, width), bf16)),
        ("weights", vm((12, slot_rows, width), bf16)),
        ("h1", vm((length, width), bf16)),
        ("q_t", vm((slot_rows, length), bf16)),
        ("k_t", vm((slot_rows, length), bf16)),
        ("v_t", vm((slot_rows, length), bf16)),
        ("k_r", vm((length, slot_rows), bf16)),
        ("v_r", vm((length, slot_rows), bf16)),
        ("probs", vm((heads, length, length), bf16)),
        ("o_t", vm((slot_rows, length), bf16)),
        ("away", vm((half, width), f32)),
        ("got", vm((half, width), f32)),
        ("attn", vm((half, width), f32)),
        ("x1", vm((half, width), f32)),
        ("h2", vm((length, width), bf16)),
        ("column", vm((length, 128), f32)),
        ("bias_sum", vm((8, 4 * slot_rows), f32)),
        ("bias", vm((1, 4 * slot_rows), f32)),
        ("vecs", vm((16, width), f32)),
        ("dh2", vm((length, width), bf16)),
        ("trade", vm((2, half, width), bf16)),
        ("out", vm((half, width), bf16)),
        ("ga", vm((length, width), bf16)),
        ("acc", vm((5, 8, width), f32)),
        ("gd", vm((4, slot_rows, width), bf16)),
        ("gu", vm((4, slot_rows, width), bf16)),
        ("load_sem", dma((2,))),
        ("stage_sem", dma((12,))),
        ("out_sem", dma((16,))),
        ("pair_sem", dma((2, 5))),
    ]
    if direct:
        wa, ps, bu = first[2:5]
        scratch += [
            ("cond", vm((8, 128), f32)),
            ("cond_near", vm((8, 128), f32)),
            ("cond_far", vm((8, 128), f32)),
            ("cond_got", vm((8, 128), f32)),
            ("ps_low", vm(ps.shape, f32)),
            ("bu_low", vm(bu.shape, f32)),
            ("ps_all", vm((2,) + ps.shape, f32)),
            ("bu_all", vm((2, 2) + bu.shape, f32)),
            ("parts", vm((2, 2, 8, wa.shape[2]), f32)),
            ("mod_got", vm((n_tp, 2, 8, wa.shape[2]), f32)),
            ("wsend", dma((3, 12))),
            ("wrecv", dma((3, 12))),
            ("small_sem", dma((2, 5))),
            ("mod_sem", dma((2, 2 * n_tp - 1))),
        ]
    names = [n for n, _ in ins] + [o[0] for o in outs] + [n for n, _ in scratch]
    results = pl.pallas_call(
        functools.partial(forward_kernel, direct, cores, n_tp, names),
        out_shape=tuple(o[1] for o in outs),
        in_specs=[spec for _, spec in ins],
        out_specs=tuple(o[2] for o in outs),
        scratch_shapes=[shape for _, shape in scratch],
        compiler_params=pltpu.CompilerParams(collective_id=0, has_side_effects=True, vmem_limit_bytes=60 * MIB),
        name="forward",
    )(*first, tokens, flags, cotangent, cosine, sine)
    return SimpleNamespace(**dict(zip([o[0] for o in outs], results)))


def pull_kernel(ga, wo, o_t, inv, probs, q_t, k_t, v_t, v_r, cosine, sine, h1, wq, dh1, gq, go, do_s, ds_s, dqkv):
    p = pl.program_id(0)
    length, width = ga.shape
    pw = 2 * HEAD_DIM
    heads_width = wq.shape[1]
    step = 256
    do_t = nt(wo[...], ga[...])
    go[...] = nn(o_t[...], ga[...]).astype(bf16)
    for h in range(2):
        rows = slice(h * HEAD_DIM, (h + 1) * HEAD_DIM)
        do_s[rows] = (do_t[rows] * inv[0, h : h + 1, :]).astype(bf16)
    raw = []
    for h in range(2):
        rows = slice(h * HEAD_DIM, (h + 1) * HEAD_DIM)
        delta = jnp.sum(do_s[rows].astype(f32) * o_t[rows].astype(f32), axis=0, keepdims=True)
        dq = []
        for i in range(length // step):
            cols = slice(i * step, (i + 1) * step)
            dp = nn(v_r[...], only_head(do_s[:, cols], h))
            ds = (probs[h, :, cols].astype(f32) * (dp - delta[:, cols])).astype(bf16)
            ds_s[:, cols] = ds
            dq.append(nn(k_t[rows], ds))
        dk = nt(q_t[rows], ds_s[...])
        dv = nt(do_s[rows], probs[h])
        raw.append((jnp.concatenate(dq, axis=1) * 0.125, dk, dv))
    cos, sin = cosine[...], sine[...]
    for k in range(3):
        both = jnp.concatenate([raw[0][k], raw[1][k]], axis=0)
        if k < 2:
            both = turn(both, cos, -sin)
        at = pl.multiple_of(k * heads_width + p * pw, pw)
        dqkv[pl.ds(at, pw)] = both.astype(bf16)

    @pl.when(p == pl.num_programs(0) - 1)
    def _():
        for k in range(3):
            part = slice(k * heads_width, (k + 1) * heads_width)
            gq[k] = nn(dqkv[part], h1[...]).astype(bf16)

        @pl.loop(0, length // step)
        def _(i):
            r = pl.ds(pl.multiple_of(i * step, step), step)
            total = jnp.zeros((step, width), f32)
            for k in range(3):
                part = slice(k * heads_width, (k + 1) * heads_width)
                total += tn(dqkv[part, r], wq[k])
            dh1[r] = total.astype(bf16)


def pull_attention(ga, wo, o_t, inv, probs, q_t, k_t, v_r, cosine, sine, h1, wq):
    length, width = ga.shape
    heads_width = wq.shape[1]
    pw = 2 * HEAD_DIM
    pairs = heads_width // pw
    half = HEAD_DIM // 2

    def body(ga, wo, o_t, inv, probs, q_t, k_t, v_r, cosine, sine, h1, wq, *rest):
        return pull_kernel(ga, wo, o_t, inv, probs, q_t, k_t, None, v_r, cosine, sine, h1, wq, *rest)

    return pl.pallas_call(
        body,
        grid=(pairs,),
        out_shape=(
            jax.ShapeDtypeStruct((length, width), bf16),
            jax.ShapeDtypeStruct((3, heads_width, width), bf16),
            jax.ShapeDtypeStruct((heads_width, width), bf16),
        ),
        in_specs=[
            pl.BlockSpec((length, width), lambda p: (0, 0)),
            pl.BlockSpec((pw, width), lambda p: (p, 0)),
            pl.BlockSpec((pw, length), lambda p: (p, 0)),
            pl.BlockSpec((1, 2, length), lambda p: (p, 0, 0)),
            pl.BlockSpec((2, length, length), lambda p: (p, 0, 0)),
            pl.BlockSpec((pw, length), lambda p: (p, 0)),
            pl.BlockSpec((pw, length), lambda p: (p, 0)),
            pl.BlockSpec((length, pw), lambda p: (0, p)),
            pl.BlockSpec((half, length), lambda p: (0, 0)),
            pl.BlockSpec((half, length), lambda p: (0, 0)),
            pl.BlockSpec((length, width), lambda p: (0, 0)),
            pl.BlockSpec((3, heads_width, width), lambda p: (0, 0, 0)),
        ],
        out_specs=(
            pl.BlockSpec((length, width), lambda p: (0, 0)),
            pl.BlockSpec((3, heads_width, width), lambda p: (0, 0, 0)),
            pl.BlockSpec((pw, width), lambda p: (p, 0)),
        ),
        scratch_shapes=[
            pltpu.VMEM((pw, length), bf16),
            pltpu.VMEM((length, length), bf16),
            pltpu.VMEM((3 * heads_width, length), bf16),
        ],
        compiler_params=pltpu.CompilerParams(vmem_limit_bytes=56 * MIB),
        name="attention_pull",
    )(ga, wo, o_t, inv, probs, q_t, k_t, v_r, cosine, sine, h1, wq)


def sibling_of(cores):
    t = lax.axis_index("tp")
    s = t // cores
    c = lax.rem(t, cores)
    return s, c, {"tp": s * cores + (1 - c)}


def last_kernel(cores, spans, dh1, dx1, tok, out, vecs, stats, gb, block_out, grad_out, shared,
                got, tbuf, grad, acc, small, dsem, tsem, osem, fsem, lsem, vsem):
    t, d = lax.axis_index("tp"), lax.rem(lax.axis_index("dp"), spans)
    n_tp = shared.shape[0]
    s, c, sibling = sibling_of(cores)
    across = {"tp": (1 - s) * cores + c}
    half = dx1.shape[0]
    own = pl.ds(pl.multiple_of(c * half, 128), half)
    other = pl.ds(pl.multiple_of((1 - c) * half, 128), half)
    barrier = pltpu.get_barrier_semaphore()
    others = []
    for dt in range(n_tp):
        for dd in range(spans):
            if dt or dd:
                dev = {"tp": lax.rem(t + dt, n_tp)}
                if spans > 1:
                    dev["dp"] = lax.rem(d + dd, spans)
                others.append(dev)
    for dev in others:
        pl.semaphore_signal(barrier, inc=1, device_id=dev, device_id_type=MESH)
    tc = pltpu.make_async_copy(tok.at[own], tbuf, tsem)
    tc.start()
    pl.semaphore_wait(barrier, len(others))

    def spread(kind, source, target):
        copies = []
        for i, dev in enumerate((sibling, across)):
            copies.append(pltpu.make_async_remote_copy(
                src_ref=source, dst_ref=target.at[s, own], send_sem=osem.at[0, kind, i], recv_sem=osem.at[1, kind, i],
                device_id=dev, device_id_type=MESH))
            copies[i].start()
        local = pltpu.make_async_copy(source, target.at[s, own], lsem.at[kind])
        local.start()
        return copies, local

    def pass_on(kind, copies, target):
        copies[1].wait_recv()
        forward = pltpu.make_async_remote_copy(
            src_ref=target.at[1 - s, own], dst_ref=target.at[1 - s, own], send_sem=fsem.at[0, kind],
            recv_sem=fsem.at[1, kind], device_id=sibling, device_id_type=MESH)
        forward.start()
        return forward

    first = pltpu.make_async_remote_copy(
        src_ref=dh1.at[other], dst_ref=got, send_sem=dsem.at[0], recv_sem=dsem.at[1],
        device_id=sibling, device_id_type=MESH)
    first.start()
    ocopies, olocal = spread(0, out, block_out)
    acc[...] = jnp.zeros_like(acc)
    tc.wait()
    first.wait()
    step = 128

    @pl.loop(0, half // step)
    def _(i):
        r = pl.ds(pl.multiple_of(i * step, step), step)
        g = pl.ds(pl.multiple_of(c * half + i * step, step), step)
        dh = dh1[g].astype(f32) + got[r].astype(f32)
        hat, inverse = normalize(tbuf[r].astype(f32))
        acc[0] += fold(dh)
        acc[1] += fold(dh * hat)
        total = dx1[r] + norm_pull(dh * (vecs[0:1] * (1.0 + vecs[4:5])), hat, inverse)
        grad[r] = total.astype(bf16)

    gcopies, glocal = spread(1, grad, grad_out)
    shift1 = jnp.sum(acc[0], axis=0, keepdims=True)
    turn1 = jnp.sum(acc[1], axis=0, keepdims=True)
    small[...] = jnp.zeros_like(small)
    small[0:1] = shift1
    small[1:2] = turn1 * vecs[0:1]
    small[2:3] = stats[2:3]
    small[3:4] = stats[0:1]
    small[4:5] = stats[1:2] * vecs[1:2]
    small[5:6] = stats[3:4]
    small[6:7] = turn1 * (1.0 + vecs[4:5])
    small[7:8] = stats[1:2] * (1.0 + vecs[7:8])
    small[8:9] = stats[4:5]
    small[9:11] = gb[...]
    shared[t, d] = small[...]
    vsends = []
    for i, dev in enumerate(others):
        cp = pltpu.make_async_remote_copy(
            src_ref=small, dst_ref=shared.at[t, d], send_sem=vsem.at[0, i], recv_sem=vsem.at[1, i],
            device_id=dev, device_id_type=MESH)
        cp.start()
        vsends.append(cp)
    forwards = [pass_on(0, ocopies, block_out), pass_on(1, gcopies, grad_out)]
    for copies, local, forward in zip((ocopies, gcopies), (olocal, glocal), forwards):
        copies[0].wait()
        copies[1].wait_send()
        local.wait()
        forward.wait()
    for cp in vsends:
        cp.wait()


def last(cores, spans, seqs, dh1, dx1, tok, out, vecs, stats, gb):
    length, width = tok.shape
    n_tp = lax.axis_size("tp")
    half = length // cores
    return pl.pallas_call(
        functools.partial(last_kernel, cores, spans),
        out_shape=(
            jax.ShapeDtypeStruct((seqs, length, width), bf16),
            jax.ShapeDtypeStruct((seqs, length, width), bf16),
            jax.ShapeDtypeStruct((n_tp, spans, 16, width), f32),
        ),
        in_specs=[VMEM, VMEM, ANY, ANY, VMEM, VMEM, VMEM],
        out_specs=(ANY, ANY, VMEM),
        scratch_shapes=[
            pltpu.VMEM((half, width), bf16),
            pltpu.VMEM((half, width), bf16),
            pltpu.VMEM((half, width), bf16),
            pltpu.VMEM((2, 8, width), f32),
            pltpu.VMEM((16, width), f32),
            pltpu.SemaphoreType.DMA((2,)),
            pltpu.SemaphoreType.DMA,
            pltpu.SemaphoreType.DMA((2, 2, 2)),
            pltpu.SemaphoreType.DMA((2, 2)),
            pltpu.SemaphoreType.DMA((2,)),
            pltpu.SemaphoreType.DMA((2, spans * n_tp - 1)),
        ],
        compiler_params=pltpu.CompilerParams(collective_id=4, has_side_effects=True, vmem_limit_bytes=48 * MIB),
        name="last_norm",
    )(dh1, dx1, tok, out, vecs, stats, gb)


def step_kernel(cores, gq, go, gu, gd, wi, wb, mi, mb, vi, vb, ea, es, eb,
                gsum, total, ta, ts, tb,
                grads, wts, firsts, seconds, got_a, send_b, got_b, diff, got_p, got_h, a_p, a_h, s_all, b_all, a_low, s_low, b_low,
                lsem, asem, bsem, psem, hsem, fsem, esem, ap_sem, ah_sem, af_sem, ss_sem, bs_sem):
    t, d, g = lax.axis_index("tp"), lax.axis_index("dp"), lax.axis_index("grp")
    s = t // cores
    c = lax.rem(t, cores)
    rows, cols = wi.shape[1:]
    xdev = {"dp": 1 - d}
    ydev = {"tp": (1 - s) * cores + c}
    inner = jnp.logical_or(g == 1, g == 2)
    outer = jnp.logical_not(inner)
    low_side = g < 2
    pair = jnp.where(g == 0, 1, jnp.where(g == 1, 0, jnp.where(g == 2, 3, 2)))
    pdev = {"grp": pair}
    mdev = {"grp": 3 - g}
    mine = jnp.where(g == 1, 0, 1)
    hrows = rows // 2

    def remote(source, target, send, recv, device):
        return pltpu.make_async_remote_copy(
            src_ref=source, dst_ref=target, send_sem=send, recv_sem=recv, device_id=device, device_id_type=MESH)

    def r_at(ss):
        return pl.ds(pl.multiple_of(ss * rows, 16), rows)

    def c_at(dd):
        return pl.ds(pl.multiple_of(dd * cols, 128), cols)

    loads = []
    for a in range(12):
        ref = gq.at[a] if a < 3 else gu.at[a - 3] if a < 7 else go if a == 7 else gd.at[a - 8]
        loads.append(pltpu.make_async_copy(ref, grads.at[a], lsem.at[a]))
    for i, (src, dst) in enumerate(((wi, wts), (mi, firsts), (vi, seconds))):
        loads.append(pltpu.make_async_copy(src, dst.at[pl.ds(0, 7)], lsem.at[12 + i]))
    for i, (src, dst) in enumerate(((wb, wts), (mb, firsts), (vb, seconds))):
        loads.append(pltpu.make_async_copy(src, dst.at[pl.ds(7, 5)], lsem.at[15 + i]))
    for cp in loads:
        cp.start()

    barrier = pltpu.get_barrier_semaphore()
    for dev in (xdev, ydev, {"grp": lax.rem(g + 1, 4)}, {"grp": lax.rem(g + 2, 4)}, {"grp": lax.rem(g + 3, 4)}):
        pl.semaphore_signal(barrier, inc=1, device_id=dev, device_id_type=MESH)
    pl.semaphore_wait(barrier, 5)

    a_low[...] = ea[...].astype(bf16)
    s_low[...] = es[...].astype(bf16).astype(f32)
    b_low[...] = eb[...].astype(bf16).astype(f32)
    tiny = []
    for i in range(3):
        dev = {"grp": lax.rem(g + 1 + i, 4)}
        tiny.append(remote(s_low, s_all.at[g], ss_sem.at[0, i], ss_sem.at[1, i], dev))
        tiny.append(remote(b_low, b_all.at[g], bs_sem.at[0, i], bs_sem.at[1, i], dev))
    for cp in tiny:
        cp.start()
    s_all[g] = s_low[...]
    b_all[g] = b_low[...]

    def first_send(a, k):
        if a % 2 == 0:
            return remote(grads.at[a, r_at(1 - s), pl.ds(k * cols, cols)], got_a.at[a, k], asem.at[0, a, k], asem.at[1, a, k], ydev)
        return remote(grads.at[a, pl.ds(k * rows, rows), c_at(1 - d)], got_a.at[a, k], asem.at[0, a, k], asem.at[1, a, k], xdev)

    def first_wait(a):
        for k in range(2):
            remote(got_a.at[a, k], got_a.at[a, k], asem.at[0, a, k], asem.at[1, a, k], xdev).wait()

    for a in range(12):
        loads[a].wait()
        for k in range(2):
            first_send(a, k).start()
    for cp in loads[12:]:
        cp.wait()

    def second_send(a, parity):
        dev = xdev if parity == 0 else ydev
        return remote(send_b.at[a], got_b.at[a], bsem.at[0, a], bsem.at[1, a], dev)

    def pair_send(a):
        return remote(diff.at[a], got_p.at[a], psem.at[0, a], psem.at[1, a], pdev)

    def h_at(k):
        return pl.ds(pl.multiple_of(k * hrows, 16), hrows)

    def half_send(a):
        return remote(got_p.at[a, h_at(1 - mine)], got_h.at[a], hsem.at[0, a], hsem.at[1, a], mdev)

    def final_mid(a):
        return remote(total.at[a, h_at(mine)], total.at[a, h_at(mine)], fsem.at[0, a, 0], fsem.at[1, a, 0], mdev)

    def final_pair(a):
        return remote(total.at[a, h_at(mine)], total.at[a, h_at(mine)], fsem.at[0, a, 1], fsem.at[1, a, 1], pdev)

    def final_pass(a):
        return remote(total.at[a, h_at(1 - mine)], total.at[a, h_at(1 - mine)], fsem.at[0, a, 2], fsem.at[1, a, 2], pdev)

    def stage_b(a, parity):
        first_wait(a)
        if parity == 0:
            send_b[a] = (grads[a, r_at(s), c_at(1 - d)].astype(f32) + got_a[a, 1 - d].astype(f32)).astype(bf16)
        else:
            send_b[a] = (grads[a, r_at(1 - s), c_at(d)].astype(f32) + got_a[a, 1 - s].astype(f32)).astype(bf16)
        second_send(a, parity).start()

    def stage_c(a, parity):
        second_send(a, parity).wait()
        keep = got_a[a, d] if parity == 0 else got_a[a, s]
        gradient = grads[a, r_at(s), c_at(d)].astype(f32) + keep.astype(f32) + got_b[a].astype(f32)
        gsum[a] = gradient
        first_new, second_new = adam_parts(gradient, firsts[a], seconds[a])
        diff[a] = adam_diff(wts[a], first_new, second_new, rate_matrix, decay_rate).astype(bf16)

        @pl.when(outer)
        def _():
            pair_send(a).start()

    def stage_d(a):
        pair_send(a).wait_recv()
        got_p[a] = (diff[a].astype(f32) + got_p[a].astype(f32)).astype(bf16)
        half_send(a).start()

    def stage_e(a):
        half_send(a).wait_recv()
        total[a, h_at(mine)] = (got_p[a, h_at(mine)].astype(f32) + got_h[a].astype(f32)).astype(bf16)
        final_mid(a).start()
        final_pair(a).start()

    def stage_f(a):
        remote(got_h.at[a], got_h.at[a], fsem.at[0, a, 0], fsem.at[1, a, 0], mdev).wait_recv()
        final_pass(a).start()

    n = 6

    @pl.loop(0, n + 4)
    def _(i):
        @pl.when(i < n)
        def _():
            for k in range(2):
                stage_b(2 * i + k, k)

        @pl.when(jnp.logical_and(i >= 1, i < n + 1))
        def _():
            for k in range(2):
                stage_c(2 * (i - 1) + k, k)

        @pl.when(jnp.logical_and(inner, jnp.logical_and(i >= 2, i < n + 2)))
        def _():
            for k in range(2):
                stage_d(2 * (i - 2) + k)

        @pl.when(jnp.logical_and(inner, jnp.logical_and(i >= 3, i < n + 3)))
        def _():
            for k in range(2):
                stage_e(2 * (i - 3) + k)

        @pl.when(jnp.logical_and(inner, i >= 4))
        def _():
            for k in range(2):
                stage_f(2 * (i - 4) + k)

    ah = a_low.shape[0] // 2

    def ada_at(ref, k):
        return ref.at[pl.ds(k * ah, ah)]

    a_pair = remote(a_low, a_p, ap_sem.at[0], ap_sem.at[1], pdev)
    a_half = remote(ada_at(a_p, 1 - mine), a_h, ah_sem.at[0], ah_sem.at[1], mdev)
    a_mid = remote(ada_at(ta, mine), ada_at(ta, mine), af_sem.at[0, 0], af_sem.at[1, 0], mdev)
    a_out = remote(ada_at(ta, mine), ada_at(ta, mine), af_sem.at[0, 1], af_sem.at[1, 1], pdev)
    a_pass = remote(ada_at(ta, 1 - mine), ada_at(ta, 1 - mine), af_sem.at[0, 2], af_sem.at[1, 2], pdev)

    @pl.when(outer)
    def _():
        a_pair.start()
        a_pair.wait_send()
        remote(a_h, a_h, af_sem.at[0, 1], af_sem.at[1, 1], pdev).wait_recv()
        remote(a_h, a_h, af_sem.at[0, 2], af_sem.at[1, 2], pdev).wait_recv()

        @pl.loop(0, 12)
        def _(a):
            pair_send(a).wait_send()
            remote(got_h.at[a], got_h.at[a], fsem.at[0, a, 1], fsem.at[1, a, 1], pdev).wait_recv()
            remote(got_h.at[a], got_h.at[a], fsem.at[0, a, 2], fsem.at[1, a, 2], pdev).wait_recv()

    @pl.when(inner)
    def _():
        a_pair.wait_recv()
        a_p[...] = (a_p[...].astype(f32) + a_low[...].astype(f32)).astype(bf16)
        a_half.start()
        a_half.wait()
        ta[pl.ds(mine * ah, ah)] = (a_p[pl.ds(mine * ah, ah)].astype(f32) + a_h[...].astype(f32)).astype(bf16)
        a_mid.start()
        a_out.start()
        a_mid.wait()
        a_pass.start()
        a_out.wait_send()
        a_pass.wait_send()

        @pl.loop(0, 12)
        def _(a):
            half_send(a).wait_send()
            final_mid(a).wait_send()
            final_pair(a).wait_send()
            final_pass(a).wait_send()

    for cp in tiny:
        cp.wait()
    ts[...] = (s_all[0] + s_all[1]) + (s_all[2] + s_all[3])
    tb[...] = (b_all[0] + b_all[1]) + (b_all[2] + b_all[3])


def step_exchange(cores, gq, go, gu, gd, wi, wb, mi, mb, vi, vb, ea, es, eb):
    rows, cols = wi.shape[1:]
    slot = (12, rows, cols)
    dma = pltpu.SemaphoreType.DMA
    return pl.pallas_call(
        functools.partial(step_kernel, cores),
        out_shape=(
            jax.ShapeDtypeStruct(slot, f32),
            jax.ShapeDtypeStruct(slot, bf16),
            jax.ShapeDtypeStruct(ea.shape, bf16),
            jax.ShapeDtypeStruct(es.shape, f32),
            jax.ShapeDtypeStruct(eb.shape, f32),
        ),
        in_specs=[ANY] * 10 + [VMEM] * 3,
        out_specs=(VMEM,) * 5,
        scratch_shapes=[
            pltpu.VMEM((12, 2 * rows, 2 * cols), bf16),
            pltpu.VMEM(slot, f32),
            pltpu.VMEM(slot, f32),
            pltpu.VMEM(slot, f32),
            pltpu.VMEM((12, 2, rows, cols), bf16),
            pltpu.VMEM(slot, bf16),
            pltpu.VMEM(slot, bf16),
            pltpu.VMEM(slot, bf16),
            pltpu.VMEM(slot, bf16),
            pltpu.VMEM((12, rows // 2, cols), bf16),
            pltpu.VMEM(ea.shape, bf16),
            pltpu.VMEM((ea.shape[0] // 2,) + ea.shape[1:], bf16),
            pltpu.VMEM((4,) + es.shape, f32),
            pltpu.VMEM((4,) + eb.shape, f32),
            pltpu.VMEM(ea.shape, bf16),
            pltpu.VMEM(es.shape, f32),
            pltpu.VMEM(eb.shape, f32),
            dma((18,)),
            dma((2, 12, 2)),
            dma((2, 12)),
            dma((2, 12)),
            dma((2, 12)),
            dma((2, 12, 3)),
            dma((2,)),
            dma((2,)),
            dma((2,)),
            dma((2, 3)),
            dma((2, 3)),
            dma((2, 3)),
        ],
        compiler_params=pltpu.CompilerParams(collective_id=5, has_side_effects=True, vmem_limit_bytes=58 * MIB),
        name="step_exchange",
    )(gq, go, gu, gd, wi, wb, mi, mb, vi, vb, ea, es, eb)


def angle_tables(length):
    half = HEAD_DIM // 2
    frequency = np.float32(10000.0) ** (np.float32(-2.0) * np.arange(half, dtype=np.float32) / np.float32(HEAD_DIM))
    angles = frequency[:, None] * np.arange(length, dtype=np.float32)[None, :]
    return jnp.asarray(np.cos(angles)), jnp.asarray(np.sin(angles))


def on_device(
    tokens, sigma_index, absorbed, cotangent, time_table,
    in_weight, back_weight, ada_weight, small_params, up_bias,
    in_first, back_first, ada_first, small_first, bias_first,
    in_second, back_second, ada_second, small_second, bias_second,
    in_moment, back_moment, ada_moment, small_moment, bias_moment,
):
    n_tp, n_dp, n_grp = lax.axis_size("tp"), lax.axis_size("dp"), lax.axis_size("grp")
    seqs, length, width = tokens.shape
    cores = n_tp // seqs
    part = in_weight.shape[2]
    heads_width = seqs * part
    direct = n_dp == 2 and n_grp == 4 and seqs == 2 and cores == 2
    t, d = lax.axis_index("tp"), lax.axis_index("dp")
    s = t // cores
    c = lax.rem(t, cores)
    groups = [[a * cores + b for a in range(seqs)] for b in range(cores)]

    wi_t = jnp.transpose(in_weight, (1, 2, 0))
    wa_t = jnp.transpose(ada_weight, (1, 0, 2))
    cosine, sine = angle_tables(length)
    if direct:
        first = (sigma_index, time_table, wa_t, small_params, up_bias, wi_t, back_weight)
    else:
        def over_tp(x, axis):
            return lax.all_gather(x, "tp", axis=axis, tiled=True, axis_index_groups=groups)

        table_ids = jnp.arange(time_table.shape[0], dtype=jnp.int32)
        onehot = (sigma_index[:, None] == table_ids[None, :]).astype(f32)
        condition = jax.nn.silu(jnp.dot(onehot, time_table, precision=highest))
        cond_low = condition.astype(bf16).astype(f32)
        wi_all = over_tp(lax.all_gather(wi_t.astype(bf16), "dp", axis=2, tiled=True), 1)
        wb_all = over_tp(lax.all_gather(back_weight.astype(bf16), "dp", axis=2, tiled=True), 1)
        weights = jnp.concatenate([wi_all[:3], wb_all[:1], wi_all[3:], wb_all[1:]], axis=0)
        bu_all = over_tp(lax.all_gather(up_bias.astype(bf16), "dp", axis=1, tiled=True)[None], 0)
        bias_row = jnp.transpose(bu_all, (1, 0, 2)).reshape(1, 4 * heads_width).astype(f32)
        small_rows = lax.all_gather(small_params.astype(bf16), "dp", axis=1, tiled=True).astype(f32)
        wa_all = lax.all_gather(ada_weight.astype(bf16), "dp", axis=0, tiled=True)
        mod_part = jnp.einsum("sc,cad->sad", cond_low.astype(bf16), wa_all, preferred_element_type=f32)
        mod_all = lax.all_gather(mod_part, "tp", axis=2, tiled=True)
        mod_rows = lax.dynamic_index_in_dim(mod_all, s, 0, keepdims=False) + small_rows[3:9]
        vecs = jnp.concatenate([small_rows[0:3], mod_rows, jnp.zeros((7, width), f32)], axis=0)
        first = (weights, vecs, bias_row)

    fw = forward(direct, cores, length, width, heads_width, first, tokens, absorbed, cotangent, cosine, sine)
    wq, wo = fw.wq_out[:3], fw.wq_out[3]
    inv = fw.inv_out.reshape(-1, 2, length)
    dh1, gq, go = pull_attention(
        fw.ga_out, wo, fw.o_out, inv, fw.probs_out, fw.q_out, fw.k_out, fw.v_out, cosine, sine, fw.h1_out, wq)
    gb = fw.gb.reshape(2, width)
    gu, gd = fw.gu_out, fw.gd_out
    tok = lax.dynamic_index_in_dim(tokens, s, 0, keepdims=False)
    if direct:
        conds = jnp.transpose(fw.cond_out[:, :seqs, : wa_t.shape[1]], (1, 0, 2))
    else:
        conds = jnp.transpose(lax.all_gather(cond_low, "dp", axis=0), (1, 0, 2))
        conds = lax.dynamic_slice_in_dim(conds, d * wa_t.shape[1], wa_t.shape[1], 2)
    block_out, grad_low, shared = last(
        cores, 2 if direct else 1, seqs, dh1, fw.dx1_out, tok, fw.block_half, fw.vecs_out, fw.stats, gb)
    input_grad = grad_low.astype(f32)

    if not direct:
        shared = lax.all_gather(shared[:, 0], "dp", axis=1)
    by_seq = shared.reshape(seqs, cores, n_dp, 16, width).sum(axis=1)
    dmod = by_seq[:, :, 0:6]
    small_grad = jnp.concatenate([by_seq[:, :, 6:9].sum(axis=(0, 1)), dmod.sum(axis=(0, 1))], axis=0)
    bias_sum = shared.reshape(seqs, cores, n_dp, 16, width)[:, :, :, 9:11].sum(axis=(0, 2))
    bias_sum = bias_sum.reshape(cores, 4, seqs, part)
    mine = lax.dynamic_index_in_dim(lax.dynamic_index_in_dim(bias_sum, c, 0, keepdims=False), s, 1, keepdims=False)
    bias_grad = lax.dynamic_slice_in_dim(mine, d * (part // n_dp), part // n_dp, 1)
    small_shard = lax.dynamic_slice_in_dim(small_grad, d * (width // n_dp), width // n_dp, 1)
    dmod_cols = lax.dynamic_slice_in_dim(dmod, t * part, part, 3)
    ada_grad = jnp.sum(conds[:, :, None, :, None] * dmod_cols[:, :, :, None, :], axis=(0, 1))

    am, av = jnp.transpose(ada_first[0], (1, 0, 2)), jnp.transpose(ada_second[0], (1, 0, 2))
    ada_m, ada_v = adam_parts(ada_grad, am, av)
    ada_d = adam_diff(wa_t, ada_m, ada_v, rate_matrix, decay_rate)
    small_m, small_v = adam_parts(small_shard, small_first[0], small_second[0])
    small_d = adam_diff(small_params, small_m, small_v, rate_small, 0.0)
    bias_m, bias_v = adam_parts(bias_grad, bias_first[0], bias_second[0])
    bias_d = adam_diff(up_bias, bias_m, bias_v, rate_small, 0.0)

    mi, vi = jnp.transpose(in_first[0], (1, 2, 0)), jnp.transpose(in_second[0], (1, 2, 0))
    mb, vb = back_first[0], back_second[0]
    if direct:
        gsum, total, ada_t, small_t, bias_t = step_exchange(
            cores, gq, go, gu, gd, wi_t, back_weight, mi, mb, vi, vb, ada_d, small_d, bias_d)
        gi, gbk = gsum[:7], gsum[7:]
        di, db = total[:7].astype(f32), total[7:].astype(f32)
        ada_t = ada_t.astype(f32)
    else:
        def scatter(x):
            x = lax.psum_scatter(x, "tp", scatter_dimension=1, tiled=True, axis_index_groups=groups)
            return lax.psum_scatter(x, "dp", scatter_dimension=2, tiled=True).astype(f32)

        def over_groups(x):
            return lax.psum(x.astype(bf16), "grp").astype(f32)

        gi = scatter(jnp.concatenate([gq, gu], axis=0))
        gbk = scatter(jnp.concatenate([go[None], gd], axis=0))
        im, iv = adam_parts(gi, mi, vi)
        bm, bv = adam_parts(gbk, mb, vb)
        di = over_groups(adam_diff(wi_t, im, iv, rate_matrix, decay_rate))
        db = over_groups(adam_diff(back_weight, bm, bv, rate_matrix, decay_rate))
        ada_t, small_t, bias_t = over_groups(ada_d), over_groups(small_d), over_groups(bias_d)
    in_m, in_v = adam_parts(gi, mi, vi)
    back_m, back_v = adam_parts(gbk, mb, vb)

    def outer(weight, moment, summed):
        diff = summed / n_grp
        moment_new = outer_mu * moment + diff
        return weight - outer_rate * (diff + outer_mu * moment_new), diff, moment_new

    def back_in(x):
        return jnp.transpose(x, (2, 0, 1))

    def back_ada(x):
        return jnp.transpose(x, (1, 0, 2))

    in_w, in_diff, in_mom = (back_in(x) for x in outer(wi_t, jnp.transpose(in_moment, (1, 2, 0)), di))
    back_w, back_diff, back_mom = outer(back_weight, back_moment, db)
    ada_w, ada_diff, ada_mom = (back_ada(x) for x in outer(wa_t, jnp.transpose(ada_moment, (1, 0, 2)), ada_t))
    small_w, small_diff, small_mom = outer(small_params, small_moment, small_t)
    bias_w, bias_diff, bias_mom = outer(up_bias, bias_moment, bias_t)
    return (
        block_out, input_grad,
        back_in(in_m)[None], back_m[None], back_ada(ada_m)[None], small_m[None], bias_m[None],
        back_in(in_v)[None], back_v[None], back_ada(ada_v)[None], small_v[None], bias_v[None],
        in_w, back_w, ada_w, small_w, bias_w,
        in_diff, back_diff, ada_diff, small_diff, bias_diff,
        in_mom, back_mom, ada_mom, small_mom, bias_mom,
    )


def solution(mesh):
    rows = P(("dp", "grp"), None, None)
    shared = (
        P("dp", None, "tp"), P(None, "tp", "dp"), P("dp", None, "tp"), P(None, "dp"), P(None, ("tp", "dp")),
    )
    grouped = (
        P("grp", "dp", None, "tp"), P("grp", None, "tp", "dp"), P("grp", "dp", None, "tp"),
        P("grp", None, "dp"), P("grp", None, ("tp", "dp")),
    )
    in_specs = (rows, P(("dp", "grp")), P(("dp", "grp"), None), rows, P()) + shared + grouped + grouped + shared
    out_specs = (rows, rows) + grouped + grouped + shared + shared + shared
    return jax.shard_map(on_device, mesh=mesh, in_specs=in_specs, out_specs=out_specs, check_vma=False)
```

```python
import functools
from types import SimpleNamespace

import jax
import jax.numpy as jnp
import numpy as np
from jax import lax
from jax.experimental import pallas as pl
from jax.experimental.pallas import tpu as pltpu
from jax.sharding import PartitionSpec as P

HEAD_DIM = 64
STEP = 10
MESH = pl.DeviceIdType.MESH
ANY = pl.BlockSpec(memory_space=pl.ANY)
VMEM = pl.BlockSpec(memory_space=pltpu.VMEM)
MIB = 2**20

f32 = jnp.float32
bf16 = jnp.bfloat16
highest = lax.Precision.HIGHEST
norm_eps = 1e-05
beta_one = 0.9
beta_two = 0.999
adam_eps = 1e-08
decay_rate = 0.1
rate_matrix = 0.03
rate_small = 0.3
outer_mu = 0.9
outer_rate = 0.7
gelu_a = 0.7978845608028654
gelu_b = 0.044715


def nn(a, b):
    return lax.dot_general(a, b, (((1,), (0,)), ((), ())), preferred_element_type=f32)


def nt(a, b):
    return lax.dot_general(a, b, (((1,), (1,)), ((), ())), preferred_element_type=f32)


def tn(a, b):
    return lax.dot_general(a, b, (((0,), (0,)), ((), ())), preferred_element_type=f32)


def fold(values):
    return jnp.sum(values.reshape(values.shape[0] // 8, 8, values.shape[1]), axis=0)


def normalize(values):
    mean = jnp.mean(values, axis=-1, keepdims=True)
    centered = values - mean
    variance = jnp.mean(centered * centered, axis=-1, keepdims=True)
    inverse = lax.rsqrt(variance + norm_eps)
    return centered * inverse, inverse


def norm_pull(grad_hat, hat, inverse):
    first = jnp.mean(grad_hat, axis=-1, keepdims=True)
    second = jnp.mean(grad_hat * hat, axis=-1, keepdims=True)
    return inverse * (grad_hat - first - hat * second)


def adam_parts(gradient, first, second):
    first_new = beta_one * first + (1.0 - beta_one) * gradient
    second_new = beta_two * second + (1.0 - beta_two) * gradient * gradient
    return first_new, second_new


def adam_diff(weight, first_new, second_new, rate, decay):
    first_hat = first_new / (1.0 - beta_one**STEP)
    second_hat = second_new / (1.0 - beta_two**STEP)
    return rate * (first_hat / (jnp.sqrt(second_hat) + adam_eps) + decay * weight)


def at(start, size, unit=128):
    return pl.ds(pl.multiple_of(start, unit), size)


def remote(source, target, send, recv, device):
    return pltpu.make_async_remote_copy(
        src_ref=source, dst_ref=target, send_sem=send, recv_sem=recv, device_id=device, device_id_type=MESH)


def turn(values, cosine, sine):
    heads = values.shape[0] // HEAD_DIM
    half = HEAD_DIM // 2
    out = []
    for h in range(heads):
        low = values[h * HEAD_DIM : h * HEAD_DIM + half]
        high = values[h * HEAD_DIM + half : (h + 1) * HEAD_DIM]
        out.append(low * cosine - high * sine)
        out.append(high * cosine + low * sine)
    return jnp.concatenate(out, axis=0)


def only_head(pair, h):
    row = lax.broadcasted_iota(jnp.int32, pair.shape, 0)
    return jnp.where(row // HEAD_DIM == h, pair, jnp.zeros_like(pair))


def greet(devices):
    barrier = pltpu.get_barrier_semaphore()
    for device in devices:
        pl.semaphore_signal(barrier, inc=1, device_id=device, device_id_type=MESH)
    pl.semaphore_wait(barrier, len(devices))


def plane_devices(t, d, n_tp, spans):
    others = []
    for dt in range(n_tp):
        for dd in range(spans):
            if dt or dd:
                dev = {"tp": lax.rem(t + dt, n_tp)}
                if spans > 1:
                    dev["dp"] = lax.rem(d + dd, spans)
                others.append(dev)
    return others


def forward_kernel(direct, cores, n_tp, names, *args):
    R = SimpleNamespace(**dict(zip(names, args)))
    t, d = lax.axis_index("tp"), lax.axis_index("dp")
    s = t // cores
    c = lax.rem(t, cores)
    length, width = R.tok.shape
    half = length // cores
    slot_rows = R.weights.shape[1]
    rows, cols = slot_rows // 2, width // 2
    own, other = at(c * half, half), at((1 - c) * half, half)
    sibling = {"tp": s * cores + (1 - c)}
    xdev = {"dp": 1 - d}
    ydev = {"tp": (1 - s) * cores + c}

    tok_load = pltpu.make_async_copy(R.tok_all.at[s], R.tok, R.load_sem.at[0])
    cot_load = pltpu.make_async_copy(R.cot_all.at[s], R.cot, R.load_sem.at[1])

    if direct:
        stages = (R.attn, R.x1, R.away)

        def staged(a):
            return stages[a // 4].at[pl.ds((a % 4 // 2) * rows, rows), pl.ds((a % 2) * cols, cols)]

        weight_loads = []
        for a in range(12):
            source = R.wi.at[a] if a < 3 else R.wb.at[0] if a == 3 else R.wi.at[a - 1] if a < 8 else R.wb.at[a - 7]
            weight_loads.append(pltpu.make_async_copy(source, staged(a), R.stage_sem.at[a]))
            weight_loads[a].start()
    else:
        weight_load = pltpu.make_async_copy(R.weights_in, R.weights, R.stage_sem.at[0])
        weight_load.start()
    tok_load.start()
    cot_load.start()

    def block(a, ss, dd):
        return R.weights.at[a, at(ss * rows, rows, 16), at(dd * cols, cols)]

    def hop(kind, a):
        if kind == 0:
            ref, dev = block(a, s, d), xdev
        elif kind == 1:
            ref, dev = block(a, s, d), ydev
        elif kind == 2:
            ref, dev = block(a, s, 1 - d), ydev
        else:
            ref, dev = block(a, 1 - s, d), xdev
        k = min(kind, 2)
        return remote(ref, ref, R.wsend.at[k, a], R.wrecv.at[k, a], dev)

    ahead = 2

    def launch(a):
        hop(0, a).start()
        hop(1, a).start()

    def pass_on(a):
        @pl.when(lax.rem(a, 2) == 0)
        def _():
            hop(0, a).wait_recv()
            hop(2, a).start()

        @pl.when(lax.rem(a, 2) == 1)
        def _():
            hop(1, a).wait_recv()
            hop(3, a).start()

        @pl.when(a + ahead < 12)
        def _():
            launch(a + ahead)

    def arrived(a):
        hop(1 - a % 2, a).wait_recv()
        hop(2 + a % 2, a).wait_recv()

    if direct:
        others = plane_devices(t, d, n_tp, 2)
        R.cond[...] = jnp.zeros_like(R.cond)
        for ss in range(2):
            row = R.table[pl.ds(R.sigma[ss], 1), :]
            R.cond[ss : ss + 1, :] = (row / (1.0 + jnp.exp(-row))).astype(bf16).astype(f32)
        turned = pltpu.roll(R.cond[...], R.cond.shape[1] // 2, 1)
        R.cond_near[...] = jnp.where(d == 0, R.cond[...], turned)
        R.cond_far[...] = jnp.where(d == 1, R.cond[...], turned)
        R.ps_low[...] = R.ps[...].astype(bf16).astype(f32)
        R.bu_low[...] = R.bu[...].astype(bf16).astype(f32)
        greet(others)
        cc = remote(R.cond_far, R.cond_got, R.small_sem.at[0, 0], R.small_sem.at[1, 0], xdev)
        cc.start()
        pc = remote(R.ps_low, R.ps_all.at[d], R.small_sem.at[0, 1], R.small_sem.at[1, 1], xdev)
        pc.start()
        bcs = []
        for i, (ds, dd) in enumerate(((0, 1), (1, 0), (1, 1))):
            dev = {"tp": lax.rem(s + ds, 2) * cores + c, "dp": lax.rem(d + dd, 2)}
            bcs.append(remote(R.bu_low, R.bu_all.at[s, d], R.small_sem.at[0, 2 + i], R.small_sem.at[1, 2 + i], dev))
            bcs[i].start()

        def prepare(a):
            weight_loads[a].wait()
            R.weights[a, at(s * rows, rows, 16), at(d * cols, cols)] = staged(a)[...].astype(bf16)

        for a in range(ahead):
            prepare(a)
            launch(a)
        R.ps_all[d] = R.ps_low[...]
        R.bu_all[s, d] = R.bu_low[...]
        span = R.wa.shape[1]
        R.parts[...] = jnp.zeros_like(R.parts)

        def partial_mod(source, dd):
            lhs = source[...][:, :span].astype(bf16)
            for a in range(6):
                product = nn(lhs, R.wa[a].astype(bf16))
                for ss in range(2):
                    R.parts[dd, ss, a : a + 1, :] = product[ss : ss + 1]

        partial_mod(R.cond_near, d)
        cc.wait()
        partial_mod(R.cond_got, 1 - d)
        mods = []
        for i, dev in enumerate(others):
            mods.append(remote(
                R.parts.at[dev["dp"], dev["tp"] // cores], R.mod_got.at[t, d], R.mod_sem.at[0, i], R.mod_sem.at[1, i], dev))
            mods[i].start()
        R.mod_got[t, d] = R.parts[d, s]
        R.cond_out[d] = R.cond_near[...]
        R.cond_out[1 - d] = R.cond_got[...]
        for a in range(ahead, 12):
            prepare(a)
        pc.wait()
        for bc in bcs:
            bc.wait()
        for mc in mods:
            mc.wait()
        small_rows = jnp.concatenate([R.ps_all[0], R.ps_all[1]], axis=1)
        mod_rows = jnp.concatenate([R.mod_got[tt, 0] + R.mod_got[tt, 1] for tt in range(n_tp)], axis=1)
        R.vecs[...] = jnp.zeros_like(R.vecs)
        R.vecs[0:3] = small_rows[0:3]
        R.vecs[3:9] = mod_rows[0:6] + small_rows[3:9]
        R.bias[...] = jnp.concatenate(
            [R.bu_all[ss, dd, j : j + 1, :] for j in range(4) for ss in range(2) for dd in range(2)], axis=1)
    else:
        greet([sibling])
        R.vecs[...] = R.vecs_in[...]
        R.bias[...] = R.bias_in[...]
        R.cond_out[...] = jnp.zeros_like(R.cond_out)

    tok_load.wait()
    step = 256

    @pl.loop(0, length // step)
    def _(i):
        r = at(i * step, step)
        hat, _ = normalize(R.tok[r].astype(f32))
        hidden = hat * (R.vecs[0:1] * (1.0 + R.vecs[4:5])) + R.vecs[3:4]
        R.h1[r] = hidden.astype(bf16)

    outs = []

    def emit(source, target):
        cp = pltpu.make_async_copy(source, target, R.out_sem.at[len(outs)])
        cp.start()
        outs.append(cp)

    emit(R.h1, R.h1_out)

    if direct:
        for a in range(3):
            pass_on(a)
        for a in range(3):
            arrived(a)
    else:
        weight_load.wait()
    @pl.loop(0, length // step)
    def _(i):
        r = at(i * step, step)
        low = R.h1[r]
        cos, sin = R.cosine[:, r], R.sine[:, r]
        R.q_t[:, r] = (turn(nt(R.weights[0], low), cos, sin) * 0.125).astype(bf16)
        keys = turn(nt(R.weights[1], low), cos, sin).astype(bf16)
        R.k_t[:, r] = keys
        R.k_r[r] = keys.T
        values = nt(R.weights[2], low).astype(bf16)
        R.v_t[:, r] = values
        R.v_r[r] = values.T

    emit(R.q_t, R.q_out)
    emit(R.k_t, R.k_out)
    emit(R.v_r, R.v_out)

    if direct:
        pass_on(3)
    heads = R.probs.shape[0]

    @pl.loop(0, heads)
    def _(h):
        pair = at(h // 2 * 2 * HEAD_DIM, 2 * HEAD_DIM)
        one = at(h * HEAD_DIM, HEAD_DIM, HEAD_DIM)
        scores = nn(R.k_r[:, pair], only_head(R.q_t[pair, :], lax.rem(h, 2)))
        top = jnp.max(scores, axis=0, keepdims=True)
        shifted = jnp.exp(scores - top)
        inverse = 1.0 / jnp.sum(shifted, axis=0, keepdims=True)
        low = shifted.astype(bf16)
        R.probs[h] = low
        R.inv_out[h] = inverse
        R.o_t[one, :] = (nn(R.v_t[one, :], low) * inverse).astype(bf16)
        if direct:
            @pl.when(lax.rem(h, 2) == 0)
            def _():
                pass_on(4 + h // 2)

    for h in range(heads):
        emit(R.probs.at[h], R.probs_out.at[h])
    emit(R.o_t, R.o_out)

    if direct:
        arrived(3)
    emit(R.weights.at[pl.ds(0, 4)], R.weights_out.at[pl.ds(0, 4)])
    away = remote(R.away, R.got, R.pair_sem.at[0, 0], R.pair_sem.at[1, 0], sibling)
    R.away[...] = tn(R.o_t[:, other], R.weights[3])
    away.start()
    R.attn[...] = tn(R.o_t[:, own], R.weights[3])
    if direct:
        pass_on(7)
    away.wait()
    small = 128

    @pl.loop(0, half // small)
    def _(i):
        r = at(i * small, small)
        total = R.attn[r] + R.got[r]
        R.attn[r] = total
        after = R.tok[at(c * half + i * small, small)].astype(f32) + R.vecs[5:6] * total
        R.x1[r] = after
        hat, _ = normalize(after)
        hidden = hat * (R.vecs[1:2] * (1.0 + R.vecs[7:8])) + R.vecs[6:7]
        R.h2[at(c * half + i * small, small)] = hidden.astype(bf16)

    share = remote(R.h2.at[own], R.h2.at[own], R.pair_sem.at[0, 1], R.pair_sem.at[1, 1], sibling)
    share.start()
    for cp in outs:
        cp.wait()
    flags = jnp.broadcast_to(R.flags[pl.ds(s, 1), :].astype(f32), (128, length)).T
    R.column[...] = flags
    cot_load.wait()

    chunks = 2
    if direct:
        pass_on(8)
        for a in range(4, 8):
            arrived(a)
    outs.clear()
    emit(R.weights.at[pl.ds(4, 4)], R.weights_out.at[pl.ds(4, 4)])
    emit(R.attn, R.attn_out)
    emit(R.x1, R.x1_out)
    emit(R.vecs, R.vecs_out)

    def up(r):
        low = R.h2[r]
        grad = R.cot[r].astype(f32) * jnp.concatenate([R.column[r]] * (width // 128), axis=1)
        R.cot[r] = grad.astype(bf16)
        R.probs[4, r, 0:width] = (R.vecs[8:9] * grad).astype(bf16)
        for j in range(chunks):
            pair = R.weights[4 + 2 * j : 6 + 2 * j].reshape(2 * slot_rows, width)
            u = nt(low, pair) + R.bias[:, j * width : (j + 1) * width]
            square = u * u
            inner = jnp.tanh(gelu_a * (u + gelu_b * square * u))
            z = 0.5 * u * (1.0 + inner)
            slope = 0.5 * (1.0 + inner) + 0.5 * u * (1.0 - inner * inner) * gelu_a * (1.0 + 3.0 * gelu_b * square)
            R.probs[j, r, 0:width] = z.astype(bf16)
            R.probs[2 + j, r, 0:width] = slope.astype(bf16)

    @pl.loop(0, half // step)
    def _(i):
        up(at(c * half + i * step, step))

    if direct:
        pass_on(9)
    share.wait()
    emit(R.h2, R.h2_out)
    emit(R.cot.at[own], R.gy_out)

    @pl.loop(0, half // step)
    def _(i):
        up(at((1 - c) * half + i * step, step))

    for k in range(4):
        emit(R.probs.at[k, :, pl.ds(0, width)], R.hidden_out.at[k])
    emit(R.probs.at[4, :, pl.ds(0, width)], R.gm_out)
    if direct:
        pass_on(10)

    for k in range(4):
        where = pl.ds((k % 2) * slot_rows, slot_rows)
        R.gd[k] = tn(R.probs[k // 2, :, where], R.probs[4, :, 0:width]).astype(bf16)
        if k == 1 and direct:
            pass_on(11)
    emit(R.gd, R.gd_out)
    if direct:
        for a in range(8, 12):
            arrived(a)
    emit(R.weights.at[pl.ds(8, 4)], R.weights_out.at[pl.ds(8, 4)])
    if direct:
        for a in range(12):
            hop(0, a).wait_send()
            hop(1, a).wait_send()
            hop(2 + a % 2, a).wait_send()
    for cp in outs:
        cp.wait()


def forward(direct, cores, length, width, slot_rows, first, tokens, flags, cotangent, cosine, sine):
    n_tp = lax.axis_size("tp")
    half = length // cores
    heads = slot_rows // HEAD_DIM
    dma = pltpu.SemaphoreType.DMA
    smem = pl.BlockSpec(memory_space=pltpu.SMEM)
    arr = jax.ShapeDtypeStruct
    vm = pltpu.VMEM
    if direct:
        ins = dict(sigma=smem, table=VMEM, wa=VMEM, ps=VMEM, bu=VMEM, wi=ANY, wb=ANY)
    else:
        ins = dict(weights_in=ANY, vecs_in=VMEM, bias_in=VMEM)
    ins |= dict(tok_all=ANY, flags=VMEM, cot_all=ANY, cosine=VMEM, sine=VMEM)
    outs = dict(
        h1_out=(arr((length, width), bf16), ANY),
        weights_out=(arr((12, slot_rows, width), bf16), ANY),
        q_out=(arr((slot_rows, length), bf16), ANY),
        k_out=(arr((slot_rows, length), bf16), ANY),
        v_out=(arr((length, slot_rows), bf16), ANY),
        probs_out=(arr((heads, length, length), bf16), ANY),
        inv_out=(arr((heads, 1, length), f32), VMEM),
        o_out=(arr((slot_rows, length), bf16), ANY),
        attn_out=(arr((half, width), f32), ANY),
        x1_out=(arr((half, width), f32), ANY),
        h2_out=(arr((length, width), bf16), ANY),
        vecs_out=(arr((16, width), f32), ANY),
        hidden_out=(arr((4, length, width), bf16), ANY),
        gm_out=(arr((length, width), bf16), ANY),
        gy_out=(arr((half, width), bf16), ANY),
        gd_out=(arr((4, slot_rows, width), bf16), ANY),
        cond_out=(arr((2, 8, 128), f32), VMEM),
    )
    scratch = dict(
        tok=vm((length, width), bf16),
        cot=vm((length, width), bf16),
        weights=vm((12, slot_rows, width), bf16),
        h1=vm((length, width), bf16),
        q_t=vm((slot_rows, length), bf16),
        k_t=vm((slot_rows, length), bf16),
        v_t=vm((slot_rows, length), bf16),
        k_r=vm((length, slot_rows), bf16),
        v_r=vm((length, slot_rows), bf16),
        probs=vm((heads, length, length), bf16),
        o_t=vm((slot_rows, length), bf16),
        away=vm((half, width), f32),
        got=vm((half, width), f32),
        attn=vm((half, width), f32),
        x1=vm((half, width), f32),
        h2=vm((length, width), bf16),
        column=vm((length, 128), f32),
        bias=vm((1, 4 * slot_rows), f32),
        vecs=vm((16, width), f32),
        gd=vm((4, slot_rows, width), bf16),
        load_sem=dma((2,)),
        stage_sem=dma((12,)),
        out_sem=dma((20,)),
        pair_sem=dma((2, 2)),
    )
    if direct:
        wa, ps, bu = first[2:5]
        scratch |= dict(
            cond=vm((8, 128), f32),
            cond_near=vm((8, 128), f32),
            cond_far=vm((8, 128), f32),
            cond_got=vm((8, 128), f32),
            ps_low=vm(ps.shape, f32),
            bu_low=vm(bu.shape, f32),
            ps_all=vm((2,) + ps.shape, f32),
            bu_all=vm((2, 2) + bu.shape, f32),
            parts=vm((2, 2, 8, wa.shape[2]), f32),
            mod_got=vm((n_tp, 2, 8, wa.shape[2]), f32),
            wsend=dma((3, 12)),
            wrecv=dma((3, 12)),
            small_sem=dma((2, 5)),
            mod_sem=dma((2, 2 * n_tp - 1)),
        )
    names = list(ins) + list(outs) + list(scratch)
    results = pl.pallas_call(
        functools.partial(forward_kernel, direct, cores, n_tp, names),
        out_shape=tuple(o[0] for o in outs.values()),
        in_specs=list(ins.values()),
        out_specs=tuple(o[1] for o in outs.values()),
        scratch_shapes=list(scratch.values()),
        compiler_params=pltpu.CompilerParams(collective_id=0, has_side_effects=True, vmem_limit_bytes=60 * MIB),
        name="forward",
    )(*first, tokens, flags, cotangent, cosine, sine)
    return SimpleNamespace(**dict(zip(outs, results)))


def backward_kernel(direct, cores, n_tp, names, *args):
    R = SimpleNamespace(**dict(zip(names, args)))
    t, g = lax.axis_index("tp"), lax.axis_index("grp")
    spans = 2 if direct else 1
    d = lax.axis_index("dp") if direct else 0
    s = t // cores
    c = lax.rem(t, cores)
    length, width = R.ga.shape
    half = length // cores
    slot_rows = R.weights.shape[1]
    rows, cols = slot_rows // 2, width // 2
    own, other = at(c * half, half), at((1 - c) * half, half)
    sibling = {"tp": s * cores + (1 - c)}
    across = {"tp": (1 - s) * cores + c}
    xdev = {"dp": 1 - d}
    heads = R.inv.shape[0]
    others = plane_devices(t, d, n_tp, spans)

    def load(source, target, i):
        cp = pltpu.make_async_copy(source, target, R.load_sem.at[i])
        cp.start()
        return cp

    def load_probs(h, slot):
        return pltpu.make_async_copy(R.probs_in.at[h], R.spare.at[slot], R.probs_sem.at[slot])

    spare = R.spare
    if direct:
        gd_load = pltpu.make_async_copy(R.gd_in, R.weights.at[pl.ds(12, 4)], R.gd_sem)
        gd_load.start()
        greet(others + [{"grp": lax.rem(g + 1 + i, 4)} for i in range(3)])
    else:
        greet(others)
    loads = [load(R.weights_in.at[pl.ds(8, 4)], R.weights.at[pl.ds(8, 4)], 0), load(R.gm_in, spare.at[4, :, pl.ds(0, width)], 1)]
    for k in (2, 3, 0, 1):
        loads.append(load(R.hidden_in.at[k], spare.at[k, :, pl.ds(0, width)], 2 + k))
    loads.append(load(R.weights_in.at[pl.ds(0, 8)], R.weights.at[pl.ds(0, 8)], 6))
    for i, (source, target) in enumerate((
        (R.x1_in, R.x1), (R.attn_in, R.attn), (R.gy_in, R.gy), (R.h2_in, R.hid), (R.o_in, R.o_t), (R.v_in, R.v_r),
        (R.k_in, R.k_t), (R.q_in, R.q_t))):
        loads.append(load(source, target, 7 + i))

    inner = jnp.logical_or(g == 1, g == 2)
    outer = jnp.logical_not(inner)
    pair = jnp.where(g == 0, 1, jnp.where(g == 1, 0, jnp.where(g == 2, 3, 2)))
    pdev = {"grp": pair}
    mdev = {"grp": 3 - g}
    mine = jnp.where(g == 1, 0, 1)
    hrows = rows // 2
    n_slots = 12
    window = 3

    pieces = 4
    size = half // pieces

    def piece(k):
        return at(c * half + k * size, size)

    def spread(kind, target):
        copies = (
            remote(R.half_out, target.at[s, own], R.spread_sem.at[0, kind, 0], R.spread_sem.at[1, kind, 0], sibling),
            pltpu.make_async_copy(R.half_out, target.at[s, own], R.spread_sem.at[0, kind, 1]),
        )
        for cp in copies:
            cp.start()
        return copies

    def cross(kind, target, k):
        source = R.half_out.at[at(k * size, size)]
        return remote(source, target.at[s, piece(k)], R.cross_sem.at[0, kind, k], R.cross_sem.at[1, kind, k], across)

    def relay(kind, target, k):
        ref = target.at[1 - s, piece(k)]
        return remote(ref, ref, R.relay_sem.at[0, kind, k], R.relay_sem.at[1, kind, k], sibling)

    def pass_piece(kind, target, k):
        cross(kind, target, k).wait_recv()
        relay(kind, target, k).start()

    def place(a):
        return jnp.where(a < 4, a + 12, jnp.where(a < 8, a + 4, a - 4))

    def order(a):
        return jnp.where(a < 4, a + 8, jnp.where(a < 8, a - 1, jnp.where(a == 8, 7, a - 9)))

    def first_hop(a):
        return remote(R.weights.at[place(a), :, at((1 - d) * cols, cols)], R.got_a.at[a], R.asem.at[0, a], R.asem.at[1, a], xdev)

    def second_hop(a):
        return remote(R.send_b.at[a], R.got_b.at[a], R.bsem.at[0, a], R.bsem.at[1, a], across)

    def state_load(a, run):
        slot = lax.rem(a, 3)
        for low, high, refs, base in (
            (0, 4, (R.wb, R.mb, R.vb), 1), (4, 8, (R.wi, R.mi, R.vi), 3), (8, 9, (R.wb, R.mb, R.vb), 0), (9, 12, (R.wi, R.mi, R.vi), 0)):
            @pl.when(jnp.logical_and(a >= low, a < high))
            def _():
                for k in range(3):
                    run(pltpu.make_async_copy(refs[k].at[a - low + base], R.state.at[slot, k], R.state_sem.at[slot, k]))

    def pair_send(a):
        return remote(R.diff.at[a], R.got_p.at[a], R.psem.at[0, a], R.psem.at[1, a], pdev)

    def h_at(k):
        return at(k * hrows, hrows, 16)

    def half_send(a):
        return remote(R.got_p.at[a, h_at(1 - mine)], R.got_h.at[a], R.hsem.at[0, a], R.hsem.at[1, a], mdev)

    def final(a, kind, dev):
        ref = R.total.at[order(a), h_at(1 - mine if kind == 2 else mine)]
        return remote(ref, ref, R.fsem.at[0, a, kind], R.fsem.at[1, a, kind], dev)

    def sum_copy(a):
        return pltpu.make_async_copy(R.sum_ring.at[lax.rem(a, 3)], R.gsum.at[order(a)], R.sum_sem.at[lax.rem(a, 3)])

    def stage_b(a):
        first_hop(a).wait_recv()

        @pl.when(a + window < n_slots)
        def _():
            first_hop(a + window).start()

        there = at((1 - s) * rows, rows, 16)
        R.send_b[a] = (R.weights[place(a), there, at(d * cols, cols)].astype(f32) + R.got_a[a, there].astype(f32)).astype(bf16)
        second_hop(a).start()
        state_load(a, lambda cp: cp.start())

    def stage_c(a):
        second_hop(a).wait_recv()
        here = at(s * rows, rows, 16)
        gradient = R.weights[place(a), here, at(d * cols, cols)].astype(f32) + R.got_a[a, here].astype(f32) + R.got_b[a].astype(f32)
        ring = lax.rem(a, 3)

        @pl.when(a >= 3)
        def _():
            sum_copy(a - 3).wait()

        R.sum_ring[ring] = gradient
        sum_copy(a).start()
        state_load(a, lambda cp: cp.wait())
        slot = lax.rem(a, 3)
        first_new, second_new = adam_parts(gradient, R.state[slot, 1], R.state[slot, 2])
        R.diff[a] = adam_diff(R.state[slot, 0], first_new, second_new, rate_matrix, decay_rate).astype(bf16)

        @pl.when(outer)
        def _():
            pair_send(a).start()

    def stage_d(a):
        pair_send(a).wait_recv()
        R.got_p[a] = (R.diff[a].astype(f32) + R.got_p[a].astype(f32)).astype(bf16)
        half_send(a).start()

    def stage_e(a):
        half_send(a).wait_recv()
        R.total[order(a), h_at(mine)] = (R.got_p[a, h_at(mine)].astype(f32) + R.got_h[a].astype(f32)).astype(bf16)
        final(a, 0, mdev).start()
        final(a, 1, pdev).start()

    def stage_f(a):
        remote(R.got_h.at[a], R.got_h.at[a], R.fsem.at[0, a, 0], R.fsem.at[1, a, 0], mdev).wait_recv()
        final(a, 2, pdev).start()

    def advance(j):
        for stage, lag, only in (
            (stage_b, 0, None), (stage_c, 2, None), (stage_d, 4, inner), (stage_e, 5, inner), (stage_f, 6, inner)):
            a = j - lag
            ok = jnp.logical_and(a >= 0, a < n_slots)

            @pl.when(ok if only is None else jnp.logical_and(ok, only))
            def _():
                stage(a)

    if direct:
        gd_load.wait()
        for a in range(window):
            first_hop(a).start()

    chunks = 2
    step = 256
    R.bias_sum[...] = jnp.zeros_like(R.bias_sum)
    for i in range(7):
        loads[i].wait()

    def down(r, target, where):
        gm = spare[4, r, 0:width]
        forward = jnp.zeros((step, width), f32)
        backward = jnp.zeros((step, width), f32)
        for j in range(chunks):
            lower = R.weights[8 + 2 * j : 10 + 2 * j].reshape(2 * slot_rows, width)
            upper = R.weights[4 + 2 * j : 6 + 2 * j].reshape(2 * slot_rows, width)
            du = (nt(gm, lower) * spare[2 + j, r, 0:width].astype(f32)).astype(bf16)
            spare[2 + j, r, 0:width] = du
            R.bias_sum[:, j * width : (j + 1) * width] += fold(du.astype(f32))
            forward += nn(spare[j, r, 0:width], lower)
            backward += nn(du, upper)
        spare[5, r, 0:width] = forward.astype(bf16)
        target[where] = backward.astype(bf16)

    @pl.loop(0, half // step)
    def _(i):
        down(at((1 - c) * half + i * step, step), R.tok, at(i * step, step))

    trades = [
        remote(spare.at[5, other, pl.ds(0, width)], R.trade.at[0], R.pair_sem.at[0, 0], R.pair_sem.at[1, 0], sibling),
        remote(R.tok, R.trade.at[1], R.pair_sem.at[0, 1], R.pair_sem.at[1, 1], sibling),
    ]
    for cp in trades:
        cp.start()

    @pl.loop(0, half // step)
    def _(i):
        down(at(c * half + i * step, step), R.half_out, at(i * step, step))

    small = 128
    R.acc[...] = jnp.zeros_like(R.acc)
    for i in range(7, 11):
        loads[i].wait()
    for cp in trades:
        cp.wait()
    loads.append(load(R.tok_all.at[s, own], R.tok, 15))

    @pl.loop(0, half // small)
    def _(i):
        r = at(i * small, small)
        g = at(c * half + i * small, small)
        after = R.x1[r]
        branch = spare[5, g, 0:width].astype(f32) + R.trade[0, r].astype(f32) + R.vecs[2:3]
        grad = R.gy[r].astype(f32)
        dh = R.half_out[r].astype(f32) + R.trade[1, r].astype(f32)
        R.half_out[r] = (after + R.vecs[8:9] * branch).astype(bf16)
        hat, inverse = normalize(after)
        total = grad + norm_pull(dh * (R.vecs[1:2] * (1.0 + R.vecs[7:8])), hat, inverse)
        R.x1[r] = total
        R.ga[g] = (R.vecs[5:6] * total).astype(bf16)
        R.acc[0] += fold(dh)
        R.acc[1] += fold(dh * hat)
        R.acc[2] += fold(total * R.attn[r])
        R.acc[3] += fold(grad * branch)
        R.acc[4] += fold(spare[4, g, 0:width].astype(f32))

    give = remote(R.ga.at[own], R.ga.at[own], R.pair_sem.at[0, 2], R.pair_sem.at[1, 2], sibling)
    give.start()
    block_copies = spread(0, R.block_out)
    cross(0, R.block_out, 0).start()
    for i in range(5):
        R.stats[i : i + 1] = jnp.sum(R.acc[i], axis=0, keepdims=True)

    for k in range(4):
        where = pl.ds((k % 2) * slot_rows, slot_rows)
        R.weights[8 + k] = tn(spare[2 + k // 2, :, where], R.hid[...]).astype(bf16)
    for h in range(4):
        load_probs(h, h).start()
    h1_load = pltpu.make_async_copy(R.h1_in, R.hid, R.load_sem.at[16])
    h1_load.start()
    if direct:
        advance(0)
        advance(1)

    for i in range(11, 16):
        loads[i].wait()
    give.wait()
    R.weights[4] = nn(R.o_t[...], R.ga[...]).astype(bf16)
    do_t = nt(R.weights[3], R.ga[...])
    for h in range(heads):
        one = pl.ds(h * HEAD_DIM, HEAD_DIM)
        R.do_t[one] = (do_t[h * HEAD_DIM : (h + 1) * HEAD_DIM] * R.inv[h]).astype(bf16)
    wide = 256

    @pl.loop(0, heads)
    def _(h):
        two = at(h // 2 * 2 * HEAD_DIM, 2 * HEAD_DIM)
        one = at(h * HEAD_DIM, HEAD_DIM, HEAD_DIM)
        slot = lax.rem(h, 4)
        load_probs(h, slot).wait()
        delta = jnp.sum(R.do_t[one].astype(f32) * R.o_t[one].astype(f32), axis=0, keepdims=True)
        for i in range(length // wide):
            q = slice(i * wide, (i + 1) * wide)
            dp = nn(R.v_r[:, two], only_head(R.do_t[two, q], lax.rem(h, 2)))
            spare[4, :, q] = (spare[slot, :, q].astype(f32) * (dp - delta[:, q])).astype(bf16)
        cos, sin = R.cosine[...], R.sine[...]
        dq = nn(R.k_t[one], spare[4]) * 0.125
        dk = nt(R.q_t[one], spare[4])
        spare[5, one] = turn(dq, cos, -sin).astype(bf16)
        spare[5, at(slot_rows + h * HEAD_DIM, HEAD_DIM, HEAD_DIM)] = turn(dk, cos, -sin).astype(bf16)
        R.dv_t[one] = nt(R.do_t[one], spare[slot]).astype(bf16)

        @pl.when(h + 4 < heads)
        def _():
            load_probs(h + 4, slot).start()

        @pl.when(h < pieces - 1)
        def _():
            cross(0, R.block_out, h + 1).start()

        if direct:
            @pl.when(jnp.logical_or(h == 2, h == 3))
            def _():
                advance(h)

    h1_load.wait()
    turned = (spare.at[5, pl.ds(0, slot_rows)], spare.at[5, pl.ds(slot_rows, slot_rows)], R.dv_t)
    for k in range(3):
        R.weights[5 + k] = nn(turned[k][...], R.hid[...]).astype(bf16)
    if direct:
        advance(4)
    for k in range(pieces):
        pass_piece(0, R.block_out, k)

    def dh1_part(r):
        total = tn(turned[0][:, r], R.weights[0])
        for k in range(1, 3):
            total += tn(turned[k][:, r], R.weights[k])
        return total

    R.trade[0] = dh1_part(other).astype(bf16)
    trade = remote(R.trade.at[0], R.trade.at[1], R.pair_sem.at[0, 3], R.pair_sem.at[1, 3], sibling)
    trade.start()
    R.attn[...] = dh1_part(own)

    R.acc[...] = jnp.zeros_like(R.acc)
    trade.wait()
    block_copies[0].wait_send()
    block_copies[1].wait()
    for k in range(pieces):
        cross(0, R.block_out, k).wait_send()

    @pl.loop(0, half // small)
    def _(i):
        r = at(i * small, small)
        dh = R.attn[r] + R.trade[1, r].astype(f32)
        hat, inverse = normalize(R.tok[r].astype(f32))
        R.acc[0] += fold(dh)
        R.acc[1] += fold(dh * hat)
        total = R.x1[r] + norm_pull(dh * (R.vecs[0:1] * (1.0 + R.vecs[4:5])), hat, inverse)
        R.half_out[r] = total.astype(bf16)

    grad_copies = spread(1, R.grad_out)
    cross(1, R.grad_out, 0).start()
    if direct:
        advance(5)
    shift1 = jnp.sum(R.acc[0], axis=0, keepdims=True)
    turn1 = jnp.sum(R.acc[1], axis=0, keepdims=True)
    R.sums[...] = jnp.zeros_like(R.sums)
    R.sums[0:1] = shift1
    R.sums[1:2] = turn1 * R.vecs[0:1]
    R.sums[2:3] = R.stats[2:3]
    R.sums[3:4] = R.stats[0:1]
    R.sums[4:5] = R.stats[1:2] * R.vecs[1:2]
    R.sums[5:6] = R.stats[3:4]
    R.sums[6:7] = turn1 * (1.0 + R.vecs[4:5])
    R.sums[7:8] = R.stats[1:2] * (1.0 + R.vecs[7:8])
    R.sums[8:9] = R.stats[4:5]
    bias_total = jnp.sum(R.bias_sum[...], axis=0, keepdims=True)
    R.sums[9:10] = bias_total[:, 0:width]
    R.sums[10:11] = bias_total[:, width : 2 * width]
    R.shared[t, d] = R.sums[...]
    casts = [
        remote(R.sums, R.shared.at[t, d], R.cast_sem.at[0, i], R.cast_sem.at[1, i], dev) for i, dev in enumerate(others)
    ]
    for cp in casts:
        cp.start()
    if direct:
        advance(6)
        advance(7)
    for cp in casts:
        cp.wait()
    if direct:
        step_small(R, t, d, g, s, c, n_tp, width)
        a_rows = R.ada_low.shape[0] // 2

        def ada_at(ref, k):
            return ref.at[pl.ds(k * a_rows, a_rows)]

        tiny = []
        for i in range(3):
            dev = {"grp": lax.rem(g + 1 + i, 4)}
            tiny.append(remote(R.small_low, R.small_all.at[g], R.tiny_sem.at[0, 0, i], R.tiny_sem.at[1, 0, i], dev))
            tiny.append(remote(R.bias_low, R.bias_all.at[g], R.tiny_sem.at[0, 1, i], R.tiny_sem.at[1, 1, i], dev))
        for cp in tiny:
            cp.start()
        R.small_all[g] = R.small_low[...]
        R.bias_all[g] = R.bias_low[...]
        ada_sem = R.ada_sem
        a_pair = remote(R.ada_low, R.ada_p, ada_sem.at[0, 0], ada_sem.at[1, 0], pdev)
        a_half = remote(ada_at(R.ada_p, 1 - mine), R.ada_h, ada_sem.at[0, 1], ada_sem.at[1, 1], mdev)
        a_mid = remote(ada_at(R.ada_total, mine), ada_at(R.ada_total, mine), ada_sem.at[0, 2], ada_sem.at[1, 2], mdev)
        a_out = remote(ada_at(R.ada_total, mine), ada_at(R.ada_total, mine), ada_sem.at[0, 3], ada_sem.at[1, 3], pdev)
        a_pass = remote(ada_at(R.ada_total, 1 - mine), ada_at(R.ada_total, 1 - mine), ada_sem.at[0, 4], ada_sem.at[1, 4], pdev)

        @pl.when(outer)
        def _():
            a_pair.start()

        @pl.loop(8, n_slots + 6)
        def _(j):
            advance(j)

            @pl.when(j < 7 + pieces)
            def _():
                cross(1, R.grad_out, j - 7).start()

            @pl.when(jnp.logical_and(j >= 10, j < 10 + pieces))
            def _():
                pass_piece(1, R.grad_out, j - 10)

            @pl.when(jnp.logical_and(inner, j == 8))
            def _():
                a_pair.wait_recv()
                R.ada_p[...] = (R.ada_p[...].astype(f32) + R.ada_low[...].astype(f32)).astype(bf16)
                a_half.start()

            @pl.when(jnp.logical_and(inner, j == 9))
            def _():
                a_half.wait()
                mine_rows = pl.ds(mine * a_rows, a_rows)
                R.ada_total[mine_rows] = (R.ada_p[mine_rows].astype(f32) + R.ada_h[...].astype(f32)).astype(bf16)
                a_mid.start()
                a_out.start()

            @pl.when(jnp.logical_and(inner, j == 10))
            def _():
                a_mid.wait()
                a_pass.start()

    else:
        for k in range(1, pieces):
            cross(1, R.grad_out, k).start()
        for k in range(pieces):
            pass_piece(1, R.grad_out, k)
    if direct:
        @pl.when(outer)
        def _():
            a_pair.wait_send()
            remote(R.ada_h, R.ada_h, ada_sem.at[0, 3], ada_sem.at[1, 3], pdev).wait_recv()
            remote(R.ada_h, R.ada_h, ada_sem.at[0, 4], ada_sem.at[1, 4], pdev).wait_recv()

            @pl.loop(0, n_slots)
            def _(a):
                pair_send(a).wait_send()
                remote(R.got_h.at[a], R.got_h.at[a], R.fsem.at[0, a, 1], R.fsem.at[1, a, 1], pdev).wait_recv()
                remote(R.got_h.at[a], R.got_h.at[a], R.fsem.at[0, a, 2], R.fsem.at[1, a, 2], pdev).wait_recv()

        @pl.when(inner)
        def _():
            a_out.wait_send()
            a_pass.wait_send()

            @pl.loop(0, n_slots)
            def _(a):
                half_send(a).wait_send()
                final(a, 0, mdev).wait_send()
                final(a, 1, pdev).wait_send()
                final(a, 2, pdev).wait_send()

        for a in range(n_slots):
            first_hop(a).wait_send()
            second_hop(a).wait_send()
        for cp in tiny:
            cp.wait()
        R.small_total[...] = (R.small_all[0] + R.small_all[1]) + (R.small_all[2] + R.small_all[3])
        R.bias_total[...] = (R.bias_all[0] + R.bias_all[1]) + (R.bias_all[2] + R.bias_all[3])
        for a in range(n_slots - 3, n_slots):
            sum_copy(a).wait()
    else:
        R.grads[...] = R.weights[4:8]
        R.grads_up[...] = R.weights[8:12]
    block_copies[0].wait_recv()
    for cp in grad_copies:
        cp.wait()
    for k in range(pieces):
        cross(1, R.grad_out, k).wait_send()
        relay(0, R.block_out, k).wait()
        relay(1, R.grad_out, k).wait()


def step_small(R, t, d, g, s, c, n_tp, width):
    part = R.wa.shape[2]
    everything = R.shared[0, 0]
    for tt in range(n_tp):
        for dd in range(2):
            if tt or dd:
                everything = everything + R.shared[tt, dd]
    R.summed[...] = everything
    near = at(d * (width // 2), width // 2)
    R.small_grad[0:3] = R.summed[6:9, near]
    R.small_grad[3:9] = R.summed[0:6, near]
    first_new, second_new = adam_parts(R.small_grad[...], R.ms[...], R.vs[...])
    R.small_low[...] = adam_diff(R.ps[...], first_new, second_new, rate_small, 0.0).astype(bf16).astype(f32)

    mine = R.shared[c, 0, 8:16]
    for ss in range(2):
        for dd in range(2):
            if ss or dd:
                mine = mine + R.shared[ss * (n_tp // 2) + c, dd, 8:16]
    size = R.bu.shape[1]
    turned = pltpu.roll(mine, lax.rem(width - (s * 2 + d) * size, width), 1)
    R.bias_grad[0:1] = turned[1:2, 0:size]
    R.bias_grad[1:2] = turned[1:2, width // 2 : width // 2 + size]
    R.bias_grad[2:3] = turned[2:3, 0:size]
    R.bias_grad[3:4] = turned[2:3, width // 2 : width // 2 + size]
    first_new, second_new = adam_parts(R.bias_grad[...], R.mu[...], R.vu[...])
    R.bias_low[...] = adam_diff(R.bu[...], first_new, second_new, rate_small, 0.0).astype(bf16).astype(f32)

    R.ada_rows[...] = jnp.zeros_like(R.ada_rows)
    R.cond_rows[...] = jnp.zeros_like(R.cond_rows)
    for ss in range(2):
        for dd in range(2):
            total = R.shared[2 * ss, dd, 0:8] + R.shared[2 * ss + 1, dd, 0:8]
            turned = pltpu.roll(total, lax.rem(width - t * part, width), 1)
            k = ss * 2 + dd
            R.cond_rows[k : k + 1] = R.cond[dd, ss : ss + 1]
            for a in range(6):
                R.ada_rows[a, k : k + 1] = turned[a : a + 1, 0:part]
    lhs = R.cond_rows[...][:, : R.wa.shape[1]]
    for a in range(6):
        gradient = lax.dot_general(
            lhs, R.ada_rows[a], (((0,), (0,)), ((), ())), precision=highest, preferred_element_type=f32)
        R.ada_grad[a] = gradient
        first_new, second_new = adam_parts(gradient, R.ma[a], R.va[a])
        R.ada_low[a] = adam_diff(R.wa[a], first_new, second_new, rate_matrix, decay_rate).astype(bf16)


def backward(direct, cores, seqs, fw, tokens, cosine, sine, states, smalls):
    n_tp = lax.axis_size("tp")
    length, width = fw.h1_out.shape
    heads = fw.inv_out.shape[0]
    slot_rows = fw.weights_out.shape[1]
    half = length // cores
    dma = pltpu.SemaphoreType.DMA
    arr = jax.ShapeDtypeStruct
    vm = pltpu.VMEM
    spans = 2 if direct else 1
    ins = dict(
        weights_in=(fw.weights_out, ANY), o_in=(fw.o_out, ANY), v_in=(fw.v_out, ANY),
        k_in=(fw.k_out, ANY), q_in=(fw.q_out, ANY), probs_in=(fw.probs_out, ANY), h1_in=(fw.h1_out, ANY),
        x1_in=(fw.x1_out, ANY), attn_in=(fw.attn_out, ANY), h2_in=(fw.h2_out, ANY), hidden_in=(fw.hidden_out, ANY),
        gm_in=(fw.gm_out, ANY), gy_in=(fw.gy_out, ANY), tok_all=(tokens, ANY),
        inv=(fw.inv_out, VMEM), vecs=(fw.vecs_out, VMEM), cosine=(cosine, VMEM), sine=(sine, VMEM),
    )
    outs = dict(
        block_out=(arr((seqs, length, width), bf16), ANY),
        grad_out=(arr((seqs, length, width), bf16), ANY),
    )
    scratch = dict(
        weights=vm((16 if direct else 12, slot_rows, width), bf16),
        spare=vm((heads, length, length), bf16),
        ga=vm((length, width), bf16),
        hid=vm((length, width), bf16),
        trade=vm((2, half, width), bf16),
        x1=vm((half, width), f32),
        attn=vm((half, width), f32),
        gy=vm((half, width), bf16),
        tok=vm((half, width), bf16),
        half_out=vm((half, width), bf16),
        o_t=vm((slot_rows, length), bf16),
        v_r=vm((length, slot_rows), bf16),
        k_t=vm((slot_rows, length), bf16),
        q_t=vm((slot_rows, length), bf16),
        do_t=vm((slot_rows, length), bf16),
        dv_t=vm((slot_rows, length), bf16),
        bias_sum=vm((8, 4 * slot_rows), f32),
        acc=vm((5, 8, width), f32),
        stats=vm((8, width), f32),
        sums=vm((16, width), f32),
        load_sem=dma((17,)),
        probs_sem=dma((4,)),
        spread_sem=dma((2, 2, 2)),
        cross_sem=dma((2, 2, 4)),
        relay_sem=dma((2, 2, 4)),
        pair_sem=dma((2, 4)),
        cast_sem=dma((2, spans * n_tp - 1)),
    )
    if direct:
        wa, ma, va, ps, ms, vs, bu, mu, vu = smalls
        rows, cols = slot_rows // 2, width // 2
        slot = (12, rows, cols)
        wi, wb, mi, mb, vi, vb = states
        ins |= dict(
            gd_in=(fw.gd_out, ANY), cond=(fw.cond_out, VMEM), wi=(wi, ANY), wb=(wb, ANY),
            mi=(mi, ANY), mb=(mb, ANY), vi=(vi, ANY), vb=(vb, ANY), wa=(wa, VMEM), ma=(ma, VMEM), va=(va, VMEM),
            ps=(ps, VMEM), ms=(ms, VMEM), vs=(vs, VMEM), bu=(bu, VMEM), mu=(mu, VMEM), vu=(vu, VMEM),
        )
        outs |= dict(
            gsum=(arr(slot, f32), ANY),
            total=(arr(slot, bf16), VMEM),
            ada_grad=(arr(wa.shape, f32), VMEM),
            small_grad=(arr(ps.shape, f32), VMEM),
            bias_grad=(arr(bu.shape, f32), VMEM),
            ada_total=(arr(wa.shape, bf16), VMEM),
            small_total=(arr(ps.shape, f32), VMEM),
            bias_total=(arr(bu.shape, f32), VMEM),
        )
        scratch |= dict(
            shared=vm((n_tp, spans, 16, width), f32),
            sum_ring=vm((3, rows, cols), f32),
            got_a=vm((12, slot_rows, cols), bf16),
            send_b=vm(slot, bf16),
            got_b=vm(slot, bf16),
            state=vm((3, 3, rows, cols), f32),
            diff=vm(slot, bf16),
            got_p=vm(slot, bf16),
            got_h=vm((12, rows // 2, cols), bf16),
            summed=vm((16, width), f32),
            ada_rows=vm((6, 8, wa.shape[2]), f32),
            cond_rows=vm((8, 128), f32),
            ada_low=vm(wa.shape, bf16),
            ada_p=vm(wa.shape, bf16),
            ada_h=vm((wa.shape[0] // 2,) + wa.shape[1:], bf16),
            small_low=vm(ps.shape, f32),
            bias_low=vm(bu.shape, f32),
            small_all=vm((4,) + ps.shape, f32),
            bias_all=vm((4,) + bu.shape, f32),
            gd_sem=dma,
            sum_sem=dma((3,)),
            state_sem=dma((3, 3)),
            asem=dma((2, 12)),
            bsem=dma((2, 12)),
            psem=dma((2, 12)),
            hsem=dma((2, 12)),
            fsem=dma((2, 12, 3)),
            tiny_sem=dma((2, 2, 3)),
            ada_sem=dma((2, 5)),
        )
    else:
        outs |= dict(
            grads=(arr((4, slot_rows, width), bf16), VMEM),
            grads_up=(arr((4, slot_rows, width), bf16), VMEM),
            shared=(arr((n_tp, spans, 16, width), f32), VMEM),
        )
    names = list(ins) + list(outs) + list(scratch)
    results = pl.pallas_call(
        functools.partial(backward_kernel, direct, cores, n_tp, names),
        out_shape=tuple(o[0] for o in outs.values()),
        in_specs=[i[1] for i in ins.values()],
        out_specs=tuple(o[1] for o in outs.values()),
        scratch_shapes=list(scratch.values()),
        compiler_params=pltpu.CompilerParams(collective_id=1, has_side_effects=True, vmem_limit_bytes=60 * MIB),
        name="backward",
    )(*[i[0] for i in ins.values()])
    return SimpleNamespace(**dict(zip(outs, results)))


def angle_tables(length):
    half = HEAD_DIM // 2
    frequency = np.float32(10000.0) ** (np.float32(-2.0) * np.arange(half, dtype=np.float32) / np.float32(HEAD_DIM))
    angles = frequency[:, None] * np.arange(length, dtype=np.float32)[None, :]
    return jnp.asarray(np.cos(angles)), jnp.asarray(np.sin(angles))


def on_device(
    tokens, sigma_index, absorbed, cotangent, time_table,
    in_weight, back_weight, ada_weight, small_params, up_bias,
    in_first, back_first, ada_first, small_first, bias_first,
    in_second, back_second, ada_second, small_second, bias_second,
    in_moment, back_moment, ada_moment, small_moment, bias_moment,
):
    n_tp, n_dp, n_grp = lax.axis_size("tp"), lax.axis_size("dp"), lax.axis_size("grp")
    seqs, length, width = tokens.shape
    cores = n_tp // seqs
    part = in_weight.shape[2]
    heads_width = seqs * part
    direct = n_dp == 2 and n_grp == 4 and seqs == 2 and cores == 2
    t, d = lax.axis_index("tp"), lax.axis_index("dp")
    s = t // cores
    c = lax.rem(t, cores)
    groups = [[a * cores + b for a in range(seqs)] for b in range(cores)]

    wi_t = jnp.transpose(in_weight, (1, 2, 0))
    wa_t = jnp.transpose(ada_weight, (1, 0, 2))
    cosine, sine = angle_tables(length)
    if direct:
        first = (sigma_index, time_table, wa_t, small_params, up_bias, wi_t, back_weight)
    else:
        def over_tp(x, axis):
            return lax.all_gather(x, "tp", axis=axis, tiled=True, axis_index_groups=groups)

        table_ids = jnp.arange(time_table.shape[0], dtype=jnp.int32)
        onehot = (sigma_index[:, None] == table_ids[None, :]).astype(f32)
        condition = jax.nn.silu(jnp.dot(onehot, time_table, precision=highest))
        cond_low = condition.astype(bf16).astype(f32)
        wi_all = over_tp(lax.all_gather(wi_t.astype(bf16), "dp", axis=2, tiled=True), 1)
        wb_all = over_tp(lax.all_gather(back_weight.astype(bf16), "dp", axis=2, tiled=True), 1)
        weights = jnp.concatenate([wi_all[:3], wb_all[:1], wi_all[3:], wb_all[1:]], axis=0)
        bu_all = over_tp(lax.all_gather(up_bias.astype(bf16), "dp", axis=1, tiled=True)[None], 0)
        bias_row = jnp.transpose(bu_all, (1, 0, 2)).reshape(1, 4 * heads_width).astype(f32)
        small_rows = lax.all_gather(small_params.astype(bf16), "dp", axis=1, tiled=True).astype(f32)
        wa_all = lax.all_gather(ada_weight.astype(bf16), "dp", axis=0, tiled=True)
        mod_part = jnp.einsum("sc,cad->sad", cond_low.astype(bf16), wa_all, preferred_element_type=f32)
        mod_all = lax.all_gather(mod_part, "tp", axis=2, tiled=True)
        mod_rows = lax.dynamic_index_in_dim(mod_all, s, 0, keepdims=False) + small_rows[3:9]
        vecs = jnp.concatenate([small_rows[0:3], mod_rows, jnp.zeros((7, width), f32)], axis=0)
        first = (weights, vecs, bias_row)

    fw = forward(direct, cores, length, width, heads_width, first, tokens, absorbed, cotangent, cosine, sine)
    mi, vi = jnp.transpose(in_first[0], (1, 2, 0)), jnp.transpose(in_second[0], (1, 2, 0))
    mb, vb = back_first[0], back_second[0]
    am, av = jnp.transpose(ada_first[0], (1, 0, 2)), jnp.transpose(ada_second[0], (1, 0, 2))
    states = (wi_t, back_weight, mi, mb, vi, vb)
    smalls = (
        wa_t, am, av, small_params, small_first[0], small_second[0], up_bias, bias_first[0], bias_second[0])
    bw = backward(direct, cores, seqs, fw, tokens, cosine, sine, states, smalls)
    block_out = bw.block_out
    input_grad = bw.grad_out.astype(f32)
    if direct:
        gi, gbk = bw.gsum[:7], bw.gsum[7:]
        di, db = bw.total[:7].astype(f32), bw.total[7:].astype(f32)
        ada_grad, small_shard, bias_grad = bw.ada_grad, bw.small_grad, bw.bias_grad
        ada_t, small_t, bias_t = bw.ada_total.astype(f32), bw.small_total, bw.bias_total
    else:
        shared = lax.all_gather(bw.shared[:, 0], "dp", axis=1).reshape(seqs, cores, n_dp, 16, width)
        by_seq = shared.sum(axis=1)
        dmod = by_seq[:, :, 0:6]
        small_grad = jnp.concatenate([by_seq[:, :, 6:9].sum(axis=(0, 1)), dmod.sum(axis=(0, 1))], axis=0)
        bias_sum = shared[:, :, :, 9:11].sum(axis=(0, 2)).reshape(cores, 4, seqs, part)
        mine = lax.dynamic_index_in_dim(lax.dynamic_index_in_dim(bias_sum, c, 0, keepdims=False), s, 1, keepdims=False)
        bias_grad = lax.dynamic_slice_in_dim(mine, d * (part // n_dp), part // n_dp, 1)
        small_shard = lax.dynamic_slice_in_dim(small_grad, d * (width // n_dp), width // n_dp, 1)
        dmod_cols = lax.dynamic_slice_in_dim(dmod, t * part, part, 3)
        conds = jnp.transpose(lax.all_gather(cond_low, "dp", axis=0), (1, 0, 2))
        conds = lax.dynamic_slice_in_dim(conds, d * wa_t.shape[1], wa_t.shape[1], 2)
        ada_grad = jnp.sum(conds[:, :, None, :, None] * dmod_cols[:, :, :, None, :], axis=(0, 1))

        def scatter(x):
            x = lax.psum_scatter(x, "tp", scatter_dimension=1, tiled=True, axis_index_groups=groups)
            return lax.psum_scatter(x, "dp", scatter_dimension=2, tiled=True).astype(f32)

        gi = scatter(jnp.concatenate([bw.grads[1:4], bw.grads_up], axis=0))
        gbk = scatter(jnp.concatenate([bw.grads[0:1], fw.gd_out], axis=0))
    ada_m, ada_v = adam_parts(ada_grad, am, av)
    small_m, small_v = adam_parts(small_shard, small_first[0], small_second[0])
    bias_m, bias_v = adam_parts(bias_grad, bias_first[0], bias_second[0])
    in_m, in_v = adam_parts(gi, mi, vi)
    back_m, back_v = adam_parts(gbk, mb, vb)
    if not direct:
        def over_groups(weight, first_new, second_new, rate, decay):
            return lax.psum(adam_diff(weight, first_new, second_new, rate, decay).astype(bf16), "grp").astype(f32)

        di = over_groups(wi_t, in_m, in_v, rate_matrix, decay_rate)
        db = over_groups(back_weight, back_m, back_v, rate_matrix, decay_rate)
        ada_t = over_groups(wa_t, ada_m, ada_v, rate_matrix, decay_rate)
        small_t = over_groups(small_params, small_m, small_v, rate_small, 0.0)
        bias_t = over_groups(up_bias, bias_m, bias_v, rate_small, 0.0)

    def outer(weight, moment, summed):
        diff = summed / n_grp
        moment_new = outer_mu * moment + diff
        return weight - outer_rate * (diff + outer_mu * moment_new), diff, moment_new

    def back_in(x):
        return jnp.transpose(x, (2, 0, 1))

    def back_ada(x):
        return jnp.transpose(x, (1, 0, 2))

    in_w, in_diff, in_mom = (back_in(x) for x in outer(wi_t, jnp.transpose(in_moment, (1, 2, 0)), di))
    back_w, back_diff, back_mom = outer(back_weight, back_moment, db)
    ada_w, ada_diff, ada_mom = (back_ada(x) for x in outer(wa_t, jnp.transpose(ada_moment, (1, 0, 2)), ada_t))
    small_w, small_diff, small_mom = outer(small_params, small_moment, small_t)
    bias_w, bias_diff, bias_mom = outer(up_bias, bias_moment, bias_t)
    return (
        block_out, input_grad,
        back_in(in_m)[None], back_m[None], back_ada(ada_m)[None], small_m[None], bias_m[None],
        back_in(in_v)[None], back_v[None], back_ada(ada_v)[None], small_v[None], bias_v[None],
        in_w, back_w, ada_w, small_w, bias_w,
        in_diff, back_diff, ada_diff, small_diff, bias_diff,
        in_mom, back_mom, ada_mom, small_mom, bias_mom,
    )


def solution(mesh):
    rows = P(("dp", "grp"), None, None)
    shared = (
        P("dp", None, "tp"), P(None, "tp", "dp"), P("dp", None, "tp"), P(None, "dp"), P(None, ("tp", "dp")),
    )
    grouped = (
        P("grp", "dp", None, "tp"), P("grp", None, "tp", "dp"), P("grp", "dp", None, "tp"),
        P("grp", None, "dp"), P("grp", None, ("tp", "dp")),
    )
    in_specs = (rows, P(("dp", "grp")), P(("dp", "grp"), None), rows, P()) + shared + grouped + grouped + shared
    out_specs = (rows, rows) + grouped + grouped + shared + shared + shared
    return jax.shard_map(on_device, mesh=mesh, in_specs=in_specs, out_specs=out_specs, check_vma=False)
```

```python
import functools
from types import SimpleNamespace

import jax
import jax.numpy as jnp
import numpy as np
from jax import lax
from jax.experimental import pallas as pl
from jax.experimental.pallas import tpu as pltpu
from jax.sharding import PartitionSpec as P

HEAD_DIM = 64
STEP = 10
MESH = pl.DeviceIdType.MESH
ANY = pl.BlockSpec(memory_space=pl.ANY)
VMEM = pl.BlockSpec(memory_space=pltpu.VMEM)
MIB = 2**20

f32 = jnp.float32
bf16 = jnp.bfloat16
highest = lax.Precision.HIGHEST
norm_eps = 1e-05
beta_one = 0.9
beta_two = 0.999
adam_eps = 1e-08
decay_rate = 0.1
rate_matrix = 0.03
rate_small = 0.3
outer_mu = 0.9
outer_rate = 0.7
gelu_a = 0.7978845608028654
gelu_b = 0.044715


def nn(a, b):
    return lax.dot_general(a, b, (((1,), (0,)), ((), ())), preferred_element_type=f32)


def nt(a, b):
    return lax.dot_general(a, b, (((1,), (1,)), ((), ())), preferred_element_type=f32)


def tn(a, b):
    return lax.dot_general(a, b, (((0,), (0,)), ((), ())), preferred_element_type=f32)


def fold(values):
    return jnp.sum(values.reshape(values.shape[0] // 8, 8, values.shape[1]), axis=0)


def normalize(values):
    mean = jnp.mean(values, axis=-1, keepdims=True)
    centered = values - mean
    variance = jnp.mean(centered * centered, axis=-1, keepdims=True)
    inverse = lax.rsqrt(variance + norm_eps)
    return centered * inverse, inverse


def norm_pull(grad_hat, hat, inverse):
    first = jnp.mean(grad_hat, axis=-1, keepdims=True)
    second = jnp.mean(grad_hat * hat, axis=-1, keepdims=True)
    return inverse * (grad_hat - first - hat * second)


def adam_parts(gradient, first, second):
    first_new = beta_one * first + (1.0 - beta_one) * gradient
    second_new = beta_two * second + (1.0 - beta_two) * gradient * gradient
    return first_new, second_new


def adam_diff(weight, first_new, second_new, rate, decay):
    first_hat = first_new / (1.0 - beta_one**STEP)
    second_hat = second_new / (1.0 - beta_two**STEP)
    return rate * (first_hat / (jnp.sqrt(second_hat) + adam_eps) + decay * weight)


def at(start, size, unit=128):
    return pl.ds(pl.multiple_of(start, unit), size)


def remote(source, target, send, recv, device):
    return pltpu.make_async_remote_copy(
        src_ref=source, dst_ref=target, send_sem=send, recv_sem=recv, device_id=device, device_id_type=MESH)


def turn(values, cosine, sine):
    heads = values.shape[0] // HEAD_DIM
    half = HEAD_DIM // 2
    out = []
    for h in range(heads):
        low = values[h * HEAD_DIM : h * HEAD_DIM + half]
        high = values[h * HEAD_DIM + half : (h + 1) * HEAD_DIM]
        out.append(low * cosine - high * sine)
        out.append(high * cosine + low * sine)
    return jnp.concatenate(out, axis=0)


def only_head(pair, h):
    row = lax.broadcasted_iota(jnp.int32, pair.shape, 0)
    return jnp.where(row // HEAD_DIM == h, pair, jnp.zeros_like(pair))


def greet(devices):
    barrier = pltpu.get_barrier_semaphore()
    for device in devices:
        pl.semaphore_signal(barrier, inc=1, device_id=device, device_id_type=MESH)
    pl.semaphore_wait(barrier, len(devices))


def plane_devices(t, d, n_tp, spans):
    others = []
    for dt in range(n_tp):
        for dd in range(spans):
            if dt or dd:
                dev = {"tp": lax.rem(t + dt, n_tp)}
                if spans > 1:
                    dev["dp"] = lax.rem(d + dd, spans)
                others.append(dev)
    return others


def forward_kernel(direct, cores, n_tp, names, *args):
    R = SimpleNamespace(**dict(zip(names, args)))
    t, d = lax.axis_index("tp"), lax.axis_index("dp")
    s = t // cores
    c = lax.rem(t, cores)
    length, width = R.tok.shape
    half = length // cores
    slot_rows = R.weights.shape[1]
    rows, cols = slot_rows // 2, width // 2
    own, other = at(c * half, half), at((1 - c) * half, half)
    sibling = {"tp": s * cores + (1 - c)}
    xdev = {"dp": 1 - d}
    ydev = {"tp": (1 - s) * cores + c}

    tok_load = pltpu.make_async_copy(R.tok_all.at[s], R.tok, R.load_sem.at[0])
    cot_load = pltpu.make_async_copy(R.cot_all.at[s], R.cot, R.load_sem.at[1])

    if direct:
        stages = (R.attn, R.x1, R.away)

        def staged(a):
            return stages[a // 4].at[pl.ds((a % 4 // 2) * rows, rows), pl.ds((a % 2) * cols, cols)]

        weight_loads = []
        for a in range(12):
            source = R.wi.at[a] if a < 3 else R.wb.at[0] if a == 3 else R.wi.at[a - 1] if a < 8 else R.wb.at[a - 7]
            weight_loads.append(pltpu.make_async_copy(source, staged(a), R.stage_sem.at[a]))
            weight_loads[a].start()
    else:
        weight_load = pltpu.make_async_copy(R.weights_in, R.weights, R.stage_sem.at[0])
        weight_load.start()
    tok_load.start()
    cot_load.start()

    def block(a, ss, dd):
        return R.weights.at[a, at(ss * rows, rows, 16), at(dd * cols, cols)]

    def hop(kind, a):
        if kind == 0:
            ref, dev = block(a, s, d), xdev
        elif kind == 1:
            ref, dev = block(a, s, d), ydev
        elif kind == 2:
            ref, dev = block(a, s, 1 - d), ydev
        else:
            ref, dev = block(a, 1 - s, d), xdev
        k = min(kind, 2)
        return remote(ref, ref, R.wsend.at[k, a], R.wrecv.at[k, a], dev)

    ahead = 3

    def launch(a):
        hop(0, a).start()
        hop(1, a).start()

    def pass_on(a):
        @pl.when(lax.rem(a, 2) == 0)
        def _():
            hop(0, a).wait_recv()
            hop(2, a).start()

        @pl.when(lax.rem(a, 2) == 1)
        def _():
            hop(1, a).wait_recv()
            hop(3, a).start()

        @pl.when(a + ahead < 12)
        def _():
            launch(a + ahead)

    def arrived(a):
        hop(1 - a % 2, a).wait_recv()
        hop(2 + a % 2, a).wait_recv()

    if direct:
        others = plane_devices(t, d, n_tp, 2)
        R.cond[...] = jnp.zeros_like(R.cond)
        for ss in range(2):
            row = R.table[pl.ds(R.sigma[ss], 1), :]
            R.cond[ss : ss + 1, :] = (row / (1.0 + jnp.exp(-row))).astype(bf16).astype(f32)
        turned = pltpu.roll(R.cond[...], R.cond.shape[1] // 2, 1)
        R.cond_near[...] = jnp.where(d == 0, R.cond[...], turned)
        R.cond_far[...] = jnp.where(d == 1, R.cond[...], turned)
        R.ps_low[...] = R.ps[...].astype(bf16).astype(f32)
        R.bu_low[...] = R.bu[...].astype(bf16).astype(f32)
        greet(others)
        cc = remote(R.cond_far, R.cond_got, R.small_sem.at[0, 0], R.small_sem.at[1, 0], xdev)
        cc.start()
        pc = remote(R.ps_low, R.ps_all.at[d], R.small_sem.at[0, 1], R.small_sem.at[1, 1], xdev)
        pc.start()
        bcs = []
        for i, (ds, dd) in enumerate(((0, 1), (1, 0), (1, 1))):
            dev = {"tp": lax.rem(s + ds, 2) * cores + c, "dp": lax.rem(d + dd, 2)}
            bcs.append(remote(R.bu_low, R.bu_all.at[s, d], R.small_sem.at[0, 2 + i], R.small_sem.at[1, 2 + i], dev))
            bcs[i].start()

        def prepare(a):
            weight_loads[a].wait()
            R.weights[a, at(s * rows, rows, 16), at(d * cols, cols)] = staged(a)[...].astype(bf16)

        for a in range(ahead):
            prepare(a)
            launch(a)
        R.ps_all[d] = R.ps_low[...]
        R.bu_all[s, d] = R.bu_low[...]
        span = R.wa.shape[1]
        R.parts[...] = jnp.zeros_like(R.parts)

        def partial_mod(source, dd):
            lhs = source[...][:, :span].astype(bf16)
            for a in range(6):
                product = nn(lhs, R.wa[a].astype(bf16))
                for ss in range(2):
                    R.parts[dd, ss, a : a + 1, :] = product[ss : ss + 1]

        partial_mod(R.cond_near, d)
        cc.wait()
        partial_mod(R.cond_got, 1 - d)
        mods = []
        for i, dev in enumerate(others):
            mods.append(remote(
                R.parts.at[dev["dp"], dev["tp"] // cores], R.mod_got.at[t, d], R.mod_sem.at[0, i], R.mod_sem.at[1, i], dev))
            mods[i].start()
        R.mod_got[t, d] = R.parts[d, s]
        R.cond_out[d] = R.cond_near[...]
        R.cond_out[1 - d] = R.cond_got[...]
        for a in range(ahead, 12):
            prepare(a)
        pc.wait()
        for bc in bcs:
            bc.wait()
        for mc in mods:
            mc.wait()
        small_rows = jnp.concatenate([R.ps_all[0], R.ps_all[1]], axis=1)
        mod_rows = jnp.concatenate([R.mod_got[tt, 0] + R.mod_got[tt, 1] for tt in range(n_tp)], axis=1)
        R.vecs[...] = jnp.zeros_like(R.vecs)
        R.vecs[0:3] = small_rows[0:3]
        R.vecs[3:9] = mod_rows[0:6] + small_rows[3:9]
        R.bias[...] = jnp.concatenate(
            [R.bu_all[ss, dd, j : j + 1, :] for j in range(4) for ss in range(2) for dd in range(2)], axis=1)
    else:
        greet([sibling])
        R.vecs[...] = R.vecs_in[...]
        R.bias[...] = R.bias_in[...]
        R.cond_out[...] = jnp.zeros_like(R.cond_out)

    tok_load.wait()
    step = 256

    @pl.loop(0, length // step)
    def _(i):
        r = at(i * step, step)
        hat, _ = normalize(R.tok[r].astype(f32))
        hidden = hat * (R.vecs[0:1] * (1.0 + R.vecs[4:5])) + R.vecs[3:4]
        R.h1[r] = hidden.astype(bf16)

    outs = []

    def emit(source, target):
        cp = pltpu.make_async_copy(source, target, R.out_sem.at[len(outs)])
        cp.start()
        outs.append(cp)

    emit(R.h1, R.h1_out)

    if direct:
        for a in range(3):
            pass_on(a)
        for a in range(3):
            arrived(a)
    else:
        weight_load.wait()
    @pl.loop(0, length // step)
    def _(i):
        r = at(i * step, step)
        low = R.h1[r]
        cos, sin = R.cosine[:, r], R.sine[:, r]
        R.q_t[:, r] = (turn(nt(R.weights[0], low), cos, sin) * 0.125).astype(bf16)
        keys = turn(nt(R.weights[1], low), cos, sin).astype(bf16)
        R.k_t[:, r] = keys
        R.k_r[r] = keys.T
        values = nt(R.weights[2], low).astype(bf16)
        R.v_t[:, r] = values
        R.v_r[r] = values.T
        if direct:
            @pl.when(lax.rem(i, 2) == 1)
            def _():
                pass_on(3 + i // 2)

    emit(R.q_t, R.q_out)
    emit(R.k_t, R.k_out)
    emit(R.v_r, R.v_out)

    heads = R.probs.shape[0]

    @pl.loop(0, heads)
    def _(h):
        pair = at(h // 2 * 2 * HEAD_DIM, 2 * HEAD_DIM)
        one = at(h * HEAD_DIM, HEAD_DIM, HEAD_DIM)
        scores = nn(R.k_r[:, pair], only_head(R.q_t[pair, :], lax.rem(h, 2)))
        top = jnp.max(scores, axis=0, keepdims=True)
        shifted = jnp.exp(scores - top)
        inverse = 1.0 / jnp.sum(shifted, axis=0, keepdims=True)
        low = shifted.astype(bf16)
        R.probs[h] = low
        R.inv_out[h] = inverse
        R.o_t[one, :] = (nn(R.v_t[one, :], low) * inverse).astype(bf16)
        if direct:
            @pl.when(lax.rem(h, 2) == 1)
            def _():
                pass_on(5 + h // 2)

    for h in range(heads):
        emit(R.probs.at[h], R.probs_out.at[h])
    emit(R.o_t, R.o_out)

    if direct:
        arrived(3)
    emit(R.weights.at[pl.ds(0, 4)], R.weights_out.at[pl.ds(0, 4)])
    away = remote(R.away, R.got, R.pair_sem.at[0, 0], R.pair_sem.at[1, 0], sibling)
    R.away[...] = tn(R.o_t[:, other], R.weights[3])
    away.start()
    R.attn[...] = tn(R.o_t[:, own], R.weights[3])
    if direct:
        pass_on(8)
    away.wait()
    small = 128

    @pl.loop(0, half // small)
    def _(i):
        r = at(i * small, small)
        total = R.attn[r] + R.got[r]
        R.attn[r] = total
        after = R.tok[at(c * half + i * small, small)].astype(f32) + R.vecs[5:6] * total
        R.x1[r] = after
        hat, _ = normalize(after)
        hidden = hat * (R.vecs[1:2] * (1.0 + R.vecs[7:8])) + R.vecs[6:7]
        R.h2[at(c * half + i * small, small)] = hidden.astype(bf16)

    share = remote(R.h2.at[own], R.h2.at[own], R.pair_sem.at[0, 1], R.pair_sem.at[1, 1], sibling)
    share.start()
    for cp in outs:
        cp.wait()
    flags = jnp.broadcast_to(R.flags[pl.ds(s, 1), :].astype(f32), (128, length)).T
    R.column[...] = flags
    cot_load.wait()

    chunks = 2
    if direct:
        pass_on(9)
        for a in range(4, 8):
            arrived(a)
    outs.clear()
    emit(R.weights.at[pl.ds(4, 4)], R.weights_out.at[pl.ds(4, 4)])
    emit(R.attn, R.attn_out)
    emit(R.x1, R.x1_out)
    emit(R.vecs, R.vecs_out)

    def up(r):
        low = R.h2[r]
        grad = R.cot[r].astype(f32) * jnp.concatenate([R.column[r]] * (width // 128), axis=1)
        R.cot[r] = grad.astype(bf16)
        R.probs[4, r, 0:width] = (R.vecs[8:9] * grad).astype(bf16)
        for j in range(chunks):
            pair = R.weights[4 + 2 * j : 6 + 2 * j].reshape(2 * slot_rows, width)
            u = nt(low, pair) + R.bias[:, j * width : (j + 1) * width]
            square = u * u
            inner = jnp.tanh(gelu_a * (u + gelu_b * square * u))
            z = 0.5 * u * (1.0 + inner)
            slope = 0.5 * (1.0 + inner) + 0.5 * u * (1.0 - inner * inner) * gelu_a * (1.0 + 3.0 * gelu_b * square)
            R.probs[j, r, 0:width] = z.astype(bf16)
            R.probs[2 + j, r, 0:width] = slope.astype(bf16)

    @pl.loop(0, half // step)
    def _(i):
        up(at(c * half + i * step, step))

    if direct:
        pass_on(10)
    share.wait()
    emit(R.h2, R.h2_out)
    emit(R.cot.at[own], R.gy_out)

    @pl.loop(0, half // step)
    def _(i):
        up(at((1 - c) * half + i * step, step))

    for k in range(4):
        emit(R.probs.at[k, :, pl.ds(0, width)], R.hidden_out.at[k])
    emit(R.probs.at[4, :, pl.ds(0, width)], R.gm_out)
    if direct:
        pass_on(11)

    for k in range(4):
        where = pl.ds((k % 2) * slot_rows, slot_rows)
        R.gd[k] = tn(R.probs[k // 2, :, where], R.probs[4, :, 0:width]).astype(bf16)
        if k == 1 and direct:
            pass
    emit(R.gd, R.gd_out)
    if direct:
        for a in range(8, 12):
            arrived(a)
    emit(R.weights.at[pl.ds(8, 4)], R.weights_out.at[pl.ds(8, 4)])
    if direct:
        for a in range(12):
            hop(0, a).wait_send()
            hop(1, a).wait_send()
            hop(2 + a % 2, a).wait_send()
    for cp in outs:
        cp.wait()


def forward(direct, cores, length, width, slot_rows, first, tokens, flags, cotangent, cosine, sine):
    n_tp = lax.axis_size("tp")
    half = length // cores
    heads = slot_rows // HEAD_DIM
    dma = pltpu.SemaphoreType.DMA
    smem = pl.BlockSpec(memory_space=pltpu.SMEM)
    arr = jax.ShapeDtypeStruct
    vm = pltpu.VMEM
    if direct:
        ins = dict(sigma=smem, table=VMEM, wa=VMEM, ps=VMEM, bu=VMEM, wi=ANY, wb=ANY)
    else:
        ins = dict(weights_in=ANY, vecs_in=VMEM, bias_in=VMEM)
    ins |= dict(tok_all=ANY, flags=VMEM, cot_all=ANY, cosine=VMEM, sine=VMEM)
    outs = dict(
        h1_out=(arr((length, width), bf16), ANY),
        weights_out=(arr((12, slot_rows, width), bf16), ANY),
        q_out=(arr((slot_rows, length), bf16), ANY),
        k_out=(arr((slot_rows, length), bf16), ANY),
        v_out=(arr((length, slot_rows), bf16), ANY),
        probs_out=(arr((heads, length, length), bf16), ANY),
        inv_out=(arr((heads, 1, length), f32), VMEM),
        o_out=(arr((slot_rows, length), bf16), ANY),
        attn_out=(arr((half, width), f32), ANY),
        x1_out=(arr((half, width), f32), ANY),
        h2_out=(arr((length, width), bf16), ANY),
        vecs_out=(arr((16, width), f32), ANY),
        hidden_out=(arr((4, length, width), bf16), ANY),
        gm_out=(arr((length, width), bf16), ANY),
        gy_out=(arr((half, width), bf16), ANY),
        gd_out=(arr((4, slot_rows, width), bf16), ANY),
        cond_out=(arr((2, 8, 128), f32), VMEM),
    )
    scratch = dict(
        tok=vm((length, width), bf16),
        cot=vm((length, width), bf16),
        weights=vm((12, slot_rows, width), bf16),
        h1=vm((length, width), bf16),
        q_t=vm((slot_rows, length), bf16),
        k_t=vm((slot_rows, length), bf16),
        v_t=vm((slot_rows, length), bf16),
        k_r=vm((length, slot_rows), bf16),
        v_r=vm((length, slot_rows), bf16),
        probs=vm((heads, length, length), bf16),
        o_t=vm((slot_rows, length), bf16),
        away=vm((half, width), f32),
        got=vm((half, width), f32),
        attn=vm((half, width), f32),
        x1=vm((half, width), f32),
        h2=vm((length, width), bf16),
        column=vm((length, 128), f32),
        bias=vm((1, 4 * slot_rows), f32),
        vecs=vm((16, width), f32),
        gd=vm((4, slot_rows, width), bf16),
        load_sem=dma((2,)),
        stage_sem=dma((12,)),
        out_sem=dma((20,)),
        pair_sem=dma((2, 2)),
    )
    if direct:
        wa, ps, bu = first[2:5]
        scratch |= dict(
            cond=vm((8, 128), f32),
            cond_near=vm((8, 128), f32),
            cond_far=vm((8, 128), f32),
            cond_got=vm((8, 128), f32),
            ps_low=vm(ps.shape, f32),
            bu_low=vm(bu.shape, f32),
            ps_all=vm((2,) + ps.shape, f32),
            bu_all=vm((2, 2) + bu.shape, f32),
            parts=vm((2, 2, 8, wa.shape[2]), f32),
            mod_got=vm((n_tp, 2, 8, wa.shape[2]), f32),
            wsend=dma((3, 12)),
            wrecv=dma((3, 12)),
            small_sem=dma((2, 5)),
            mod_sem=dma((2, 2 * n_tp - 1)),
        )
    names = list(ins) + list(outs) + list(scratch)
    results = pl.pallas_call(
        functools.partial(forward_kernel, direct, cores, n_tp, names),
        out_shape=tuple(o[0] for o in outs.values()),
        in_specs=list(ins.values()),
        out_specs=tuple(o[1] for o in outs.values()),
        scratch_shapes=list(scratch.values()),
        compiler_params=pltpu.CompilerParams(collective_id=0, has_side_effects=True, vmem_limit_bytes=61 * MIB),
        name="forward",
    )(*first, tokens, flags, cotangent, cosine, sine)
    return SimpleNamespace(**dict(zip(outs, results)))


def backward_kernel(direct, cores, n_tp, names, *args):
    R = SimpleNamespace(**dict(zip(names, args)))
    t, g = lax.axis_index("tp"), lax.axis_index("grp")
    spans = 2 if direct else 1
    d = lax.axis_index("dp") if direct else 0
    s = t // cores
    c = lax.rem(t, cores)
    length, width = R.ga.shape
    half = length // cores
    slot_rows = R.weights.shape[1]
    rows, cols = slot_rows // 2, width // 2
    own, other = at(c * half, half), at((1 - c) * half, half)
    sibling = {"tp": s * cores + (1 - c)}
    across = {"tp": (1 - s) * cores + c}
    xdev = {"dp": 1 - d}
    heads = R.inv.shape[0]
    others = plane_devices(t, d, n_tp, spans)

    def load(source, target, i):
        cp = pltpu.make_async_copy(source, target, R.load_sem.at[i])
        cp.start()
        return cp

    def load_probs(h, slot):
        return pltpu.make_async_copy(R.probs_in.at[h], R.spare.at[slot], R.probs_sem.at[slot])

    spare = R.spare
    if direct:
        gd_load = pltpu.make_async_copy(R.gd_in, R.weights.at[pl.ds(12, 4)], R.gd_sem)
        gd_load.start()
        greet(others + [{"grp": lax.rem(g + 1 + i, 4)} for i in range(3)])
    else:
        greet(others)
    loads = [load(R.weights_in.at[pl.ds(8, 4)], R.weights.at[pl.ds(8, 4)], 0), load(R.gm_in, spare.at[4, :, pl.ds(0, width)], 1)]
    for k in (2, 3, 0, 1):
        loads.append(load(R.hidden_in.at[k], spare.at[k, :, pl.ds(0, width)], 2 + k))
    loads.append(load(R.weights_in.at[pl.ds(0, 8)], R.weights.at[pl.ds(0, 8)], 6))
    for i, (source, target) in enumerate((
        (R.x1_in, R.x1), (R.attn_in, R.attn), (R.gy_in, R.gy), (R.h2_in, R.hid), (R.o_in, R.o_t), (R.v_in, R.v_r),
        (R.k_in, R.k_t), (R.q_in, R.q_t))):
        loads.append(load(source, target, 7 + i))

    inner = jnp.logical_or(g == 1, g == 2)
    outer = jnp.logical_not(inner)
    pair = jnp.where(g == 0, 1, jnp.where(g == 1, 0, jnp.where(g == 2, 3, 2)))
    pdev = {"grp": pair}
    mdev = {"grp": 3 - g}
    mine = jnp.where(g == 1, 0, 1)
    hrows = rows // 2
    n_slots = 12
    window = 3

    pieces = 4
    size = half // pieces

    def piece(k):
        return at(c * half + k * size, size)

    def spread(kind, target):
        copies = (
            remote(R.half_out, target.at[s, own], R.spread_sem.at[0, kind, 0], R.spread_sem.at[1, kind, 0], sibling),
            pltpu.make_async_copy(R.half_out, target.at[s, own], R.spread_sem.at[0, kind, 1]),
        )
        for cp in copies:
            cp.start()
        return copies

    def cross(kind, target, k):
        source = R.half_out.at[at(k * size, size)]
        return remote(source, target.at[s, piece(k)], R.cross_sem.at[0, kind, k], R.cross_sem.at[1, kind, k], across)

    def relay(kind, target, k):
        ref = target.at[1 - s, piece(k)]
        return remote(ref, ref, R.relay_sem.at[0, kind, k], R.relay_sem.at[1, kind, k], sibling)

    def pass_piece(kind, target, k):
        cross(kind, target, k).wait_recv()
        relay(kind, target, k).start()

    def place(a):
        return jnp.where(a < 4, a + 12, jnp.where(a < 8, a + 4, a - 4))

    def order(a):
        return jnp.where(a < 4, a + 8, jnp.where(a < 8, a - 1, jnp.where(a == 8, 7, a - 9)))

    def first_hop(a):
        return remote(R.weights.at[place(a), :, at((1 - d) * cols, cols)], R.got_a.at[a], R.asem.at[0, a], R.asem.at[1, a], xdev)

    def second_hop(a):
        return remote(R.send_b.at[a], R.got_b.at[a], R.bsem.at[0, a], R.bsem.at[1, a], across)

    def state_load(a, run):
        slot = lax.rem(a, 4)
        for low, high, refs, base in (
            (0, 4, (R.wb, R.mb, R.vb), 1), (4, 8, (R.wi, R.mi, R.vi), 3), (8, 9, (R.wb, R.mb, R.vb), 0), (9, 12, (R.wi, R.mi, R.vi), 0)):
            @pl.when(jnp.logical_and(a >= low, a < high))
            def _():
                for k in range(3):
                    run(pltpu.make_async_copy(refs[k].at[a - low + base], R.state.at[slot, k], R.state_sem.at[slot, k]))

    def pair_send(a):
        return remote(R.diff.at[a], R.got_p.at[a], R.psem.at[0, a], R.psem.at[1, a], pdev)

    def h_at(k):
        return at(k * hrows, hrows, 16)

    def half_send(a):
        return remote(R.got_p.at[a, h_at(1 - mine)], R.got_h.at[a], R.hsem.at[0, a], R.hsem.at[1, a], mdev)

    def final(a, kind, dev):
        ref = R.total.at[order(a), h_at(1 - mine if kind == 2 else mine)]
        return remote(ref, ref, R.fsem.at[0, a, kind], R.fsem.at[1, a, kind], dev)

    def sum_copy(a):
        return pltpu.make_async_copy(R.sum_ring.at[lax.rem(a, 2)], R.gsum.at[order(a)], R.sum_sem.at[lax.rem(a, 2)])

    def stage_b(a):
        first_hop(a).wait_recv()

        @pl.when(a + window < n_slots)
        def _():
            first_hop(a + window).start()

        there = at((1 - s) * rows, rows, 16)
        R.send_b[a] = (R.weights[place(a), there, at(d * cols, cols)].astype(f32) + R.got_a[a, there].astype(f32)).astype(bf16)
        second_hop(a).start()
        state_load(a, lambda cp: cp.start())

    def stage_c(a):
        second_hop(a).wait_recv()
        here = at(s * rows, rows, 16)
        gradient = R.weights[place(a), here, at(d * cols, cols)].astype(f32) + R.got_a[a, here].astype(f32) + R.got_b[a].astype(f32)
        ring = lax.rem(a, 2)

        @pl.when(a >= 2)
        def _():
            sum_copy(a - 2).wait()

        R.sum_ring[ring] = gradient
        sum_copy(a).start()
        state_load(a, lambda cp: cp.wait())
        slot = lax.rem(a, 4)
        first_new, second_new = adam_parts(gradient, R.state[slot, 1], R.state[slot, 2])
        R.diff[a] = adam_diff(R.state[slot, 0], first_new, second_new, rate_matrix, decay_rate).astype(bf16)

        @pl.when(outer)
        def _():
            pair_send(a).start()

    def stage_d(a):
        pair_send(a).wait_recv()
        R.got_p[a] = (R.diff[a].astype(f32) + R.got_p[a].astype(f32)).astype(bf16)
        half_send(a).start()

    def stage_e(a):
        half_send(a).wait_recv()
        R.total[order(a), h_at(mine)] = (R.got_p[a, h_at(mine)].astype(f32) + R.got_h[a].astype(f32)).astype(bf16)
        final(a, 0, mdev).start()
        final(a, 1, pdev).start()

    def stage_f(a):
        remote(R.got_h.at[a], R.got_h.at[a], R.fsem.at[0, a, 0], R.fsem.at[1, a, 0], mdev).wait_recv()
        final(a, 2, pdev).start()

    def advance(j):
        for stage, lag, only in (
            (stage_b, 0, None), (stage_c, 3, None), (stage_d, 5, inner), (stage_e, 6, inner), (stage_f, 7, inner)):
            a = j - lag
            ok = jnp.logical_and(a >= 0, a < n_slots)

            @pl.when(ok if only is None else jnp.logical_and(ok, only))
            def _():
                stage(a)

    if direct:
        gd_load.wait()
        for a in range(window):
            first_hop(a).start()

    chunks = 2
    step = 256
    R.bias_sum[...] = jnp.zeros_like(R.bias_sum)
    for i in range(7):
        loads[i].wait()

    def down(r, target, where):
        gm = spare[4, r, 0:width]
        forward = jnp.zeros((step, width), f32)
        backward = jnp.zeros((step, width), f32)
        for j in range(chunks):
            lower = R.weights[8 + 2 * j : 10 + 2 * j].reshape(2 * slot_rows, width)
            upper = R.weights[4 + 2 * j : 6 + 2 * j].reshape(2 * slot_rows, width)
            du = (nt(gm, lower) * spare[2 + j, r, 0:width].astype(f32)).astype(bf16)
            spare[2 + j, r, 0:width] = du
            R.bias_sum[:, j * width : (j + 1) * width] += fold(du.astype(f32))
            forward += nn(spare[j, r, 0:width], lower)
            backward += nn(du, upper)
        spare[5, r, 0:width] = forward.astype(bf16)
        target[where] = backward.astype(bf16)

    @pl.loop(0, half // step)
    def _(i):
        down(at((1 - c) * half + i * step, step), R.tok, at(i * step, step))

    trades = [
        remote(spare.at[5, other, pl.ds(0, width)], R.trade.at[0], R.pair_sem.at[0, 0], R.pair_sem.at[1, 0], sibling),
        remote(R.tok, R.trade.at[1], R.pair_sem.at[0, 1], R.pair_sem.at[1, 1], sibling),
    ]
    for cp in trades:
        cp.start()

    @pl.loop(0, half // step)
    def _(i):
        down(at(c * half + i * step, step), R.half_out, at(i * step, step))

    small = 128
    R.acc[...] = jnp.zeros_like(R.acc)
    for i in range(7, 11):
        loads[i].wait()
    for cp in trades:
        cp.wait()
    loads.append(load(R.tok_all.at[s, own], R.tok, 15))

    @pl.loop(0, half // small)
    def _(i):
        r = at(i * small, small)
        g = at(c * half + i * small, small)
        after = R.x1[r]
        branch = spare[5, g, 0:width].astype(f32) + R.trade[0, r].astype(f32) + R.vecs[2:3]
        grad = R.gy[r].astype(f32)
        dh = R.half_out[r].astype(f32) + R.trade[1, r].astype(f32)
        R.half_out[r] = (after + R.vecs[8:9] * branch).astype(bf16)
        hat, inverse = normalize(after)
        total = grad + norm_pull(dh * (R.vecs[1:2] * (1.0 + R.vecs[7:8])), hat, inverse)
        R.x1[r] = total
        R.ga[g] = (R.vecs[5:6] * total).astype(bf16)
        R.acc[0] += fold(dh)
        R.acc[1] += fold(dh * hat)
        R.acc[2] += fold(total * R.attn[r])
        R.acc[3] += fold(grad * branch)
        R.acc[4] += fold(spare[4, g, 0:width].astype(f32))

    give = remote(R.ga.at[own], R.ga.at[own], R.pair_sem.at[0, 2], R.pair_sem.at[1, 2], sibling)
    give.start()
    block_copies = spread(0, R.block_out)
    cross(0, R.block_out, 0).start()
    for i in range(5):
        R.stats[i : i + 1] = jnp.sum(R.acc[i], axis=0, keepdims=True)

    for k in range(4):
        where = pl.ds((k % 2) * slot_rows, slot_rows)
        R.weights[8 + k] = tn(spare[2 + k // 2, :, where], R.hid[...]).astype(bf16)
    for h in range(4):
        load_probs(h, h).start()
    h1_load = pltpu.make_async_copy(R.h1_in, R.hid, R.load_sem.at[16])
    h1_load.start()
    if direct:
        advance(0)
        advance(1)

    for i in range(11, 16):
        loads[i].wait()
    give.wait()
    R.weights[4] = nn(R.o_t[...], R.ga[...]).astype(bf16)
    do_t = nt(R.weights[3], R.ga[...])
    for h in range(heads):
        one = pl.ds(h * HEAD_DIM, HEAD_DIM)
        R.do_t[one] = (do_t[h * HEAD_DIM : (h + 1) * HEAD_DIM] * R.inv[h]).astype(bf16)
    wide = 256

    @pl.loop(0, heads)
    def _(h):
        two = at(h // 2 * 2 * HEAD_DIM, 2 * HEAD_DIM)
        one = at(h * HEAD_DIM, HEAD_DIM, HEAD_DIM)
        slot = lax.rem(h, 4)
        load_probs(h, slot).wait()
        delta = jnp.sum(R.do_t[one].astype(f32) * R.o_t[one].astype(f32), axis=0, keepdims=True)
        for i in range(length // wide):
            q = slice(i * wide, (i + 1) * wide)
            dp = nn(R.v_r[:, two], only_head(R.do_t[two, q], lax.rem(h, 2)))
            spare[4, :, q] = (spare[slot, :, q].astype(f32) * (dp - delta[:, q])).astype(bf16)
        cos, sin = R.cosine[...], R.sine[...]
        dq = nn(R.k_t[one], spare[4]) * 0.125
        dk = nt(R.q_t[one], spare[4])
        spare[5, one] = turn(dq, cos, -sin).astype(bf16)
        spare[5, at(slot_rows + h * HEAD_DIM, HEAD_DIM, HEAD_DIM)] = turn(dk, cos, -sin).astype(bf16)
        R.dv_t[one] = nt(R.do_t[one], spare[slot]).astype(bf16)

        @pl.when(h + 4 < heads)
        def _():
            load_probs(h + 4, slot).start()

        @pl.when(h < pieces - 1)
        def _():
            cross(0, R.block_out, h + 1).start()

        if direct:
            @pl.when(jnp.logical_or(h == 2, h == 3))
            def _():
                advance(h)

    h1_load.wait()
    turned = (spare.at[5, pl.ds(0, slot_rows)], spare.at[5, pl.ds(slot_rows, slot_rows)], R.dv_t)
    for k in range(3):
        R.weights[5 + k] = nn(turned[k][...], R.hid[...]).astype(bf16)
    if direct:
        advance(4)
    for k in range(pieces):
        pass_piece(0, R.block_out, k)

    def dh1_part(r):
        total = tn(turned[0][:, r], R.weights[0])
        for k in range(1, 3):
            total += tn(turned[k][:, r], R.weights[k])
        return total

    R.trade[0] = dh1_part(other).astype(bf16)
    trade = remote(R.trade.at[0], R.trade.at[1], R.pair_sem.at[0, 3], R.pair_sem.at[1, 3], sibling)
    trade.start()
    R.attn[...] = dh1_part(own)

    R.acc[...] = jnp.zeros_like(R.acc)
    trade.wait()
    block_copies[0].wait_send()
    block_copies[1].wait()
    for k in range(pieces):
        cross(0, R.block_out, k).wait_send()

    @pl.loop(0, half // small)
    def _(i):
        r = at(i * small, small)
        dh = R.attn[r] + R.trade[1, r].astype(f32)
        hat, inverse = normalize(R.tok[r].astype(f32))
        R.acc[0] += fold(dh)
        R.acc[1] += fold(dh * hat)
        total = R.x1[r] + norm_pull(dh * (R.vecs[0:1] * (1.0 + R.vecs[4:5])), hat, inverse)
        R.half_out[r] = total.astype(bf16)

    grad_copies = spread(1, R.grad_out)
    cross(1, R.grad_out, 0).start()
    if direct:
        advance(5)
    shift1 = jnp.sum(R.acc[0], axis=0, keepdims=True)
    turn1 = jnp.sum(R.acc[1], axis=0, keepdims=True)
    R.sums[...] = jnp.zeros_like(R.sums)
    R.sums[0:1] = shift1
    R.sums[1:2] = turn1 * R.vecs[0:1]
    R.sums[2:3] = R.stats[2:3]
    R.sums[3:4] = R.stats[0:1]
    R.sums[4:5] = R.stats[1:2] * R.vecs[1:2]
    R.sums[5:6] = R.stats[3:4]
    R.sums[6:7] = turn1 * (1.0 + R.vecs[4:5])
    R.sums[7:8] = R.stats[1:2] * (1.0 + R.vecs[7:8])
    R.sums[8:9] = R.stats[4:5]
    bias_total = jnp.sum(R.bias_sum[...], axis=0, keepdims=True)
    R.sums[9:10] = bias_total[:, 0:width]
    R.sums[10:11] = bias_total[:, width : 2 * width]
    R.shared[t, d] = R.sums[...]
    casts = [
        remote(R.sums, R.shared.at[t, d], R.cast_sem.at[0, i], R.cast_sem.at[1, i], dev) for i, dev in enumerate(others)
    ]
    for cp in casts:
        cp.start()
    if direct:
        advance(6)
        advance(7)
        advance(8)
    for cp in casts:
        cp.wait()
    if direct:
        step_small(R, t, d, g, s, c, n_tp, width)
        a_rows = R.ada_low.shape[0] // 2

        def ada_at(ref, k):
            return ref.at[pl.ds(k * a_rows, a_rows)]

        tiny = []
        for i in range(3):
            dev = {"grp": lax.rem(g + 1 + i, 4)}
            tiny.append(remote(R.small_low, R.small_all.at[g], R.tiny_sem.at[0, 0, i], R.tiny_sem.at[1, 0, i], dev))
            tiny.append(remote(R.bias_low, R.bias_all.at[g], R.tiny_sem.at[0, 1, i], R.tiny_sem.at[1, 1, i], dev))
        for cp in tiny:
            cp.start()
        R.small_all[g] = R.small_low[...]
        R.bias_all[g] = R.bias_low[...]
        ada_sem = R.ada_sem
        a_pair = remote(R.ada_low, R.ada_p, ada_sem.at[0, 0], ada_sem.at[1, 0], pdev)
        a_half = remote(ada_at(R.ada_p, 1 - mine), R.ada_h, ada_sem.at[0, 1], ada_sem.at[1, 1], mdev)
        a_mid = remote(ada_at(R.ada_total, mine), ada_at(R.ada_total, mine), ada_sem.at[0, 2], ada_sem.at[1, 2], mdev)
        a_out = remote(ada_at(R.ada_total, mine), ada_at(R.ada_total, mine), ada_sem.at[0, 3], ada_sem.at[1, 3], pdev)
        a_pass = remote(ada_at(R.ada_total, 1 - mine), ada_at(R.ada_total, 1 - mine), ada_sem.at[0, 4], ada_sem.at[1, 4], pdev)

        @pl.when(outer)
        def _():
            a_pair.start()

        @pl.loop(9, n_slots + 7)
        def _(j):
            advance(j)

            @pl.when(j < 8 + pieces)
            def _():
                cross(1, R.grad_out, j - 8).start()

            @pl.when(jnp.logical_and(j >= 11, j < 11 + pieces))
            def _():
                pass_piece(1, R.grad_out, j - 11)

            @pl.when(jnp.logical_and(inner, j == 9))
            def _():
                a_pair.wait_recv()
                R.ada_p[...] = (R.ada_p[...].astype(f32) + R.ada_low[...].astype(f32)).astype(bf16)
                a_half.start()

            @pl.when(jnp.logical_and(inner, j == 10))
            def _():
                a_half.wait()
                mine_rows = pl.ds(mine * a_rows, a_rows)
                R.ada_total[mine_rows] = (R.ada_p[mine_rows].astype(f32) + R.ada_h[...].astype(f32)).astype(bf16)
                a_mid.start()
                a_out.start()

            @pl.when(jnp.logical_and(inner, j == 11))
            def _():
                a_mid.wait()
                a_pass.start()

    else:
        for k in range(1, pieces):
            cross(1, R.grad_out, k).start()
        for k in range(pieces):
            pass_piece(1, R.grad_out, k)
    if direct:
        @pl.when(outer)
        def _():
            a_pair.wait_send()
            remote(R.ada_h, R.ada_h, ada_sem.at[0, 3], ada_sem.at[1, 3], pdev).wait_recv()
            remote(R.ada_h, R.ada_h, ada_sem.at[0, 4], ada_sem.at[1, 4], pdev).wait_recv()

            @pl.loop(0, n_slots)
            def _(a):
                pair_send(a).wait_send()
                remote(R.got_h.at[a], R.got_h.at[a], R.fsem.at[0, a, 1], R.fsem.at[1, a, 1], pdev).wait_recv()
                remote(R.got_h.at[a], R.got_h.at[a], R.fsem.at[0, a, 2], R.fsem.at[1, a, 2], pdev).wait_recv()

        @pl.when(inner)
        def _():
            a_out.wait_send()
            a_pass.wait_send()

            @pl.loop(0, n_slots)
            def _(a):
                half_send(a).wait_send()
                final(a, 0, mdev).wait_send()
                final(a, 1, pdev).wait_send()
                final(a, 2, pdev).wait_send()

        for a in range(n_slots):
            first_hop(a).wait_send()
            second_hop(a).wait_send()
        for cp in tiny:
            cp.wait()
        R.small_total[...] = (R.small_all[0] + R.small_all[1]) + (R.small_all[2] + R.small_all[3])
        R.bias_total[...] = (R.bias_all[0] + R.bias_all[1]) + (R.bias_all[2] + R.bias_all[3])
        for a in range(n_slots - 2, n_slots):
            sum_copy(a).wait()
    else:
        R.grads[...] = R.weights[4:8]
        R.grads_up[...] = R.weights[8:12]
    block_copies[0].wait_recv()
    for cp in grad_copies:
        cp.wait()
    for k in range(pieces):
        cross(1, R.grad_out, k).wait_send()
        relay(0, R.block_out, k).wait()
        relay(1, R.grad_out, k).wait()


def step_small(R, t, d, g, s, c, n_tp, width):
    part = R.wa.shape[2]
    everything = R.shared[0, 0]
    for tt in range(n_tp):
        for dd in range(2):
            if tt or dd:
                everything = everything + R.shared[tt, dd]
    R.summed[...] = everything
    near = at(d * (width // 2), width // 2)
    R.small_grad[0:3] = R.summed[6:9, near]
    R.small_grad[3:9] = R.summed[0:6, near]
    first_new, second_new = adam_parts(R.small_grad[...], R.ms[...], R.vs[...])
    R.small_low[...] = adam_diff(R.ps[...], first_new, second_new, rate_small, 0.0).astype(bf16).astype(f32)

    mine = R.shared[c, 0, 8:16]
    for ss in range(2):
        for dd in range(2):
            if ss or dd:
                mine = mine + R.shared[ss * (n_tp // 2) + c, dd, 8:16]
    size = R.bu.shape[1]
    turned = pltpu.roll(mine, lax.rem(width - (s * 2 + d) * size, width), 1)
    R.bias_grad[0:1] = turned[1:2, 0:size]
    R.bias_grad[1:2] = turned[1:2, width // 2 : width // 2 + size]
    R.bias_grad[2:3] = turned[2:3, 0:size]
    R.bias_grad[3:4] = turned[2:3, width // 2 : width // 2 + size]
    first_new, second_new = adam_parts(R.bias_grad[...], R.mu[...], R.vu[...])
    R.bias_low[...] = adam_diff(R.bu[...], first_new, second_new, rate_small, 0.0).astype(bf16).astype(f32)

    R.ada_rows[...] = jnp.zeros_like(R.ada_rows)
    R.cond_rows[...] = jnp.zeros_like(R.cond_rows)
    for ss in range(2):
        for dd in range(2):
            total = R.shared[2 * ss, dd, 0:8] + R.shared[2 * ss + 1, dd, 0:8]
            turned = pltpu.roll(total, lax.rem(width - t * part, width), 1)
            k = ss * 2 + dd
            R.cond_rows[k : k + 1] = R.cond[dd, ss : ss + 1]
            for a in range(6):
                R.ada_rows[a, k : k + 1] = turned[a : a + 1, 0:part]
    lhs = R.cond_rows[...][:, : R.wa.shape[1]]
    for a in range(6):
        gradient = lax.dot_general(
            lhs, R.ada_rows[a], (((0,), (0,)), ((), ())), precision=highest, preferred_element_type=f32)
        R.ada_grad[a] = gradient
        first_new, second_new = adam_parts(gradient, R.ma[a], R.va[a])
        R.ada_low[a] = adam_diff(R.wa[a], first_new, second_new, rate_matrix, decay_rate).astype(bf16)


def backward(direct, cores, seqs, fw, tokens, cosine, sine, states, smalls):
    n_tp = lax.axis_size("tp")
    length, width = fw.h1_out.shape
    heads = fw.inv_out.shape[0]
    slot_rows = fw.weights_out.shape[1]
    half = length // cores
    dma = pltpu.SemaphoreType.DMA
    arr = jax.ShapeDtypeStruct
    vm = pltpu.VMEM
    spans = 2 if direct else 1
    ins = dict(
        weights_in=(fw.weights_out, ANY), o_in=(fw.o_out, ANY), v_in=(fw.v_out, ANY),
        k_in=(fw.k_out, ANY), q_in=(fw.q_out, ANY), probs_in=(fw.probs_out, ANY), h1_in=(fw.h1_out, ANY),
        x1_in=(fw.x1_out, ANY), attn_in=(fw.attn_out, ANY), h2_in=(fw.h2_out, ANY), hidden_in=(fw.hidden_out, ANY),
        gm_in=(fw.gm_out, ANY), gy_in=(fw.gy_out, ANY), tok_all=(tokens, ANY),
        inv=(fw.inv_out, VMEM), vecs=(fw.vecs_out, VMEM), cosine=(cosine, VMEM), sine=(sine, VMEM),
    )
    outs = dict(
        block_out=(arr((seqs, length, width), bf16), ANY),
        grad_out=(arr((seqs, length, width), bf16), ANY),
    )
    scratch = dict(
        weights=vm((16 if direct else 12, slot_rows, width), bf16),
        spare=vm((heads, length, length), bf16),
        ga=vm((length, width), bf16),
        hid=vm((length, width), bf16),
        trade=vm((2, half, width), bf16),
        x1=vm((half, width), f32),
        attn=vm((half, width), f32),
        gy=vm((half, width), bf16),
        tok=vm((half, width), bf16),
        half_out=vm((half, width), bf16),
        o_t=vm((slot_rows, length), bf16),
        v_r=vm((length, slot_rows), bf16),
        k_t=vm((slot_rows, length), bf16),
        q_t=vm((slot_rows, length), bf16),
        do_t=vm((slot_rows, length), bf16),
        dv_t=vm((slot_rows, length), bf16),
        bias_sum=vm((8, 4 * slot_rows), f32),
        acc=vm((5, 8, width), f32),
        stats=vm((8, width), f32),
        sums=vm((16, width), f32),
        load_sem=dma((17,)),
        probs_sem=dma((4,)),
        spread_sem=dma((2, 2, 2)),
        cross_sem=dma((2, 2, 4)),
        relay_sem=dma((2, 2, 4)),
        pair_sem=dma((2, 4)),
        cast_sem=dma((2, spans * n_tp - 1)),
    )
    if direct:
        wa, ma, va, ps, ms, vs, bu, mu, vu = smalls
        rows, cols = slot_rows // 2, width // 2
        slot = (12, rows, cols)
        wi, wb, mi, mb, vi, vb = states
        ins |= dict(
            gd_in=(fw.gd_out, ANY), cond=(fw.cond_out, VMEM), wi=(wi, ANY), wb=(wb, ANY),
            mi=(mi, ANY), mb=(mb, ANY), vi=(vi, ANY), vb=(vb, ANY), wa=(wa, VMEM), ma=(ma, VMEM), va=(va, VMEM),
            ps=(ps, VMEM), ms=(ms, VMEM), vs=(vs, VMEM), bu=(bu, VMEM), mu=(mu, VMEM), vu=(vu, VMEM),
        )
        outs |= dict(
            gsum=(arr(slot, f32), ANY),
            total=(arr(slot, bf16), VMEM),
            ada_grad=(arr(wa.shape, f32), VMEM),
            small_grad=(arr(ps.shape, f32), VMEM),
            bias_grad=(arr(bu.shape, f32), VMEM),
            ada_total=(arr(wa.shape, bf16), VMEM),
            small_total=(arr(ps.shape, f32), VMEM),
            bias_total=(arr(bu.shape, f32), VMEM),
        )
        scratch |= dict(
            shared=vm((n_tp, spans, 16, width), f32),
            sum_ring=vm((2, rows, cols), f32),
            got_a=vm((12, slot_rows, cols), bf16),
            send_b=vm(slot, bf16),
            got_b=vm(slot, bf16),
            state=vm((4, 3, rows, cols), f32),
            diff=vm(slot, bf16),
            got_p=vm(slot, bf16),
            got_h=vm((12, rows // 2, cols), bf16),
            summed=vm((16, width), f32),
            ada_rows=vm((6, 8, wa.shape[2]), f32),
            cond_rows=vm((8, 128), f32),
            ada_low=vm(wa.shape, bf16),
            ada_p=vm(wa.shape, bf16),
            ada_h=vm((wa.shape[0] // 2,) + wa.shape[1:], bf16),
            small_low=vm(ps.shape, f32),
            bias_low=vm(bu.shape, f32),
            small_all=vm((4,) + ps.shape, f32),
            bias_all=vm((4,) + bu.shape, f32),
            gd_sem=dma,
            sum_sem=dma((2,)),
            state_sem=dma((4, 3)),
            asem=dma((2, 12)),
            bsem=dma((2, 12)),
            psem=dma((2, 12)),
            hsem=dma((2, 12)),
            fsem=dma((2, 12, 3)),
            tiny_sem=dma((2, 2, 3)),
            ada_sem=dma((2, 5)),
        )
    else:
        outs |= dict(
            grads=(arr((4, slot_rows, width), bf16), VMEM),
            grads_up=(arr((4, slot_rows, width), bf16), VMEM),
            shared=(arr((n_tp, spans, 16, width), f32), VMEM),
        )
    names = list(ins) + list(outs) + list(scratch)
    results = pl.pallas_call(
        functools.partial(backward_kernel, direct, cores, n_tp, names),
        out_shape=tuple(o[0] for o in outs.values()),
        in_specs=[i[1] for i in ins.values()],
        out_specs=tuple(o[1] for o in outs.values()),
        scratch_shapes=list(scratch.values()),
        compiler_params=pltpu.CompilerParams(collective_id=1, has_side_effects=True, vmem_limit_bytes=61 * MIB),
        name="backward",
    )(*[i[0] for i in ins.values()])
    return SimpleNamespace(**dict(zip(outs, results)))


def angle_tables(length):
    half = HEAD_DIM // 2
    frequency = np.float32(10000.0) ** (np.float32(-2.0) * np.arange(half, dtype=np.float32) / np.float32(HEAD_DIM))
    angles = frequency[:, None] * np.arange(length, dtype=np.float32)[None, :]
    return jnp.asarray(np.cos(angles)), jnp.asarray(np.sin(angles))


def on_device(
    tokens, sigma_index, absorbed, cotangent, time_table,
    in_weight, back_weight, ada_weight, small_params, up_bias,
    in_first, back_first, ada_first, small_first, bias_first,
    in_second, back_second, ada_second, small_second, bias_second,
    in_moment, back_moment, ada_moment, small_moment, bias_moment,
):
    n_tp, n_dp, n_grp = lax.axis_size("tp"), lax.axis_size("dp"), lax.axis_size("grp")
    seqs, length, width = tokens.shape
    cores = n_tp // seqs
    part = in_weight.shape[2]
    heads_width = seqs * part
    direct = n_dp == 2 and n_grp == 4 and seqs == 2 and cores == 2
    t, d = lax.axis_index("tp"), lax.axis_index("dp")
    s = t // cores
    c = lax.rem(t, cores)
    groups = [[a * cores + b for a in range(seqs)] for b in range(cores)]

    wi_t = jnp.transpose(in_weight, (1, 2, 0))
    wa_t = jnp.transpose(ada_weight, (1, 0, 2))
    cosine, sine = angle_tables(length)
    if direct:
        first = (sigma_index, time_table, wa_t, small_params, up_bias, wi_t, back_weight)
    else:
        def over_tp(x, axis):
            return lax.all_gather(x, "tp", axis=axis, tiled=True, axis_index_groups=groups)

        table_ids = jnp.arange(time_table.shape[0], dtype=jnp.int32)
        onehot = (sigma_index[:, None] == table_ids[None, :]).astype(f32)
        condition = jax.nn.silu(jnp.dot(onehot, time_table, precision=highest))
        cond_low = condition.astype(bf16).astype(f32)
        wi_all = over_tp(lax.all_gather(wi_t.astype(bf16), "dp", axis=2, tiled=True), 1)
        wb_all = over_tp(lax.all_gather(back_weight.astype(bf16), "dp", axis=2, tiled=True), 1)
        weights = jnp.concatenate([wi_all[:3], wb_all[:1], wi_all[3:], wb_all[1:]], axis=0)
        bu_all = over_tp(lax.all_gather(up_bias.astype(bf16), "dp", axis=1, tiled=True)[None], 0)
        bias_row = jnp.transpose(bu_all, (1, 0, 2)).reshape(1, 4 * heads_width).astype(f32)
        small_rows = lax.all_gather(small_params.astype(bf16), "dp", axis=1, tiled=True).astype(f32)
        wa_all = lax.all_gather(ada_weight.astype(bf16), "dp", axis=0, tiled=True)
        mod_part = jnp.einsum("sc,cad->sad", cond_low.astype(bf16), wa_all, preferred_element_type=f32)
        mod_all = lax.all_gather(mod_part, "tp", axis=2, tiled=True)
        mod_rows = lax.dynamic_index_in_dim(mod_all, s, 0, keepdims=False) + small_rows[3:9]
        vecs = jnp.concatenate([small_rows[0:3], mod_rows, jnp.zeros((7, width), f32)], axis=0)
        first = (weights, vecs, bias_row)

    fw = forward(direct, cores, length, width, heads_width, first, tokens, absorbed, cotangent, cosine, sine)
    mi, vi = jnp.transpose(in_first[0], (1, 2, 0)), jnp.transpose(in_second[0], (1, 2, 0))
    mb, vb = back_first[0], back_second[0]
    am, av = jnp.transpose(ada_first[0], (1, 0, 2)), jnp.transpose(ada_second[0], (1, 0, 2))
    states = (wi_t, back_weight, mi, mb, vi, vb)
    smalls = (
        wa_t, am, av, small_params, small_first[0], small_second[0], up_bias, bias_first[0], bias_second[0])
    bw = backward(direct, cores, seqs, fw, tokens, cosine, sine, states, smalls)
    block_out = bw.block_out
    input_grad = bw.grad_out.astype(f32)
    if direct:
        gi, gbk = bw.gsum[:7], bw.gsum[7:]
        di, db = bw.total[:7].astype(f32), bw.total[7:].astype(f32)
        ada_grad, small_shard, bias_grad = bw.ada_grad, bw.small_grad, bw.bias_grad
        ada_t, small_t, bias_t = bw.ada_total.astype(f32), bw.small_total, bw.bias_total
    else:
        shared = lax.all_gather(bw.shared[:, 0], "dp", axis=1).reshape(seqs, cores, n_dp, 16, width)
        by_seq = shared.sum(axis=1)
        dmod = by_seq[:, :, 0:6]
        small_grad = jnp.concatenate([by_seq[:, :, 6:9].sum(axis=(0, 1)), dmod.sum(axis=(0, 1))], axis=0)
        bias_sum = shared[:, :, :, 9:11].sum(axis=(0, 2)).reshape(cores, 4, seqs, part)
        mine = lax.dynamic_index_in_dim(lax.dynamic_index_in_dim(bias_sum, c, 0, keepdims=False), s, 1, keepdims=False)
        bias_grad = lax.dynamic_slice_in_dim(mine, d * (part // n_dp), part // n_dp, 1)
        small_shard = lax.dynamic_slice_in_dim(small_grad, d * (width // n_dp), width // n_dp, 1)
        dmod_cols = lax.dynamic_slice_in_dim(dmod, t * part, part, 3)
        conds = jnp.transpose(lax.all_gather(cond_low, "dp", axis=0), (1, 0, 2))
        conds = lax.dynamic_slice_in_dim(conds, d * wa_t.shape[1], wa_t.shape[1], 2)
        ada_grad = jnp.sum(conds[:, :, None, :, None] * dmod_cols[:, :, :, None, :], axis=(0, 1))

        def scatter(x):
            x = lax.psum_scatter(x, "tp", scatter_dimension=1, tiled=True, axis_index_groups=groups)
            return lax.psum_scatter(x, "dp", scatter_dimension=2, tiled=True).astype(f32)

        gi = scatter(jnp.concatenate([bw.grads[1:4], bw.grads_up], axis=0))
        gbk = scatter(jnp.concatenate([bw.grads[0:1], fw.gd_out], axis=0))
    ada_m, ada_v = adam_parts(ada_grad, am, av)
    small_m, small_v = adam_parts(small_shard, small_first[0], small_second[0])
    bias_m, bias_v = adam_parts(bias_grad, bias_first[0], bias_second[0])
    in_m, in_v = adam_parts(gi, mi, vi)
    back_m, back_v = adam_parts(gbk, mb, vb)
    if not direct:
        def over_groups(weight, first_new, second_new, rate, decay):
            return lax.psum(adam_diff(weight, first_new, second_new, rate, decay).astype(bf16), "grp").astype(f32)

        di = over_groups(wi_t, in_m, in_v, rate_matrix, decay_rate)
        db = over_groups(back_weight, back_m, back_v, rate_matrix, decay_rate)
        ada_t = over_groups(wa_t, ada_m, ada_v, rate_matrix, decay_rate)
        small_t = over_groups(small_params, small_m, small_v, rate_small, 0.0)
        bias_t = over_groups(up_bias, bias_m, bias_v, rate_small, 0.0)

    def outer(weight, moment, summed):
        diff = summed / n_grp
        moment_new = outer_mu * moment + diff
        return weight - outer_rate * (diff + outer_mu * moment_new), diff, moment_new

    def back_in(x):
        return jnp.transpose(x, (2, 0, 1))

    def back_ada(x):
        return jnp.transpose(x, (1, 0, 2))

    in_w, in_diff, in_mom = (back_in(x) for x in outer(wi_t, jnp.transpose(in_moment, (1, 2, 0)), di))
    back_w, back_diff, back_mom = outer(back_weight, back_moment, db)
    ada_w, ada_diff, ada_mom = (back_ada(x) for x in outer(wa_t, jnp.transpose(ada_moment, (1, 0, 2)), ada_t))
    small_w, small_diff, small_mom = outer(small_params, small_moment, small_t)
    bias_w, bias_diff, bias_mom = outer(up_bias, bias_moment, bias_t)
    return (
        block_out, input_grad,
        back_in(in_m)[None], back_m[None], back_ada(ada_m)[None], small_m[None], bias_m[None],
        back_in(in_v)[None], back_v[None], back_ada(ada_v)[None], small_v[None], bias_v[None],
        in_w, back_w, ada_w, small_w, bias_w,
        in_diff, back_diff, ada_diff, small_diff, bias_diff,
        in_mom, back_mom, ada_mom, small_mom, bias_mom,
    )


def solution(mesh):
    rows = P(("dp", "grp"), None, None)
    shared = (
        P("dp", None, "tp"), P(None, "tp", "dp"), P("dp", None, "tp"), P(None, "dp"), P(None, ("tp", "dp")),
    )
    grouped = (
        P("grp", "dp", None, "tp"), P("grp", None, "tp", "dp"), P("grp", "dp", None, "tp"),
        P("grp", None, "dp"), P("grp", None, ("tp", "dp")),
    )
    in_specs = (rows, P(("dp", "grp")), P(("dp", "grp"), None), rows, P()) + shared + grouped + grouped + shared
    out_specs = (rows, rows) + grouped + grouped + shared + shared + shared
    return jax.shard_map(on_device, mesh=mesh, in_specs=in_specs, out_specs=out_specs, check_vma=False)
```

```python
import functools
from types import SimpleNamespace

import jax
import jax.numpy as jnp
import numpy as np
from jax import lax
from jax.experimental import pallas as pl
from jax.experimental.pallas import tpu as pltpu
from jax.sharding import PartitionSpec as P

HEAD_DIM = 64
STEP = 10
MESH = pl.DeviceIdType.MESH
ANY = pl.BlockSpec(memory_space=pl.ANY)
VMEM = pl.BlockSpec(memory_space=pltpu.VMEM)
MIB = 2**20

f32 = jnp.float32
bf16 = jnp.bfloat16
highest = lax.Precision.HIGHEST
norm_eps = 1e-05
beta_one = 0.9
beta_two = 0.999
adam_eps = 1e-08
decay_rate = 0.1
rate_matrix = 0.03
rate_small = 0.3
outer_mu = 0.9
outer_rate = 0.7
gelu_a = 0.7978845608028654
gelu_b = 0.044715


def nn(a, b):
    return lax.dot_general(a, b, (((1,), (0,)), ((), ())), preferred_element_type=f32)


def nt(a, b):
    return lax.dot_general(a, b, (((1,), (1,)), ((), ())), preferred_element_type=f32)


def tn(a, b):
    return lax.dot_general(a, b, (((0,), (0,)), ((), ())), preferred_element_type=f32)


def fold(values):
    return jnp.sum(values.reshape(values.shape[0] // 8, 8, values.shape[1]), axis=0)


def normalize(values):
    mean = jnp.mean(values, axis=-1, keepdims=True)
    centered = values - mean
    variance = jnp.mean(centered * centered, axis=-1, keepdims=True)
    inverse = lax.rsqrt(variance + norm_eps)
    return centered * inverse, inverse


def norm_pull(grad_hat, hat, inverse):
    first = jnp.mean(grad_hat, axis=-1, keepdims=True)
    second = jnp.mean(grad_hat * hat, axis=-1, keepdims=True)
    return inverse * (grad_hat - first - hat * second)


def adam_parts(gradient, first, second):
    first_new = beta_one * first + (1.0 - beta_one) * gradient
    second_new = beta_two * second + (1.0 - beta_two) * gradient * gradient
    return first_new, second_new


def adam_diff(weight, first_new, second_new, rate, decay):
    first_hat = first_new / (1.0 - beta_one**STEP)
    second_hat = second_new / (1.0 - beta_two**STEP)
    return rate * (first_hat / (jnp.sqrt(second_hat) + adam_eps) + decay * weight)


def at(start, size, unit=128):
    return pl.ds(pl.multiple_of(start, unit), size)


def remote(source, target, send, recv, device):
    return pltpu.make_async_remote_copy(
        src_ref=source, dst_ref=target, send_sem=send, recv_sem=recv, device_id=device, device_id_type=MESH)


def turn(values, cosine, sine):
    heads = values.shape[0] // HEAD_DIM
    half = HEAD_DIM // 2
    out = []
    for h in range(heads):
        low = values[h * HEAD_DIM : h * HEAD_DIM + half]
        high = values[h * HEAD_DIM + half : (h + 1) * HEAD_DIM]
        out.append(low * cosine - high * sine)
        out.append(high * cosine + low * sine)
    return jnp.concatenate(out, axis=0)


def only_head(pair, h):
    row = lax.broadcasted_iota(jnp.int32, pair.shape, 0)
    return jnp.where(row // HEAD_DIM == h, pair, jnp.zeros_like(pair))


def greet(devices):
    barrier = pltpu.get_barrier_semaphore()
    for device in devices:
        pl.semaphore_signal(barrier, inc=1, device_id=device, device_id_type=MESH)
    pl.semaphore_wait(barrier, len(devices))


def plane_devices(t, d, n_tp, spans):
    others = []
    for dt in range(n_tp):
        for dd in range(spans):
            if dt or dd:
                dev = {"tp": lax.rem(t + dt, n_tp)}
                if spans > 1:
                    dev["dp"] = lax.rem(d + dd, spans)
                others.append(dev)
    return others


def forward_kernel(direct, cores, n_tp, names, *args):
    R = SimpleNamespace(**dict(zip(names, args)))
    t, d = lax.axis_index("tp"), lax.axis_index("dp")
    s = t // cores
    c = lax.rem(t, cores)
    length, width = R.tok.shape
    half = length // cores
    slot_rows = R.weights.shape[1]
    rows, cols = slot_rows // 2, width // 2
    own, other = at(c * half, half), at((1 - c) * half, half)
    sibling = {"tp": s * cores + (1 - c)}
    xdev = {"dp": 1 - d}
    ydev = {"tp": (1 - s) * cores + c}

    tok_load = pltpu.make_async_copy(R.tok_all.at[s], R.tok, R.load_sem.at[0])
    cot_load = pltpu.make_async_copy(R.cot_all.at[s], R.cot, R.load_sem.at[1])

    if direct:
        stages = (R.attn, R.x1, R.away)

        def staged(a):
            return stages[a // 4].at[pl.ds((a % 4 // 2) * rows, rows), pl.ds((a % 2) * cols, cols)]

        weight_loads = []
        for a in range(12):
            source = R.wi.at[a] if a < 3 else R.wb.at[0] if a == 3 else R.wi.at[a - 1] if a < 8 else R.wb.at[a - 7]
            weight_loads.append(pltpu.make_async_copy(source, staged(a), R.stage_sem.at[a]))
            weight_loads[a].start()
    else:
        weight_load = pltpu.make_async_copy(R.weights_in, R.weights, R.stage_sem.at[0])
        weight_load.start()
    tok_load.start()
    cot_load.start()

    def block(a, ss, dd):
        return R.weights.at[a, at(ss * rows, rows, 16), at(dd * cols, cols)]

    def hop(kind, a):
        if kind == 0:
            ref, dev = block(a, s, d), xdev
        elif kind == 1:
            ref, dev = block(a, s, d), ydev
        elif kind == 2:
            ref, dev = block(a, s, 1 - d), ydev
        else:
            ref, dev = block(a, 1 - s, d), xdev
        k = min(kind, 2)
        return remote(ref, ref, R.wsend.at[k, a], R.wrecv.at[k, a], dev)

    ahead = 3

    def launch(a):
        hop(0, a).start()
        hop(1, a).start()

    def pass_on(a):
        @pl.when(lax.rem(a, 2) == 0)
        def _():
            hop(0, a).wait_recv()
            hop(2, a).start()

        @pl.when(lax.rem(a, 2) == 1)
        def _():
            hop(1, a).wait_recv()
            hop(3, a).start()

        @pl.when(a + ahead < 12)
        def _():
            launch(a + ahead)

    def arrived(a):
        hop(1 - a % 2, a).wait_recv()
        hop(2 + a % 2, a).wait_recv()

    if direct:
        others = plane_devices(t, d, n_tp, 2)
        R.cond[...] = jnp.zeros_like(R.cond)
        for ss in range(2):
            row = R.table[pl.ds(R.sigma[ss], 1), :]
            R.cond[ss : ss + 1, :] = (row / (1.0 + jnp.exp(-row))).astype(bf16).astype(f32)
        turned = pltpu.roll(R.cond[...], R.cond.shape[1] // 2, 1)
        R.cond_near[...] = jnp.where(d == 0, R.cond[...], turned)
        R.cond_far[...] = jnp.where(d == 1, R.cond[...], turned)
        R.ps_low[...] = R.ps[...].astype(bf16).astype(f32)
        R.bu_low[...] = R.bu[...].astype(bf16).astype(f32)
        greet(others)
        cc = remote(R.cond_far, R.cond_got, R.small_sem.at[0, 0], R.small_sem.at[1, 0], xdev)
        cc.start()
        pc = remote(R.ps_low, R.ps_all.at[d], R.small_sem.at[0, 1], R.small_sem.at[1, 1], xdev)
        pc.start()
        bcs = []
        for i, (ds, dd) in enumerate(((0, 1), (1, 0), (1, 1))):
            dev = {"tp": lax.rem(s + ds, 2) * cores + c, "dp": lax.rem(d + dd, 2)}
            bcs.append(remote(R.bu_low, R.bu_all.at[s, d], R.small_sem.at[0, 2 + i], R.small_sem.at[1, 2 + i], dev))
            bcs[i].start()

        def prepare(a):
            weight_loads[a].wait()
            R.weights[a, at(s * rows, rows, 16), at(d * cols, cols)] = staged(a)[...].astype(bf16)

        for a in range(ahead):
            prepare(a)
            launch(a)
        R.ps_all[d] = R.ps_low[...]
        R.bu_all[s, d] = R.bu_low[...]
        span = R.wa.shape[1]
        R.parts[...] = jnp.zeros_like(R.parts)

        def partial_mod(source, dd):
            lhs = source[...][:, :span].astype(bf16)
            for a in range(6):
                product = nn(lhs, R.wa[a].astype(bf16))
                for ss in range(2):
                    R.parts[dd, ss, a : a + 1, :] = product[ss : ss + 1]

        partial_mod(R.cond_near, d)
        cc.wait()
        partial_mod(R.cond_got, 1 - d)
        mods = []
        for i, dev in enumerate(others):
            mods.append(remote(
                R.parts.at[dev["dp"], dev["tp"] // cores], R.mod_got.at[t, d], R.mod_sem.at[0, i], R.mod_sem.at[1, i], dev))
            mods[i].start()
        R.mod_got[t, d] = R.parts[d, s]
        R.cond_out[d] = R.cond_near[...]
        R.cond_out[1 - d] = R.cond_got[...]
        for a in range(ahead, 12):
            prepare(a)
        pc.wait()
        for bc in bcs:
            bc.wait()
        for mc in mods:
            mc.wait()
        small_rows = jnp.concatenate([R.ps_all[0], R.ps_all[1]], axis=1)
        mod_rows = jnp.concatenate([R.mod_got[tt, 0] + R.mod_got[tt, 1] for tt in range(n_tp)], axis=1)
        R.vecs[...] = jnp.zeros_like(R.vecs)
        R.vecs[0:3] = small_rows[0:3]
        R.vecs[3:9] = mod_rows[0:6] + small_rows[3:9]
        R.bias[...] = jnp.concatenate(
            [R.bu_all[ss, dd, j : j + 1, :] for j in range(4) for ss in range(2) for dd in range(2)], axis=1)
    else:
        greet([sibling])
        R.vecs[...] = R.vecs_in[...]
        R.bias[...] = R.bias_in[...]
        R.cond_out[...] = jnp.zeros_like(R.cond_out)

    tok_load.wait()
    step = 256

    @pl.loop(0, length // step)
    def _(i):
        r = at(i * step, step)
        hat, _ = normalize(R.tok[r].astype(f32))
        hidden = hat * (R.vecs[0:1] * (1.0 + R.vecs[4:5])) + R.vecs[3:4]
        R.h1[r] = hidden.astype(bf16)

    outs = []

    def emit(source, target):
        cp = pltpu.make_async_copy(source, target, R.out_sem.at[len(outs)])
        cp.start()
        outs.append(cp)

    emit(R.h1, R.h1_out)

    if direct:
        for a in range(3):
            pass_on(a)
        for a in range(3):
            arrived(a)
    else:
        weight_load.wait()
    @pl.loop(0, length // step)
    def _(i):
        r = at(i * step, step)
        low = R.h1[r]
        cos, sin = R.cosine[:, r], R.sine[:, r]
        R.q_t[:, r] = (turn(nt(R.weights[0], low), cos, sin) * 0.125).astype(bf16)
        keys = turn(nt(R.weights[1], low), cos, sin).astype(bf16)
        R.k_t[:, r] = keys
        R.k_r[r] = keys.T
        values = nt(R.weights[2], low).astype(bf16)
        R.v_t[:, r] = values
        R.v_r[r] = values.T
        if direct:
            @pl.when(lax.rem(i, 2) == 1)
            def _():
                pass_on(3 + i // 2)

    emit(R.q_t, R.q_out)
    emit(R.k_t, R.k_out)
    emit(R.v_r, R.v_out)

    heads = R.probs.shape[0]

    @pl.loop(0, heads)
    def _(h):
        pair = at(h // 2 * 2 * HEAD_DIM, 2 * HEAD_DIM)
        one = at(h * HEAD_DIM, HEAD_DIM, HEAD_DIM)
        scores = nn(R.k_r[:, pair], only_head(R.q_t[pair, :], lax.rem(h, 2)))
        top = jnp.max(scores, axis=0, keepdims=True)
        shifted = jnp.exp(scores - top)
        inverse = 1.0 / jnp.sum(shifted, axis=0, keepdims=True)
        low = shifted.astype(bf16)
        R.probs[h] = low
        R.inv_out[h] = inverse
        R.o_t[one, :] = (nn(R.v_t[one, :], low) * inverse).astype(bf16)
        if direct:
            @pl.when(lax.rem(h, 2) == 1)
            def _():
                pass_on(5 + h // 2)

    for h in range(heads):
        emit(R.probs.at[h], R.probs_out.at[h])
    emit(R.o_t, R.o_out)

    if direct:
        arrived(3)
    emit(R.weights.at[pl.ds(0, 4)], R.weights_out.at[pl.ds(0, 4)])
    away = remote(R.away, R.got, R.pair_sem.at[0, 0], R.pair_sem.at[1, 0], sibling)
    R.away[...] = tn(R.o_t[:, other], R.weights[3])
    away.start()
    R.attn[...] = tn(R.o_t[:, own], R.weights[3])
    if direct:
        pass_on(8)
    away.wait()
    small = 128

    @pl.loop(0, half // small)
    def _(i):
        r = at(i * small, small)
        total = R.attn[r] + R.got[r]
        R.attn[r] = total
        after = R.tok[at(c * half + i * small, small)].astype(f32) + R.vecs[5:6] * total
        R.x1[r] = after
        hat, _ = normalize(after)
        hidden = hat * (R.vecs[1:2] * (1.0 + R.vecs[7:8])) + R.vecs[6:7]
        R.h2[at(c * half + i * small, small)] = hidden.astype(bf16)

    share = remote(R.h2.at[own], R.h2.at[own], R.pair_sem.at[0, 1], R.pair_sem.at[1, 1], sibling)
    share.start()
    for cp in outs:
        cp.wait()
    flags = jnp.broadcast_to(R.flags[pl.ds(s, 1), :].astype(f32), (128, length)).T
    R.column[...] = flags
    cot_load.wait()

    chunks = 2
    if direct:
        pass_on(9)
        for a in range(4, 8):
            arrived(a)
    outs.clear()
    emit(R.weights.at[pl.ds(4, 4)], R.weights_out.at[pl.ds(4, 4)])
    emit(R.attn, R.attn_out)
    emit(R.x1, R.x1_out)
    emit(R.vecs, R.vecs_out)

    def up(r):
        low = R.h2[r]
        grad = R.cot[r].astype(f32) * jnp.concatenate([R.column[r]] * (width // 128), axis=1)
        R.cot[r] = grad.astype(bf16)
        R.probs[4, r, 0:width] = (R.vecs[8:9] * grad).astype(bf16)
        for j in range(chunks):
            pair = R.weights[4 + 2 * j : 6 + 2 * j].reshape(2 * slot_rows, width)
            u = nt(low, pair) + R.bias[:, j * width : (j + 1) * width]
            square = u * u
            inner = jnp.tanh(gelu_a * (u + gelu_b * square * u))
            z = 0.5 * u * (1.0 + inner)
            slope = 0.5 * (1.0 + inner) + 0.5 * u * (1.0 - inner * inner) * gelu_a * (1.0 + 3.0 * gelu_b * square)
            R.probs[j, r, 0:width] = z.astype(bf16)
            R.probs[2 + j, r, 0:width] = slope.astype(bf16)

    @pl.loop(0, half // step)
    def _(i):
        up(at(c * half + i * step, step))

    if direct:
        pass_on(10)
    share.wait()
    emit(R.h2, R.h2_out)
    emit(R.cot.at[own], R.gy_out)

    @pl.loop(0, half // step)
    def _(i):
        up(at((1 - c) * half + i * step, step))

    for k in range(4):
        emit(R.probs.at[k, :, pl.ds(0, width)], R.hidden_out.at[k])
    emit(R.probs.at[4, :, pl.ds(0, width)], R.gm_out)
    if direct:
        pass_on(11)

    for k in range(4):
        where = pl.ds((k % 2) * slot_rows, slot_rows)
        R.gd[k] = tn(R.probs[k // 2, :, where], R.probs[4, :, 0:width]).astype(bf16)
        if k == 1 and direct:
            pass
    emit(R.gd, R.gd_out)
    if direct:
        for a in range(8, 12):
            arrived(a)
    emit(R.weights.at[pl.ds(8, 4)], R.weights_out.at[pl.ds(8, 4)])
    if direct:
        for a in range(12):
            hop(0, a).wait_send()
            hop(1, a).wait_send()
            hop(2 + a % 2, a).wait_send()
    for cp in outs:
        cp.wait()


def forward(direct, cores, length, width, slot_rows, first, tokens, flags, cotangent, cosine, sine):
    n_tp = lax.axis_size("tp")
    half = length // cores
    heads = slot_rows // HEAD_DIM
    dma = pltpu.SemaphoreType.DMA
    smem = pl.BlockSpec(memory_space=pltpu.SMEM)
    arr = jax.ShapeDtypeStruct
    vm = pltpu.VMEM
    if direct:
        ins = dict(sigma=smem, table=VMEM, wa=VMEM, ps=VMEM, bu=VMEM, wi=ANY, wb=ANY)
    else:
        ins = dict(weights_in=ANY, vecs_in=VMEM, bias_in=VMEM)
    ins |= dict(tok_all=ANY, flags=VMEM, cot_all=ANY, cosine=VMEM, sine=VMEM)
    outs = dict(
        h1_out=(arr((length, width), bf16), ANY),
        weights_out=(arr((12, slot_rows, width), bf16), ANY),
        q_out=(arr((slot_rows, length), bf16), ANY),
        k_out=(arr((slot_rows, length), bf16), ANY),
        v_out=(arr((length, slot_rows), bf16), ANY),
        probs_out=(arr((heads, length, length), bf16), ANY),
        inv_out=(arr((heads, 1, length), f32), VMEM),
        o_out=(arr((slot_rows, length), bf16), ANY),
        attn_out=(arr((half, width), f32), ANY),
        x1_out=(arr((half, width), f32), ANY),
        h2_out=(arr((length, width), bf16), ANY),
        vecs_out=(arr((16, width), f32), ANY),
        hidden_out=(arr((4, length, width), bf16), ANY),
        gm_out=(arr((length, width), bf16), ANY),
        gy_out=(arr((half, width), bf16), ANY),
        gd_out=(arr((4, slot_rows, width), bf16), ANY),
        cond_out=(arr((2, 8, 128), f32), VMEM),
    )
    scratch = dict(
        tok=vm((length, width), bf16),
        cot=vm((length, width), bf16),
        weights=vm((12, slot_rows, width), bf16),
        h1=vm((length, width), bf16),
        q_t=vm((slot_rows, length), bf16),
        k_t=vm((slot_rows, length), bf16),
        v_t=vm((slot_rows, length), bf16),
        k_r=vm((length, slot_rows), bf16),
        v_r=vm((length, slot_rows), bf16),
        probs=vm((heads, length, length), bf16),
        o_t=vm((slot_rows, length), bf16),
        away=vm((half, width), f32),
        got=vm((half, width), f32),
        attn=vm((half, width), f32),
        x1=vm((half, width), f32),
        h2=vm((length, width), bf16),
        column=vm((length, 128), f32),
        bias=vm((1, 4 * slot_rows), f32),
        vecs=vm((16, width), f32),
        gd=vm((4, slot_rows, width), bf16),
        load_sem=dma((2,)),
        stage_sem=dma((12,)),
        out_sem=dma((20,)),
        pair_sem=dma((2, 2)),
    )
    if direct:
        wa, ps, bu = first[2:5]
        scratch |= dict(
            cond=vm((8, 128), f32),
            cond_near=vm((8, 128), f32),
            cond_far=vm((8, 128), f32),
            cond_got=vm((8, 128), f32),
            ps_low=vm(ps.shape, f32),
            bu_low=vm(bu.shape, f32),
            ps_all=vm((2,) + ps.shape, f32),
            bu_all=vm((2, 2) + bu.shape, f32),
            parts=vm((2, 2, 8, wa.shape[2]), f32),
            mod_got=vm((n_tp, 2, 8, wa.shape[2]), f32),
            wsend=dma((3, 12)),
            wrecv=dma((3, 12)),
            small_sem=dma((2, 5)),
            mod_sem=dma((2, 2 * n_tp - 1)),
        )
    names = list(ins) + list(outs) + list(scratch)
    results = pl.pallas_call(
        functools.partial(forward_kernel, direct, cores, n_tp, names),
        out_shape=tuple(o[0] for o in outs.values()),
        in_specs=list(ins.values()),
        out_specs=tuple(o[1] for o in outs.values()),
        scratch_shapes=list(scratch.values()),
        compiler_params=pltpu.CompilerParams(collective_id=0, has_side_effects=True, vmem_limit_bytes=61 * MIB),
        name="forward",
    )(*first, tokens, flags, cotangent, cosine, sine)
    return SimpleNamespace(**dict(zip(outs, results)))


def backward_kernel(direct, cores, n_tp, names, *args):
    R = SimpleNamespace(**dict(zip(names, args)))
    t, g = lax.axis_index("tp"), lax.axis_index("grp")
    spans = 2 if direct else 1
    d = lax.axis_index("dp") if direct else 0
    s = t // cores
    c = lax.rem(t, cores)
    length, width = R.ga.shape
    half = length // cores
    slot_rows = R.weights.shape[1]
    rows, cols = slot_rows // 2, width // 2
    own, other = at(c * half, half), at((1 - c) * half, half)
    sibling = {"tp": s * cores + (1 - c)}
    across = {"tp": (1 - s) * cores + c}
    xdev = {"dp": 1 - d}
    heads = R.inv.shape[0]
    others = plane_devices(t, d, n_tp, spans)

    def load(source, target, i):
        cp = pltpu.make_async_copy(source, target, R.load_sem.at[i])
        cp.start()
        return cp

    def load_probs(h, slot):
        return pltpu.make_async_copy(R.probs_in.at[h], R.spare.at[slot], R.probs_sem.at[slot])

    spare = R.spare
    if direct:
        gd_load = pltpu.make_async_copy(R.gd_in, R.weights.at[pl.ds(12, 4)], R.gd_sem)
        gd_load.start()
        greet(others + [{"grp": lax.rem(g + 1 + i, 4)} for i in range(3)])
    else:
        greet(others)
    loads = [load(R.weights_in.at[pl.ds(8, 4)], R.weights.at[pl.ds(8, 4)], 0), load(R.gm_in, spare.at[4, :, pl.ds(0, width)], 1)]
    for k in (2, 3, 0, 1):
        loads.append(load(R.hidden_in.at[k], spare.at[k, :, pl.ds(0, width)], 2 + k))
    loads.append(load(R.weights_in.at[pl.ds(0, 8)], R.weights.at[pl.ds(0, 8)], 6))
    for i, (source, target) in enumerate((
        (R.x1_in, R.x1), (R.attn_in, R.attn), (R.gy_in, R.gy), (R.h2_in, R.hid), (R.o_in, R.o_t), (R.v_in, R.v_r),
        (R.k_in, R.k_t), (R.q_in, R.q_t))):
        loads.append(load(source, target, 7 + i))

    inner = jnp.logical_or(g == 1, g == 2)
    outer = jnp.logical_not(inner)
    pair = jnp.where(g == 0, 1, jnp.where(g == 1, 0, jnp.where(g == 2, 3, 2)))
    pdev = {"grp": pair}
    mdev = {"grp": 3 - g}
    mine = jnp.where(g == 1, 0, 1)
    hrows = rows // 2
    n_slots = 12
    window = 3

    pieces = 4
    size = half // pieces

    def piece(k):
        return at(c * half + k * size, size)

    def spread(kind, target):
        copies = (
            remote(R.half_out, target.at[s, own], R.spread_sem.at[0, kind, 0], R.spread_sem.at[1, kind, 0], sibling),
            pltpu.make_async_copy(R.half_out, target.at[s, own], R.spread_sem.at[0, kind, 1]),
        )
        for cp in copies:
            cp.start()
        return copies

    def cross(kind, target, k):
        source = R.half_out.at[at(k * size, size)]
        return remote(source, target.at[s, piece(k)], R.cross_sem.at[0, kind, k], R.cross_sem.at[1, kind, k], across)

    def relay(kind, target, k):
        ref = target.at[1 - s, piece(k)]
        return remote(ref, ref, R.relay_sem.at[0, kind, k], R.relay_sem.at[1, kind, k], sibling)

    def pass_piece(kind, target, k):
        cross(kind, target, k).wait_recv()
        relay(kind, target, k).start()

    def place(a):
        return jnp.where(a < 4, a + 12, jnp.where(a < 8, a + 4, a - 4))

    def order(a):
        return jnp.where(a < 4, a + 8, jnp.where(a < 8, a - 1, jnp.where(a == 8, 7, a - 9)))

    def first_hop(a):
        return remote(R.weights.at[place(a), :, at((1 - d) * cols, cols)], R.got_a.at[a], R.asem.at[0, a], R.asem.at[1, a], xdev)

    def second_hop(a):
        return remote(R.send_b.at[a], R.got_b.at[a], R.bsem.at[0, a], R.bsem.at[1, a], across)

    def state_load(a, run):
        slot = lax.rem(a, 4)
        for low, high, refs, base in (
            (0, 4, (R.wb, R.mb, R.vb), 1), (4, 8, (R.wi, R.mi, R.vi), 3), (8, 9, (R.wb, R.mb, R.vb), 0), (9, 12, (R.wi, R.mi, R.vi), 0)):
            @pl.when(jnp.logical_and(a >= low, a < high))
            def _():
                for k in range(3):
                    run(pltpu.make_async_copy(refs[k].at[a - low + base], R.state.at[slot, k], R.state_sem.at[slot, k]))

    def pair_send(a):
        return remote(R.diff.at[a], R.got_p.at[a], R.psem.at[0, a], R.psem.at[1, a], pdev)

    def h_at(k):
        return at(k * hrows, hrows, 16)

    def half_send(a):
        return remote(R.got_p.at[a, h_at(1 - mine)], R.got_h.at[a], R.hsem.at[0, a], R.hsem.at[1, a], mdev)

    def final(a, kind, dev):
        ref = R.total.at[order(a), h_at(1 - mine if kind == 2 else mine)]
        return remote(ref, ref, R.fsem.at[0, a, kind], R.fsem.at[1, a, kind], dev)

    def sum_copy(a):
        return pltpu.make_async_copy(R.sum_ring.at[lax.rem(a, 2)], R.gsum.at[order(a)], R.sum_sem.at[lax.rem(a, 2)])

    def stage_b(a):
        first_hop(a).wait_recv()

        @pl.when(a + window < n_slots)
        def _():
            first_hop(a + window).start()

        there = at((1 - s) * rows, rows, 16)
        R.send_b[a] = (R.weights[place(a), there, at(d * cols, cols)].astype(f32) + R.got_a[a, there].astype(f32)).astype(bf16)
        second_hop(a).start()
        state_load(a, lambda cp: cp.start())

    def stage_c(a):
        second_hop(a).wait_recv()
        here = at(s * rows, rows, 16)
        gradient = R.weights[place(a), here, at(d * cols, cols)].astype(f32) + R.got_a[a, here].astype(f32) + R.got_b[a].astype(f32)
        ring = lax.rem(a, 2)

        @pl.when(a >= 2)
        def _():
            sum_copy(a - 2).wait()

        R.sum_ring[ring] = gradient
        sum_copy(a).start()
        state_load(a, lambda cp: cp.wait())
        slot = lax.rem(a, 4)
        first_new, second_new = adam_parts(gradient, R.state[slot, 1], R.state[slot, 2])
        R.diff[a] = adam_diff(R.state[slot, 0], first_new, second_new, rate_matrix, decay_rate).astype(bf16)

        @pl.when(outer)
        def _():
            pair_send(a).start()

    def stage_d(a):
        pair_send(a).wait_recv()
        R.got_p[a] = (R.diff[a].astype(f32) + R.got_p[a].astype(f32)).astype(bf16)
        half_send(a).start()

    def stage_e(a):
        half_send(a).wait_recv()
        R.total[order(a), h_at(mine)] = (R.got_p[a, h_at(mine)].astype(f32) + R.got_h[a].astype(f32)).astype(bf16)
        final(a, 0, mdev).start()
        final(a, 1, pdev).start()

    def stage_f(a):
        remote(R.got_h.at[a], R.got_h.at[a], R.fsem.at[0, a, 0], R.fsem.at[1, a, 0], mdev).wait_recv()
        final(a, 2, pdev).start()

    def advance(j):
        for stage, lag, only in (
            (stage_b, 0, None), (stage_c, 3, None), (stage_d, 4, inner), (stage_e, 5, inner), (stage_f, 6, inner)):
            a = j - lag
            ok = jnp.logical_and(a >= 0, a < n_slots)

            @pl.when(ok if only is None else jnp.logical_and(ok, only))
            def _():
                stage(a)

    if direct:
        gd_load.wait()
        for a in range(window):
            first_hop(a).start()

    chunks = 2
    step = 256
    R.bias_sum[...] = jnp.zeros_like(R.bias_sum)
    for i in range(7):
        loads[i].wait()

    def down(r, target, where):
        gm = spare[4, r, 0:width]
        forward = jnp.zeros((step, width), f32)
        backward = jnp.zeros((step, width), f32)
        for j in range(chunks):
            lower = R.weights[8 + 2 * j : 10 + 2 * j].reshape(2 * slot_rows, width)
            upper = R.weights[4 + 2 * j : 6 + 2 * j].reshape(2 * slot_rows, width)
            du = (nt(gm, lower) * spare[2 + j, r, 0:width].astype(f32)).astype(bf16)
            spare[2 + j, r, 0:width] = du
            R.bias_sum[:, j * width : (j + 1) * width] += fold(du.astype(f32))
            forward += nn(spare[j, r, 0:width], lower)
            backward += nn(du, upper)
        spare[5, r, 0:width] = forward.astype(bf16)
        target[where] = backward.astype(bf16)

    @pl.loop(0, half // step)
    def _(i):
        down(at((1 - c) * half + i * step, step), R.tok, at(i * step, step))

    trades = [
        remote(spare.at[5, other, pl.ds(0, width)], R.trade.at[0], R.pair_sem.at[0, 0], R.pair_sem.at[1, 0], sibling),
        remote(R.tok, R.trade.at[1], R.pair_sem.at[0, 1], R.pair_sem.at[1, 1], sibling),
    ]
    for cp in trades:
        cp.start()

    @pl.loop(0, half // step)
    def _(i):
        down(at(c * half + i * step, step), R.half_out, at(i * step, step))

    small = 128
    R.acc[...] = jnp.zeros_like(R.acc)
    for i in range(7, 11):
        loads[i].wait()
    for cp in trades:
        cp.wait()
    loads.append(load(R.tok_all.at[s, own], R.tok, 15))

    @pl.loop(0, half // small)
    def _(i):
        r = at(i * small, small)
        g = at(c * half + i * small, small)
        after = R.x1[r]
        branch = spare[5, g, 0:width].astype(f32) + R.trade[0, r].astype(f32) + R.vecs[2:3]
        grad = R.gy[r].astype(f32)
        dh = R.half_out[r].astype(f32) + R.trade[1, r].astype(f32)
        R.half_out[r] = (after + R.vecs[8:9] * branch).astype(bf16)
        hat, inverse = normalize(after)
        total = grad + norm_pull(dh * (R.vecs[1:2] * (1.0 + R.vecs[7:8])), hat, inverse)
        R.x1[r] = total
        R.ga[g] = (R.vecs[5:6] * total).astype(bf16)
        R.acc[0] += fold(dh)
        R.acc[1] += fold(dh * hat)
        R.acc[2] += fold(total * R.attn[r])
        R.acc[3] += fold(grad * branch)
        R.acc[4] += fold(spare[4, g, 0:width].astype(f32))

    give = remote(R.ga.at[own], R.ga.at[own], R.pair_sem.at[0, 2], R.pair_sem.at[1, 2], sibling)
    give.start()
    block_copies = spread(0, R.block_out)
    cross(0, R.block_out, 0).start()
    for i in range(5):
        R.stats[i : i + 1] = jnp.sum(R.acc[i], axis=0, keepdims=True)

    for k in range(4):
        where = pl.ds((k % 2) * slot_rows, slot_rows)
        R.weights[8 + k] = tn(spare[2 + k // 2, :, where], R.hid[...]).astype(bf16)
    for h in range(4):
        load_probs(h, h).start()
    h1_load = pltpu.make_async_copy(R.h1_in, R.hid, R.load_sem.at[16])
    h1_load.start()
    if direct:
        advance(0)
        advance(1)

    for i in range(11, 16):
        loads[i].wait()
    give.wait()
    R.weights[4] = nn(R.o_t[...], R.ga[...]).astype(bf16)
    do_t = nt(R.weights[3], R.ga[...])
    for h in range(heads):
        one = pl.ds(h * HEAD_DIM, HEAD_DIM)
        R.do_t[one] = (do_t[h * HEAD_DIM : (h + 1) * HEAD_DIM] * R.inv[h]).astype(bf16)
    wide = 256

    @pl.loop(0, heads)
    def _(h):
        two = at(h // 2 * 2 * HEAD_DIM, 2 * HEAD_DIM)
        one = at(h * HEAD_DIM, HEAD_DIM, HEAD_DIM)
        slot = lax.rem(h, 4)
        load_probs(h, slot).wait()
        delta = jnp.sum(R.do_t[one].astype(f32) * R.o_t[one].astype(f32), axis=0, keepdims=True)
        for i in range(length // wide):
            q = slice(i * wide, (i + 1) * wide)
            dp = nn(R.v_r[:, two], only_head(R.do_t[two, q], lax.rem(h, 2)))
            spare[4, :, q] = (spare[slot, :, q].astype(f32) * (dp - delta[:, q])).astype(bf16)
        cos, sin = R.cosine[...], R.sine[...]
        dq = nn(R.k_t[one], spare[4]) * 0.125
        dk = nt(R.q_t[one], spare[4])
        spare[5, one] = turn(dq, cos, -sin).astype(bf16)
        spare[5, at(slot_rows + h * HEAD_DIM, HEAD_DIM, HEAD_DIM)] = turn(dk, cos, -sin).astype(bf16)
        R.dv_t[one] = nt(R.do_t[one], spare[slot]).astype(bf16)

        @pl.when(h + 4 < heads)
        def _():
            load_probs(h + 4, slot).start()

        @pl.when(h < pieces - 1)
        def _():
            cross(0, R.block_out, h + 1).start()

        if direct:
            @pl.when(jnp.logical_or(h == 2, h == 3))
            def _():
                advance(h)

    h1_load.wait()
    turned = (spare.at[5, pl.ds(0, slot_rows)], spare.at[5, pl.ds(slot_rows, slot_rows)], R.dv_t)
    for k in range(3):
        R.weights[5 + k] = nn(turned[k][...], R.hid[...]).astype(bf16)
    if direct:
        advance(4)
    for k in range(pieces):
        pass_piece(0, R.block_out, k)

    def dh1_part(r):
        total = tn(turned[0][:, r], R.weights[0])
        for k in range(1, 3):
            total += tn(turned[k][:, r], R.weights[k])
        return total

    R.trade[0] = dh1_part(other).astype(bf16)
    trade = remote(R.trade.at[0], R.trade.at[1], R.pair_sem.at[0, 3], R.pair_sem.at[1, 3], sibling)
    trade.start()
    R.attn[...] = dh1_part(own)

    R.acc[...] = jnp.zeros_like(R.acc)
    trade.wait()
    block_copies[0].wait_send()
    block_copies[1].wait()
    for k in range(pieces):
        cross(0, R.block_out, k).wait_send()

    @pl.loop(0, half // small)
    def _(i):
        r = at(i * small, small)
        dh = R.attn[r] + R.trade[1, r].astype(f32)
        hat, inverse = normalize(R.tok[r].astype(f32))
        R.acc[0] += fold(dh)
        R.acc[1] += fold(dh * hat)
        total = R.x1[r] + norm_pull(dh * (R.vecs[0:1] * (1.0 + R.vecs[4:5])), hat, inverse)
        R.half_out[r] = total.astype(bf16)

    grad_copies = spread(1, R.grad_out)
    cross(1, R.grad_out, 0).start()
    if direct:
        advance(5)
    shift1 = jnp.sum(R.acc[0], axis=0, keepdims=True)
    turn1 = jnp.sum(R.acc[1], axis=0, keepdims=True)
    R.sums[...] = jnp.zeros_like(R.sums)
    R.sums[0:1] = shift1
    R.sums[1:2] = turn1 * R.vecs[0:1]
    R.sums[2:3] = R.stats[2:3]
    R.sums[3:4] = R.stats[0:1]
    R.sums[4:5] = R.stats[1:2] * R.vecs[1:2]
    R.sums[5:6] = R.stats[3:4]
    R.sums[6:7] = turn1 * (1.0 + R.vecs[4:5])
    R.sums[7:8] = R.stats[1:2] * (1.0 + R.vecs[7:8])
    R.sums[8:9] = R.stats[4:5]
    bias_total = jnp.sum(R.bias_sum[...], axis=0, keepdims=True)
    R.sums[9:10] = bias_total[:, 0:width]
    R.sums[10:11] = bias_total[:, width : 2 * width]
    R.shared[t, d] = R.sums[...]
    casts = [
        remote(R.sums, R.shared.at[t, d], R.cast_sem.at[0, i], R.cast_sem.at[1, i], dev) for i, dev in enumerate(others)
    ]
    for cp in casts:
        cp.start()
    if direct:
        advance(6)
        advance(7)
        advance(8)
    for cp in casts:
        cp.wait()
    if direct:
        step_small(R, t, d, g, s, c, n_tp, width)
        a_rows = R.ada_low.shape[0] // 2

        def ada_at(ref, k):
            return ref.at[pl.ds(k * a_rows, a_rows)]

        tiny = []
        for i in range(3):
            dev = {"grp": lax.rem(g + 1 + i, 4)}
            tiny.append(remote(R.small_low, R.small_all.at[g], R.tiny_sem.at[0, 0, i], R.tiny_sem.at[1, 0, i], dev))
            tiny.append(remote(R.bias_low, R.bias_all.at[g], R.tiny_sem.at[0, 1, i], R.tiny_sem.at[1, 1, i], dev))
        for cp in tiny:
            cp.start()
        R.small_all[g] = R.small_low[...]
        R.bias_all[g] = R.bias_low[...]
        ada_sem = R.ada_sem
        a_pair = remote(R.ada_low, R.ada_p, ada_sem.at[0, 0], ada_sem.at[1, 0], pdev)
        a_half = remote(ada_at(R.ada_p, 1 - mine), R.ada_h, ada_sem.at[0, 1], ada_sem.at[1, 1], mdev)
        a_mid = remote(ada_at(R.ada_total, mine), ada_at(R.ada_total, mine), ada_sem.at[0, 2], ada_sem.at[1, 2], mdev)
        a_out = remote(ada_at(R.ada_total, mine), ada_at(R.ada_total, mine), ada_sem.at[0, 3], ada_sem.at[1, 3], pdev)
        a_pass = remote(ada_at(R.ada_total, 1 - mine), ada_at(R.ada_total, 1 - mine), ada_sem.at[0, 4], ada_sem.at[1, 4], pdev)

        @pl.when(outer)
        def _():
            a_pair.start()

        @pl.loop(9, n_slots + 6)
        def _(j):
            advance(j)

            @pl.when(j < 8 + pieces)
            def _():
                cross(1, R.grad_out, j - 8).start()

            @pl.when(jnp.logical_and(j >= 11, j < 11 + pieces))
            def _():
                pass_piece(1, R.grad_out, j - 11)

            @pl.when(jnp.logical_and(inner, j == 9))
            def _():
                a_pair.wait_recv()
                R.ada_p[...] = (R.ada_p[...].astype(f32) + R.ada_low[...].astype(f32)).astype(bf16)
                a_half.start()

            @pl.when(jnp.logical_and(inner, j == 10))
            def _():
                a_half.wait()
                mine_rows = pl.ds(mine * a_rows, a_rows)
                R.ada_total[mine_rows] = (R.ada_p[mine_rows].astype(f32) + R.ada_h[...].astype(f32)).astype(bf16)
                a_mid.start()
                a_out.start()

            @pl.when(jnp.logical_and(inner, j == 11))
            def _():
                a_mid.wait()
                a_pass.start()

    else:
        for k in range(1, pieces):
            cross(1, R.grad_out, k).start()
        for k in range(pieces):
            pass_piece(1, R.grad_out, k)
    if direct:
        @pl.when(outer)
        def _():
            a_pair.wait_send()
            remote(R.ada_h, R.ada_h, ada_sem.at[0, 3], ada_sem.at[1, 3], pdev).wait_recv()
            remote(R.ada_h, R.ada_h, ada_sem.at[0, 4], ada_sem.at[1, 4], pdev).wait_recv()

            @pl.loop(0, n_slots)
            def _(a):
                pair_send(a).wait_send()
                remote(R.got_h.at[a], R.got_h.at[a], R.fsem.at[0, a, 1], R.fsem.at[1, a, 1], pdev).wait_recv()
                remote(R.got_h.at[a], R.got_h.at[a], R.fsem.at[0, a, 2], R.fsem.at[1, a, 2], pdev).wait_recv()

        @pl.when(inner)
        def _():
            a_out.wait_send()
            a_pass.wait_send()

            @pl.loop(0, n_slots)
            def _(a):
                half_send(a).wait_send()
                final(a, 0, mdev).wait_send()
                final(a, 1, pdev).wait_send()
                final(a, 2, pdev).wait_send()

        for a in range(n_slots):
            first_hop(a).wait_send()
            second_hop(a).wait_send()
        for cp in tiny:
            cp.wait()
        R.small_total[...] = (R.small_all[0] + R.small_all[1]) + (R.small_all[2] + R.small_all[3])
        R.bias_total[...] = (R.bias_all[0] + R.bias_all[1]) + (R.bias_all[2] + R.bias_all[3])
        for a in range(n_slots - 2, n_slots):
            sum_copy(a).wait()
    else:
        R.grads[...] = R.weights[4:8]
        R.grads_up[...] = R.weights[8:12]
    block_copies[0].wait_recv()
    for cp in grad_copies:
        cp.wait()
    for k in range(pieces):
        cross(1, R.grad_out, k).wait_send()
        relay(0, R.block_out, k).wait()
        relay(1, R.grad_out, k).wait()


def step_small(R, t, d, g, s, c, n_tp, width):
    part = R.wa.shape[2]
    everything = R.shared[0, 0]
    for tt in range(n_tp):
        for dd in range(2):
            if tt or dd:
                everything = everything + R.shared[tt, dd]
    R.summed[...] = everything
    near = at(d * (width // 2), width // 2)
    R.small_grad[0:3] = R.summed[6:9, near]
    R.small_grad[3:9] = R.summed[0:6, near]
    first_new, second_new = adam_parts(R.small_grad[...], R.ms[...], R.vs[...])
    R.small_low[...] = adam_diff(R.ps[...], first_new, second_new, rate_small, 0.0).astype(bf16).astype(f32)

    mine = R.shared[c, 0, 8:16]
    for ss in range(2):
        for dd in range(2):
            if ss or dd:
                mine = mine + R.shared[ss * (n_tp // 2) + c, dd, 8:16]
    size = R.bu.shape[1]
    turned = pltpu.roll(mine, lax.rem(width - (s * 2 + d) * size, width), 1)
    R.bias_grad[0:1] = turned[1:2, 0:size]
    R.bias_grad[1:2] = turned[1:2, width // 2 : width // 2 + size]
    R.bias_grad[2:3] = turned[2:3, 0:size]
    R.bias_grad[3:4] = turned[2:3, width // 2 : width // 2 + size]
    first_new, second_new = adam_parts(R.bias_grad[...], R.mu[...], R.vu[...])
    R.bias_low[...] = adam_diff(R.bu[...], first_new, second_new, rate_small, 0.0).astype(bf16).astype(f32)

    R.ada_rows[...] = jnp.zeros_like(R.ada_rows)
    R.cond_rows[...] = jnp.zeros_like(R.cond_rows)
    for ss in range(2):
        for dd in range(2):
            total = R.shared[2 * ss, dd, 0:8] + R.shared[2 * ss + 1, dd, 0:8]
            turned = pltpu.roll(total, lax.rem(width - t * part, width), 1)
            k = ss * 2 + dd
            R.cond_rows[k : k + 1] = R.cond[dd, ss : ss + 1]
            for a in range(6):
                R.ada_rows[a, k : k + 1] = turned[a : a + 1, 0:part]
    lhs = R.cond_rows[...][:, : R.wa.shape[1]]
    for a in range(6):
        gradient = lax.dot_general(
            lhs, R.ada_rows[a], (((0,), (0,)), ((), ())), precision=highest, preferred_element_type=f32)
        R.ada_grad[a] = gradient
        first_new, second_new = adam_parts(gradient, R.ma[a], R.va[a])
        R.ada_low[a] = adam_diff(R.wa[a], first_new, second_new, rate_matrix, decay_rate).astype(bf16)


def backward(direct, cores, seqs, fw, tokens, cosine, sine, states, smalls):
    n_tp = lax.axis_size("tp")
    length, width = fw.h1_out.shape
    heads = fw.inv_out.shape[0]
    slot_rows = fw.weights_out.shape[1]
    half = length // cores
    dma = pltpu.SemaphoreType.DMA
    arr = jax.ShapeDtypeStruct
    vm = pltpu.VMEM
    spans = 2 if direct else 1
    ins = dict(
        weights_in=(fw.weights_out, ANY), o_in=(fw.o_out, ANY), v_in=(fw.v_out, ANY),
        k_in=(fw.k_out, ANY), q_in=(fw.q_out, ANY), probs_in=(fw.probs_out, ANY), h1_in=(fw.h1_out, ANY),
        x1_in=(fw.x1_out, ANY), attn_in=(fw.attn_out, ANY), h2_in=(fw.h2_out, ANY), hidden_in=(fw.hidden_out, ANY),
        gm_in=(fw.gm_out, ANY), gy_in=(fw.gy_out, ANY), tok_all=(tokens, ANY),
        inv=(fw.inv_out, VMEM), vecs=(fw.vecs_out, VMEM), cosine=(cosine, VMEM), sine=(sine, VMEM),
    )
    outs = dict(
        block_out=(arr((seqs, length, width), bf16), ANY),
        grad_out=(arr((seqs, length, width), bf16), ANY),
    )
    scratch = dict(
        weights=vm((16 if direct else 12, slot_rows, width), bf16),
        spare=vm((heads, length, length), bf16),
        ga=vm((length, width), bf16),
        hid=vm((length, width), bf16),
        trade=vm((2, half, width), bf16),
        x1=vm((half, width), f32),
        attn=vm((half, width), f32),
        gy=vm((half, width), bf16),
        tok=vm((half, width), bf16),
        half_out=vm((half, width), bf16),
        o_t=vm((slot_rows, length), bf16),
        v_r=vm((length, slot_rows), bf16),
        k_t=vm((slot_rows, length), bf16),
        q_t=vm((slot_rows, length), bf16),
        do_t=vm((slot_rows, length), bf16),
        dv_t=vm((slot_rows, length), bf16),
        bias_sum=vm((8, 4 * slot_rows), f32),
        acc=vm((5, 8, width), f32),
        stats=vm((8, width), f32),
        sums=vm((16, width), f32),
        load_sem=dma((17,)),
        probs_sem=dma((4,)),
        spread_sem=dma((2, 2, 2)),
        cross_sem=dma((2, 2, 4)),
        relay_sem=dma((2, 2, 4)),
        pair_sem=dma((2, 4)),
        cast_sem=dma((2, spans * n_tp - 1)),
    )
    if direct:
        wa, ma, va, ps, ms, vs, bu, mu, vu = smalls
        rows, cols = slot_rows // 2, width // 2
        slot = (12, rows, cols)
        wi, wb, mi, mb, vi, vb = states
        ins |= dict(
            gd_in=(fw.gd_out, ANY), cond=(fw.cond_out, VMEM), wi=(wi, ANY), wb=(wb, ANY),
            mi=(mi, ANY), mb=(mb, ANY), vi=(vi, ANY), vb=(vb, ANY), wa=(wa, VMEM), ma=(ma, VMEM), va=(va, VMEM),
            ps=(ps, VMEM), ms=(ms, VMEM), vs=(vs, VMEM), bu=(bu, VMEM), mu=(mu, VMEM), vu=(vu, VMEM),
        )
        outs |= dict(
            gsum=(arr(slot, f32), ANY),
            total=(arr(slot, bf16), VMEM),
            ada_grad=(arr(wa.shape, f32), VMEM),
            small_grad=(arr(ps.shape, f32), VMEM),
            bias_grad=(arr(bu.shape, f32), VMEM),
            ada_total=(arr(wa.shape, bf16), VMEM),
            small_total=(arr(ps.shape, f32), VMEM),
            bias_total=(arr(bu.shape, f32), VMEM),
        )
        scratch |= dict(
            shared=vm((n_tp, spans, 16, width), f32),
            sum_ring=vm((2, rows, cols), f32),
            got_a=vm((12, slot_rows, cols), bf16),
            send_b=vm(slot, bf16),
            got_b=vm(slot, bf16),
            state=vm((4, 3, rows, cols), f32),
            diff=vm(slot, bf16),
            got_p=vm(slot, bf16),
            got_h=vm((12, rows // 2, cols), bf16),
            summed=vm((16, width), f32),
            ada_rows=vm((6, 8, wa.shape[2]), f32),
            cond_rows=vm((8, 128), f32),
            ada_low=vm(wa.shape, bf16),
            ada_p=vm(wa.shape, bf16),
            ada_h=vm((wa.shape[0] // 2,) + wa.shape[1:], bf16),
            small_low=vm(ps.shape, f32),
            bias_low=vm(bu.shape, f32),
            small_all=vm((4,) + ps.shape, f32),
            bias_all=vm((4,) + bu.shape, f32),
            gd_sem=dma,
            sum_sem=dma((2,)),
            state_sem=dma((4, 3)),
            asem=dma((2, 12)),
            bsem=dma((2, 12)),
            psem=dma((2, 12)),
            hsem=dma((2, 12)),
            fsem=dma((2, 12, 3)),
            tiny_sem=dma((2, 2, 3)),
            ada_sem=dma((2, 5)),
        )
    else:
        outs |= dict(
            grads=(arr((4, slot_rows, width), bf16), VMEM),
            grads_up=(arr((4, slot_rows, width), bf16), VMEM),
            shared=(arr((n_tp, spans, 16, width), f32), VMEM),
        )
    names = list(ins) + list(outs) + list(scratch)
    results = pl.pallas_call(
        functools.partial(backward_kernel, direct, cores, n_tp, names),
        out_shape=tuple(o[0] for o in outs.values()),
        in_specs=[i[1] for i in ins.values()],
        out_specs=tuple(o[1] for o in outs.values()),
        scratch_shapes=list(scratch.values()),
        compiler_params=pltpu.CompilerParams(collective_id=1, has_side_effects=True, vmem_limit_bytes=61 * MIB),
        name="backward",
    )(*[i[0] for i in ins.values()])
    return SimpleNamespace(**dict(zip(outs, results)))


def angle_tables(length):
    half = HEAD_DIM // 2
    frequency = np.float32(10000.0) ** (np.float32(-2.0) * np.arange(half, dtype=np.float32) / np.float32(HEAD_DIM))
    angles = frequency[:, None] * np.arange(length, dtype=np.float32)[None, :]
    return jnp.asarray(np.cos(angles)), jnp.asarray(np.sin(angles))


def on_device(
    tokens, sigma_index, absorbed, cotangent, time_table,
    in_weight, back_weight, ada_weight, small_params, up_bias,
    in_first, back_first, ada_first, small_first, bias_first,
    in_second, back_second, ada_second, small_second, bias_second,
    in_moment, back_moment, ada_moment, small_moment, bias_moment,
):
    n_tp, n_dp, n_grp = lax.axis_size("tp"), lax.axis_size("dp"), lax.axis_size("grp")
    seqs, length, width = tokens.shape
    cores = n_tp // seqs
    part = in_weight.shape[2]
    heads_width = seqs * part
    direct = n_dp == 2 and n_grp == 4 and seqs == 2 and cores == 2
    t, d = lax.axis_index("tp"), lax.axis_index("dp")
    s = t // cores
    c = lax.rem(t, cores)
    groups = [[a * cores + b for a in range(seqs)] for b in range(cores)]

    wi_t = jnp.transpose(in_weight, (1, 2, 0))
    wa_t = jnp.transpose(ada_weight, (1, 0, 2))
    cosine, sine = angle_tables(length)
    if direct:
        first = (sigma_index, time_table, wa_t, small_params, up_bias, wi_t, back_weight)
    else:
        def over_tp(x, axis):
            return lax.all_gather(x, "tp", axis=axis, tiled=True, axis_index_groups=groups)

        table_ids = jnp.arange(time_table.shape[0], dtype=jnp.int32)
        onehot = (sigma_index[:, None] == table_ids[None, :]).astype(f32)
        condition = jax.nn.silu(jnp.dot(onehot, time_table, precision=highest))
        cond_low = condition.astype(bf16).astype(f32)
        wi_all = over_tp(lax.all_gather(wi_t.astype(bf16), "dp", axis=2, tiled=True), 1)
        wb_all = over_tp(lax.all_gather(back_weight.astype(bf16), "dp", axis=2, tiled=True), 1)
        weights = jnp.concatenate([wi_all[:3], wb_all[:1], wi_all[3:], wb_all[1:]], axis=0)
        bu_all = over_tp(lax.all_gather(up_bias.astype(bf16), "dp", axis=1, tiled=True)[None], 0)
        bias_row = jnp.transpose(bu_all, (1, 0, 2)).reshape(1, 4 * heads_width).astype(f32)
        small_rows = lax.all_gather(small_params.astype(bf16), "dp", axis=1, tiled=True).astype(f32)
        wa_all = lax.all_gather(ada_weight.astype(bf16), "dp", axis=0, tiled=True)
        mod_part = jnp.einsum("sc,cad->sad", cond_low.astype(bf16), wa_all, preferred_element_type=f32)
        mod_all = lax.all_gather(mod_part, "tp", axis=2, tiled=True)
        mod_rows = lax.dynamic_index_in_dim(mod_all, s, 0, keepdims=False) + small_rows[3:9]
        vecs = jnp.concatenate([small_rows[0:3], mod_rows, jnp.zeros((7, width), f32)], axis=0)
        first = (weights, vecs, bias_row)

    fw = forward(direct, cores, length, width, heads_width, first, tokens, absorbed, cotangent, cosine, sine)
    mi, vi = jnp.transpose(in_first[0], (1, 2, 0)), jnp.transpose(in_second[0], (1, 2, 0))
    mb, vb = back_first[0], back_second[0]
    am, av = jnp.transpose(ada_first[0], (1, 0, 2)), jnp.transpose(ada_second[0], (1, 0, 2))
    states = (wi_t, back_weight, mi, mb, vi, vb)
    smalls = (
        wa_t, am, av, small_params, small_first[0], small_second[0], up_bias, bias_first[0], bias_second[0])
    bw = backward(direct, cores, seqs, fw, tokens, cosine, sine, states, smalls)
    block_out = bw.block_out
    input_grad = bw.grad_out.astype(f32)
    if direct:
        gi, gbk = bw.gsum[:7], bw.gsum[7:]
        di, db = bw.total[:7].astype(f32), bw.total[7:].astype(f32)
        ada_grad, small_shard, bias_grad = bw.ada_grad, bw.small_grad, bw.bias_grad
        ada_t, small_t, bias_t = bw.ada_total.astype(f32), bw.small_total, bw.bias_total
    else:
        shared = lax.all_gather(bw.shared[:, 0], "dp", axis=1).reshape(seqs, cores, n_dp, 16, width)
        by_seq = shared.sum(axis=1)
        dmod = by_seq[:, :, 0:6]
        small_grad = jnp.concatenate([by_seq[:, :, 6:9].sum(axis=(0, 1)), dmod.sum(axis=(0, 1))], axis=0)
        bias_sum = shared[:, :, :, 9:11].sum(axis=(0, 2)).reshape(cores, 4, seqs, part)
        mine = lax.dynamic_index_in_dim(lax.dynamic_index_in_dim(bias_sum, c, 0, keepdims=False), s, 1, keepdims=False)
        bias_grad = lax.dynamic_slice_in_dim(mine, d * (part // n_dp), part // n_dp, 1)
        small_shard = lax.dynamic_slice_in_dim(small_grad, d * (width // n_dp), width // n_dp, 1)
        dmod_cols = lax.dynamic_slice_in_dim(dmod, t * part, part, 3)
        conds = jnp.transpose(lax.all_gather(cond_low, "dp", axis=0), (1, 0, 2))
        conds = lax.dynamic_slice_in_dim(conds, d * wa_t.shape[1], wa_t.shape[1], 2)
        ada_grad = jnp.sum(conds[:, :, None, :, None] * dmod_cols[:, :, :, None, :], axis=(0, 1))

        def scatter(x):
            x = lax.psum_scatter(x, "tp", scatter_dimension=1, tiled=True, axis_index_groups=groups)
            return lax.psum_scatter(x, "dp", scatter_dimension=2, tiled=True).astype(f32)

        gi = scatter(jnp.concatenate([bw.grads[1:4], bw.grads_up], axis=0))
        gbk = scatter(jnp.concatenate([bw.grads[0:1], fw.gd_out], axis=0))
    ada_m, ada_v = adam_parts(ada_grad, am, av)
    small_m, small_v = adam_parts(small_shard, small_first[0], small_second[0])
    bias_m, bias_v = adam_parts(bias_grad, bias_first[0], bias_second[0])
    in_m, in_v = adam_parts(gi, mi, vi)
    back_m, back_v = adam_parts(gbk, mb, vb)
    if not direct:
        def over_groups(weight, first_new, second_new, rate, decay):
            return lax.psum(adam_diff(weight, first_new, second_new, rate, decay).astype(bf16), "grp").astype(f32)

        di = over_groups(wi_t, in_m, in_v, rate_matrix, decay_rate)
        db = over_groups(back_weight, back_m, back_v, rate_matrix, decay_rate)
        ada_t = over_groups(wa_t, ada_m, ada_v, rate_matrix, decay_rate)
        small_t = over_groups(small_params, small_m, small_v, rate_small, 0.0)
        bias_t = over_groups(up_bias, bias_m, bias_v, rate_small, 0.0)

    def outer(weight, moment, summed):
        diff = summed / n_grp
        moment_new = outer_mu * moment + diff
        return weight - outer_rate * (diff + outer_mu * moment_new), diff, moment_new

    def back_in(x):
        return jnp.transpose(x, (2, 0, 1))

    def back_ada(x):
        return jnp.transpose(x, (1, 0, 2))

    in_w, in_diff, in_mom = (back_in(x) for x in outer(wi_t, jnp.transpose(in_moment, (1, 2, 0)), di))
    back_w, back_diff, back_mom = outer(back_weight, back_moment, db)
    ada_w, ada_diff, ada_mom = (back_ada(x) for x in outer(wa_t, jnp.transpose(ada_moment, (1, 0, 2)), ada_t))
    small_w, small_diff, small_mom = outer(small_params, small_moment, small_t)
    bias_w, bias_diff, bias_mom = outer(up_bias, bias_moment, bias_t)
    return (
        block_out, input_grad,
        back_in(in_m)[None], back_m[None], back_ada(ada_m)[None], small_m[None], bias_m[None],
        back_in(in_v)[None], back_v[None], back_ada(ada_v)[None], small_v[None], bias_v[None],
        in_w, back_w, ada_w, small_w, bias_w,
        in_diff, back_diff, ada_diff, small_diff, bias_diff,
        in_mom, back_mom, ada_mom, small_mom, bias_mom,
    )


def solution(mesh):
    rows = P(("dp", "grp"), None, None)
    shared = (
        P("dp", None, "tp"), P(None, "tp", "dp"), P("dp", None, "tp"), P(None, "dp"), P(None, ("tp", "dp")),
    )
    grouped = (
        P("grp", "dp", None, "tp"), P("grp", None, "tp", "dp"), P("grp", "dp", None, "tp"),
        P("grp", None, "dp"), P("grp", None, ("tp", "dp")),
    )
    in_specs = (rows, P(("dp", "grp")), P(("dp", "grp"), None), rows, P()) + shared + grouped + grouped + shared
    out_specs = (rows, rows) + grouped + grouped + shared + shared + shared
    return jax.shard_map(on_device, mesh=mesh, in_specs=in_specs, out_specs=out_specs, check_vma=False)
```
